32 devices in a mesh: parts: 2 (over y), dp: 4 (over z), section: 2 (over x), chan: 2 (over core).
Axes of the slice: x: 2, y: 2, z: 4, core: 2. Of those that a mesh axis runs over, the one named last changes fastest.
Arguments:
- block_inputs: bfloat16 [2, 16, 8, 8, 1024], P('section', ('parts', 'dp')), parts along dimension 1, may hold values from -6 to 6
- out_pre: bfloat16 [2, 16, 8, 8, 1024], P('section', ('parts', 'dp')), parts along dimension 1, may hold values from -6 to 6
- first_pre: bfloat16 [2, 16, 8, 8, 1024], P('section', ('parts', 'dp'), None, None, 'chan'), parts along dimension 1, may hold values from -6 to 6
- second_pre: bfloat16 [2, 16, 8, 8, 1024], P('section', ('parts', 'dp'), None, None, 'chan'), parts along dimension 1, may hold values from -6 to 6
- w_reduce: bfloat16 [2, 1024, 1024], P('section', None, 'chan'), may hold values from -0.1875 to 0.1875
- w_group: bfloat16 [2, 9, 64, 16, 16], P('section', None, 'chan'), may hold values from -0.5 to 0.5
- w_expand: bfloat16 [2, 1024, 1024], P('section', 'chan'), may hold values from -0.1875 to 0.1875
- w_lateral: bfloat16 [1024, 256], replicated, may hold values from -0.1875 to 0.1875
- teacher: bfloat16 [16, 8, 8, 256], P(('parts', 'dp')), parts along dimension 0, may hold values from -6 to 6
- top_grad: bfloat16 [16, 8, 8, 1024], P(('parts', 'dp')), parts along dimension 0, may hold values from -6 to 6
- boxes: int32 [16, 8, 4], P(('parts', 'dp')), parts along dimension 0, may hold values from 0 to 8, as said below
- region_counts: int32 [16], P(('parts', 'dp')), parts along dimension 0, may hold values from 1 to 8
Outputs:
- input_grads: bfloat16 [2, 16, 8, 8, 1024], P('section', ('parts', 'dp')), parts along dimension 1
- reduce_grads: float32 [4, 1024, 1024], P(('parts', 'section'), 'dp', 'chan'), parts along dimension 0
- group_grads: float32 [4, 9, 64, 16, 16], P(('parts', 'section'), None, 'chan', 'dp'), parts along dimension 0
- expand_grads: float32 [4, 1024, 1024], P(('parts', 'section'), 'chan', 'dp'), parts along dimension 0
The draws below stay inside these ranges and needn't reach their ends.
There are 2 independent parts, one for each index of `parts`. The reference program is written for one: setup_inputs(seed, part) draws one part's arguments, and reference() takes and returns one part's arrays. A program takes and returns all parts, laid end to end along the dimension named above; an argument that names none is the same for every part. Nothing has to cross between parts.
Inputs may be any that keep to these rules, and one draw needn't show every extreme that they name: `boxes`: each used row is a region with top < bottom and left < right; only the first region_counts[i] rows of page i are used, the others are padding.
All inputs are finite; a program needn't handle non-finite values.
Results may differ from the reference program's by a relative error of at most 0.0059.
Values may be sent and summed in bfloat16 or wider, within the bound.
A program may use at most 128 MiB of HBM per device.

```python
import math
import jax
import jax.numpy as jnp
from jax import lax

C = 1024
G = 64
GW = 16
LAT = 256
SIDE = 8
R_MAX = 8
IMAGES = 8
PIXELS = 512
BLOCKS = 2


def draw_boxes(key, part):
    height_key, width_key, top_key, left_key = jax.random.split(jax.random.fold_in(key, 11), 4)
    page_index = jnp.arange(IMAGES, dtype=jnp.int32)
    largest = jnp.maximum(1, SIDE * (IMAGES + 2 * page_index) // (3 * IMAGES))[:, None]
    height = jax.random.randint(height_key, (IMAGES, R_MAX), 1, largest + 1)
    width = jax.random.randint(width_key, (IMAGES, R_MAX), 1, largest + 1)
    top_edge = jax.random.randint(top_key, (IMAGES, R_MAX), 0, SIDE - height + 1)
    left_edge = jax.random.randint(left_key, (IMAGES, R_MAX), 0, SIDE - width + 1)
    layout = jnp.stack([top_edge, top_edge + height, left_edge, left_edge + width], axis=-1)
    whole_page = jnp.array([0, SIDE, 0, SIDE], dtype=jnp.int32)
    layout = layout.at[IMAGES - 1, 0].set(whole_page)
    return layout.astype(jnp.int32)


def draw_region_counts(key, part):
    counts = jax.random.randint(jax.random.fold_in(key, 23), (IMAGES,), 1, R_MAX + 1)
    counts = counts.at[0].set(R_MAX)
    counts = counts.at[IMAGES - 1].set(1)
    return counts.astype(jnp.int32)


def raised(values, rng, source, target, parts, factor):
    owner, partner = [(jnp.arange(values.shape[dim]) // (values.shape[dim] // parts)).reshape([-1 if axis == dim else 1 for axis in range(values.ndim)]) for dim in (source, target)]
    chosen = jax.random.permutation(rng, parts)[partner]
    strong = (owner == chosen) | (owner == (partner + parts // 2) % parts)
    return jnp.where(strong, factor * values, values)


def steps_of(stream_key, dims, cuts, smallest, top_value):
    def one(dim, blocks):
        steps = jax.random.uniform(jax.random.fold_in(jax.random.fold_in(stream_key, 6), dim), (blocks,), jnp.float32, smallest / len(cuts), top_value / len(cuts))
        return jnp.repeat(jnp.exp(steps), dims[dim] // blocks).reshape((-1,) + (1,) * (len(dims) - dim - 1))

    loudness = one(*cuts[0])
    for cut in cuts[1:]:
        loudness = loudness * one(*cut)
    return loudness


def centred(rng, dims, scale, most, cuts=(), kind=jnp.bfloat16):
    values = jax.random.normal(rng, dims, jnp.float32) * scale
    if len(cuts) > 0:
        values = steps_of(rng, dims, cuts, -0.22, 0.18) * values
    return jnp.clip(values, min=-most, max=most).astype(kind)


def gaussian_with(own_key, shape, deviation, reach, cuts, heavy, kind=jnp.bfloat16):
    result = deviation * jax.random.normal(own_key, shape, jnp.float32)
    if cuts:
        result = result * steps_of(own_key, shape, cuts, -0.22, 0.18)
    return jnp.clip(raised(result, jax.random.fold_in(own_key, 3), *heavy), -reach, reach).astype(kind)


def setup_inputs(seed: int = 0, part: int = 0) -> dict:
    keys = jax.random.split(jax.random.key(seed), 13)
    part_splits = jax.random.split(jax.random.fold_in(keys[12], part), 13)
    block_inputs = gaussian_with(part_splits[0], (BLOCKS, IMAGES, SIDE, SIDE, C), 1.0, 6.0, ((0, 2), (1, 4)), (1, 4, 4, 2.0))
    out_pre = centred(part_splits[1], (BLOCKS, IMAGES, SIDE, SIDE, C), 1.0, 6.0, ((0, 2), (1, 4)))
    first_pre = centred(part_splits[2], (BLOCKS, IMAGES, SIDE, SIDE, C), 1.0, 6.0, ((0, 2), (1, 4), (4, 2)))
    second_pre = centred(part_splits[3], (BLOCKS, IMAGES, SIDE, SIDE, C), 1.0, 6.0, ((0, 2), (1, 4), (4, 2)))
    w_reduce = centred(keys[4], (BLOCKS, C, C), C ** -0.5, 0.1875, ((0, 2), (2, 2)))
    w_group = centred(keys[5], (BLOCKS, 9, G, GW, GW), (9 * GW) ** -0.5, 0.5, ((0, 2), (2, 2)))
    w_expand = centred(keys[6], (BLOCKS, C, C), C ** -0.5, 0.1875, ((0, 2), (1, 2)))
    w_lateral = centred(keys[7], (C, LAT), C ** -0.5, 0.1875)
    teacher = centred(part_splits[8], (IMAGES, SIDE, SIDE, LAT), 1.0, 6.0, ((0, 4),))
    top_grad = centred(part_splits[9], (IMAGES, SIDE, SIDE, C), 1.0, 6.0, ((0, 4),))
    boxes = draw_boxes(jax.random.fold_in(jax.random.fold_in(keys[12], part), 71), part)
    region_counts = draw_region_counts(jax.random.fold_in(jax.random.fold_in(keys[12], part), 71), part)
    return {"block_inputs": block_inputs, "out_pre": out_pre, "first_pre": first_pre, "second_pre": second_pre, "w_reduce": w_reduce, "w_group": w_group, "w_expand": w_expand, "w_lateral": w_lateral, "teacher": teacher, "top_grad": top_grad, "boxes": boxes, "region_counts": region_counts}


imitation_weight = 0.5
tap_offsets = [(tap_index // 3 - 1, tap_index % 3 - 1) for tap_index in range(9)]

def region_mask(boxes, region_counts):
    cells = jnp.arange(SIDE, dtype=jnp.int32)
    row_inside = (cells[None, None, :] >= boxes[:, :, 0:1]) & (cells[None, None, :] < boxes[:, :, 1:2])
    col_inside = (cells[None, None, :] >= boxes[:, :, 2:3]) & (cells[None, None, :] < boxes[:, :, 3:4])
    used = jnp.arange(R_MAX, dtype=jnp.int32)[None, :] < region_counts[:, None]
    inside = row_inside[:, :, :, None] & col_inside[:, :, None, :] & used[:, :, None, None]
    return jnp.any(inside, axis=1).astype(jnp.float32)

def reference(block_inputs, out_pre, first_pre, second_pre, w_reduce, w_group, w_expand, w_lateral, teacher, top_grad, boxes, region_counts):
    page_mask = region_mask(boxes, region_counts).reshape(-1, 1)
    covered = jnp.sum(page_mask)
    feature = jnp.maximum(out_pre[BLOCKS - 1], 0).reshape(-1, C)
    lateral = jnp.dot(feature, w_lateral, preferred_element_type=jnp.float32)
    error = (page_mask * (lateral - teacher.reshape(-1, LAT).astype(jnp.float32)) * (imitation_weight * PIXELS / covered)).astype(jnp.bfloat16)
    imitation = jnp.dot(error, w_lateral.T, preferred_element_type=jnp.float32)
    cotangent = (top_grad.reshape(-1, C).astype(jnp.float32) + imitation).astype(jnp.bfloat16)
    highest = lax.Precision.HIGHEST
    input_list, reduce_list, group_list, expand_list = ([], [], [], [])
    for block in range(BLOCKS - 1, -1, -1):
        out_rows = out_pre[block].reshape(-1, C)
        passed = jnp.where(out_rows > 0, cotangent, jnp.zeros_like(cotangent))
        second_rows = second_pre[block].reshape(-1, C)
        second_full = jnp.dot(passed, w_expand[block].T, preferred_element_type=jnp.float32)
        d_second = jnp.where(second_rows > 0, second_full, jnp.zeros_like(second_full)).astype(jnp.bfloat16)
        expand_sum = jnp.dot(jnp.maximum(second_rows, 0).T, passed, preferred_element_type=jnp.float32)
        relu_first = jnp.maximum(first_pre[block], 0).astype(jnp.float32).reshape(IMAGES, SIDE, SIDE, G, GW)
        padded_first = jnp.pad(relu_first, ((0, 0), (1, 1), (1, 1), (0, 0), (0, 0)))
        second_grid = d_second.astype(jnp.float32).reshape(IMAGES, SIDE, SIDE, G, GW)
        padded_second = jnp.pad(second_grid, ((0, 0), (1, 1), (1, 1), (0, 0), (0, 0)))
        group_weight = w_group[block].astype(jnp.float32)
        first_grad = jnp.zeros((IMAGES, SIDE, SIDE, G, GW), jnp.float32)
        group_terms = []
        for tap_index, (row_shift, col_shift) in enumerate(tap_offsets):
            shifted = padded_first[:, 1 + row_shift:1 + row_shift + SIDE, 1 + col_shift:1 + col_shift + SIDE]
            group_terms.append(jnp.einsum('nhwgi,nhwgo->gio', shifted, second_grid, precision=highest))
            behind = padded_second[:, 1 - row_shift:1 - row_shift + SIDE, 1 - col_shift:1 - col_shift + SIDE]
            first_grad = first_grad + jnp.einsum('nhwgo,gio->nhwgi', behind, group_weight[tap_index], precision=highest)
        first_rows = first_pre[block].reshape(-1, C)
        first_flat = first_grad.reshape(-1, C)
        d_first = jnp.where(first_rows > 0, first_flat, jnp.zeros_like(first_flat)).astype(jnp.bfloat16)
        reduce_sum = jnp.dot(block_inputs[block].reshape(-1, C).T, d_first, preferred_element_type=jnp.float32)
        cotangent = (jnp.dot(d_first, w_reduce[block].T, preferred_element_type=jnp.float32) + passed.astype(jnp.float32)).astype(jnp.bfloat16)
        input_list.append(cotangent.reshape(IMAGES, SIDE, SIDE, C))
        reduce_list.append(reduce_sum)
        group_list.append(jnp.stack(group_terms))
        expand_list.append(expand_sum)
    scale = 1.0 / math.sqrt(PIXELS)
    input_grads = jnp.stack(input_list[::-1])
    reduce_grads = jnp.stack(reduce_list[::-1]) * scale
    group_grads = jnp.stack(group_list[::-1]) * scale
    expand_grads = jnp.stack(expand_list[::-1]) * scale
    return (input_grads, reduce_grads, group_grads, expand_grads)
```

```python
import functools
import math

import jax
import jax.numpy as jnp
from jax import lax
from jax.experimental import pallas as pl
from jax.experimental.pallas import tpu as pltpu
from jax.sharding import PartitionSpec as P

imitation_weight = 0.5
tap_offsets = [(tap // 3 - 1, tap % 3 - 1) for tap in range(9)]
f32 = jnp.float32
bf16 = jnp.bfloat16


def dot_nn(a, b):
    return lax.dot_general(a, b, (((1,), (0,)), ((), ())), preferred_element_type=f32)


def dot_nt(a, b):
    return lax.dot_general(a, b, (((1,), (1,)), ((), ())), preferred_element_type=f32)


def dot_tn(a, b):
    return lax.dot_general(a, b, (((0,), (0,)), ((), ())), preferred_element_type=f32)


def kernel(
    dims,
    boxes_hbm, counts_hbm, bi_hbm, out_hbm, first_hbm, second_hbm, wr_hbm, wg_hbm, we_hbm,
    wl_hbm, teacher_hbm, top_hbm,
    grads_ref, reduce_ref, group_ref, expand_ref,
    boxes_ref, counts_ref,
    bi_ref, out_ref, first_ref, second_ref, wr_ref, wg_ref, we_ref, wl_ref, teacher_ref, top_ref,
    load_sem,
    inc, pas, wr_peer, dfx, ng, ds, d_all, sec_all, bi_send, bi_all, ps_send, ps_all,
    gf, g_send, g_all, cnt, taps, ft,
    dp_send, dp_recv, core_send, core_recv, hop_send, hop_recv, fwd_send, fwd_recv,
    right_send, right_recv, left_send, left_recv, share_send, share_recv,
):
    n, sections, crops, side, slots, pixels = dims
    rows, channels = bi_ref.shape
    half = channels // 2
    width = first_ref.shape[1]
    groups = wg_ref.shape[1]
    gw = width // groups
    blk = taps.shape[2]
    blocks = width // blk
    cells = side * side
    share = channels // n
    k = gw // n
    hrows = rows // 2
    me = lax.axis_index("dp")
    s = lax.axis_index("section")
    c = lax.axis_index("chan")
    other = 1 - c
    last = sections - 1
    norm = 1.0 / math.sqrt(pixels)

    def remote(src, dst, send, recv, where):
        return pltpu.make_async_remote_copy(
            src_ref=src, dst_ref=dst, send_sem=send, recv_sem=recv,
            device_id=where, device_id_type=pl.DeviceIdType.MESH,
        )

    def dp_copies(what, src_of, dst):
        out = []
        for step in range(1, n):
            to = lax.rem(me + step, n)
            out.append(remote(src_of(to), dst, dp_send.at[what, step - 1],
                              dp_recv.at[what, step - 1], {"dp": to}))
        return out

    mine = pl.ds(pl.multiple_of(c * hrows, hrows), hrows)

    def part(q):
        return pl.ds(q * hrows, hrows)

    def share_copies(which, buf):
        out = []
        for step in range(1, n):
            rows_ref = buf.at[lax.rem(me + n - step, n), mine]
            out.append(remote(rows_ref, rows_ref, share_send.at[which, step - 1],
                              share_recv.at[which, step - 1], {"chan": other}))
        return out

    def line(what, step, q, buf):
        ahead = buf.at[lax.max(me - step, 0), part(q)]
        behind = buf.at[lax.min(me + step, n - 1), part(q)]
        right = remote(ahead, ahead, right_send.at[what, step, q], right_recv.at[what, step, q],
                       {"dp": lax.min(me + 1, n - 1)})
        left = remote(behind, behind, left_send.at[what, step, q], left_recv.at[what, step, q],
                      {"dp": lax.max(me - 1, 0)})
        return (
            (right, (me - step >= 0) & (me + 1 < n), me - 1 - step >= 0),
            (left, (me + step < n) & (me >= 1), me + 1 + step < n),
        )

    def line_start(moves):
        for copy, sends, _ in moves:
            pl.when(sends)(copy.start)

    def line_recv(moves):
        for copy, _, receives in moves:
            pl.when(receives)(copy.wait_recv)

    barrier = pltpu.get_barrier_semaphore()
    mesh_type = pl.DeviceIdType.MESH
    for step in range(1, n):
        pl.semaphore_signal(barrier, inc=1, device_id={"dp": lax.rem(me + step, n)},
                            device_id_type=mesh_type)
    pl.semaphore_signal(barrier, inc=1, device_id={"chan": other}, device_id_type=mesh_type)

    @pl.when(s > 0)
    def _():
        pl.semaphore_signal(barrier, inc=1, device_id={"section": s - 1},
                            device_id_type=mesh_type)

    @pl.when(s < last)
    def _():
        pl.semaphore_signal(barrier, inc=1, device_id={"section": s + 1},
                            device_id_type=mesh_type)

    pairs = {
        "boxes": (boxes_hbm, boxes_ref), "counts": (counts_hbm, counts_ref),
        "out": (out_hbm, out_ref), "wl": (wl_hbm, wl_ref), "teacher": (teacher_hbm, teacher_ref),
        "second": (second_hbm, second_ref), "bi": (bi_hbm, bi_ref), "wg": (wg_hbm, wg_ref),
        "top": (top_hbm, top_ref), "we0": (we_hbm.at[:, :half], we_ref.at[0]),
        "we1": (we_hbm.at[:, half:], we_ref.at[1]), "first": (first_hbm, first_ref),
        "wr": (wr_hbm, wr_ref),
    }
    loads = {name: pltpu.make_async_copy(a, b, load_sem.at[i])
             for i, (name, (a, b)) in enumerate(pairs.items())}
    for load in loads.values():
        load.start()

    def loaded(*names):
        for name in names:
            loads[name].wait()

    loaded("boxes", "counts")
    row = lax.broadcasted_iota(jnp.int32, (cells, 128), 0)
    row_h, row_w = row // side, row % side
    masks = []
    for crop in range(crops):
        inside = jnp.zeros((cells, 128), f32)
        for r in range(slots):
            hit = ((row_h >= boxes_ref[crop, 0, r]) & (row_h < boxes_ref[crop, 1, r])
                   & (row_w >= boxes_ref[crop, 2, r]) & (row_w < boxes_ref[crop, 3, r])
                   & (counts_ref[0, crop] > r))
            inside = jnp.where(hit, 1.0, inside)
        masks.append(inside)
    mask = jnp.concatenate(masks, axis=0)
    cnt[me] = jnp.broadcast_to(jnp.sum(mask, axis=0, keepdims=True), (8, 128))

    pl.semaphore_wait(barrier, n + jnp.where(s > 0, 1, 0) + jnp.where(s < last, 1, 0))

    cnt_copies = dp_copies(0, lambda to: cnt.at[me], cnt.at[me])

    @pl.when(s == last)
    def _():
        for copy in cnt_copies:
            copy.start()

    loaded("second", "bi", "wr")
    sec_all[me] = jnp.maximum(second_ref[...], 0)
    for j in range(n):
        bi_send[j] = bi_ref[:, j * share : (j + 1) * share]
    bi_all[me] = bi_send[me]

    wr_copy = remote(wr_ref.at[pl.ds(pl.multiple_of(other * half, half), half)], wr_peer,
                     core_send.at[0], core_recv.at[0], {"chan": other})
    sec_moves = [[line(0, step, q, sec_all) for q in range(2)] for step in range(n - 1)]
    bi_copies = dp_copies(1, lambda to: bi_send.at[to, mine], bi_all.at[me, mine])
    bi_shares = share_copies(0, bi_all)

    def bulk_start():
        for q in range(2):
            line_start(sec_moves[0][q])
        for copy in bi_copies:
            copy.start()
        wr_copy.start()

    def sec_forward():
        for step in range(n - 2):
            for q in range(2):
                line_recv(sec_moves[step][q])
                line_start(sec_moves[step + 1][q])

    def bi_forward():
        for copy, share_copy in zip(bi_copies, bi_shares):
            copy.wait_recv()
            share_copy.start()

    pair = gw * gw
    iota = lambda shape, dim: lax.broadcasted_iota(jnp.int32, shape, dim)
    same = iota((blk, blk), 0) // gw == iota((blk, blk), 1) // gw

    def build_taps():
        same_out = iota((blk, pair), 0) % gw == iota((blk, pair), 1) % gw
        spread = (iota((pair, blk), 0) // gw == iota((pair, blk), 1) % gw).astype(f32).astype(bf16)
        for b in range(blocks):
            pick = (iota((blk, groups), 1) == b * (blk // gw) + iota((blk, groups), 0) // gw)
            pick = pick.astype(f32).astype(bf16)
            for t in range(9):
                values = dot_nt(pick, wg_ref[t * pair : (t + 1) * pair, :])
                values = jnp.where(same_out, values, 0.0).astype(bf16)
                dense = dot_nn(values, spread)
                taps[t, b * blk : (b + 1) * blk, :] = jnp.where(same, dense, 0.0).astype(bf16)

    def shifter(count):
        prow = lax.broadcasted_iota(jnp.int32, (count, blk), 0)
        p_w = prow % side
        p_h = (prow // side) % side

        def moved(x, a, b):
            shift = (side * a + b) % count
            if shift:
                x = pltpu.roll(x, shift, 0)
            if a:
                x = jnp.where(p_h >= 1 if a == 1 else p_h < side - 1, x, 0.0)
            if b:
                x = jnp.where(p_w >= 1 if b == 1 else p_w < side - 1, x, 0.0)
            return x

        return moved

    def prepare_first():
        moved = shifter(rows)
        for b in range(blocks):
            first = jnp.maximum(first_ref[:, b * blk : (b + 1) * blk], 0).astype(f32)
            for t, (da, db) in enumerate(tap_offsets):
                ft[t, b] = moved(first, -da, -db).T.astype(bf16)

    hop_copies = [
        remote(ng.at[c, part(q)], inc.at[c, part(q)],
               hop_send.at[q], hop_recv.at[q], {"section": lax.max(s - 1, 0)})
        for q in range(2)
    ]
    fwd_copies = [
        remote(inc.at[c, part(q)], inc.at[c, part(q)],
               fwd_send.at[q], fwd_recv.at[q], {"chan": other})
        for q in range(2)
    ]

    @pl.when(s == last)
    def _():
        loaded("out", "wl", "teacher", "top", "wg", "first", "we0", "we1")
        feature = jnp.maximum(out_ref[...], 0)
        lateral = dot_nn(feature, wl_ref[...])
        error = (mask[:, 0:1] * (lateral - teacher_ref[...].astype(f32))).astype(bf16)
        imitation = dot_nt(error, wl_ref[...])
        build_taps()
        for copy in cnt_copies:
            copy.wait_recv()
        bulk_start()
        covered = cnt[0]
        for j in range(1, n):
            covered = covered + cnt[j]
        scale = (imitation_weight * pixels) / covered[0:1, 0:1]
        start = (top_ref[...].astype(f32) + imitation * scale).astype(bf16)
        start = jnp.where(out_ref[...] > 0, start, jnp.zeros_like(start))
        pas[0] = start[:, :half]
        pas[1] = start[:, half:]

    @pl.when(s < last)
    def _():
        bulk_start()
        loaded("out", "wl", "teacher", "top", "wg", "first", "we0", "we1")
        build_taps()
        prepare_first()
        sec_forward()
        bi_forward()
        for q in range(2):
            hop_copies[q].wait_recv()
            fwd_copies[q].start()
        own_gate = out_ref[:, pl.ds(pl.multiple_of(c * half, half), half)] > 0
        pas[c] = jnp.where(own_gate, inc[c], jnp.zeros_like(inc[c]))

    ps_copies = dp_copies(2, lambda to: ps_send.at[to, mine], ps_all.at[me, mine])
    ps_shares = share_copies(1, ps_all)
    d_moves = [[line(1, step, q, d_all) for q in range(2)] for step in range(n - 1)]
    dfx_copies = [remote(d_all.at[me, part(q)], dfx.at[part(q)],
                         core_send.at[1 + q], core_recv.at[1 + q], {"chan": other})
                  for q in range(2)]
    ng_copies = [remote(ng.at[c, part(q)], ng.at[c, part(q)],
                        core_send.at[3 + q], core_recv.at[3 + q], {"chan": other})
                 for q in range(2)]

    moved = shifter(hrows)
    second_own = dot_nt(pas[c], we_ref[c])
    for q in range(2):
        lo, hi = q * hrows, (q + 1) * hrows

        @pl.when(s < last)
        def _():
            fwd_copies[q].wait_recv()
            gate = out_ref[lo:hi, pl.ds(pl.multiple_of(other * half, half), half)] > 0
            value = inc[other, lo:hi]
            pas[other, lo:hi] = jnp.where(gate, value, jnp.zeros_like(value))

        for j in range(n):
            at = (j * share) // half
            ps_send[j, lo:hi] = pas[at, lo:hi, j * share - at * half : (j + 1) * share - at * half]
        ps_all[me, lo:hi] = ps_send[me, lo:hi]

        @pl.when(c == q)
        def _():
            for copy in ps_copies:
                copy.start()

        second_full = second_own[lo:hi] + dot_nt(pas[other, lo:hi], we_ref[other])
        d_second = jnp.where(second_ref[lo:hi] > 0, second_full, 0.0).astype(bf16)
        ds[lo:hi] = d_second
        for b in range(blocks):
            lhs = d_second[:, b * blk : (b + 1) * blk]
            total = None
            for db in (-1, 0, 1):
                column = None
                for da in (-1, 0, 1):
                    t = 3 * (da + 1) + db + 1
                    y = moved(dot_nn(lhs, taps[t, b * blk : (b + 1) * blk, :]), da, 0)
                    column = y if column is None else column + y
                column = moved(column, 0, db)
                total = column if total is None else total + column
            d_all[me, lo:hi, b * blk : (b + 1) * blk] = jnp.where(
                first_ref[lo:hi, b * blk : (b + 1) * blk] > 0, total, 0.0).astype(bf16)
        dfx_copies[q].start()
        if n > 1:
            line_start(d_moves[0][q])

    own_rows = pl.ds(pl.multiple_of(c * half, half), half)
    grad = dot_nt(d_all[me], wr_ref[own_rows, :]) + pas[c].astype(f32)
    wr_copy.wait_recv()
    for q in range(2):
        lo, hi = q * hrows, (q + 1) * hrows
        dfx_copies[q].wait_recv()
        ng[c, lo:hi] = (grad[lo:hi] + dot_nt(dfx[lo:hi], wr_peer[...])).astype(bf16)

        @pl.when(s > 0)
        def _():
            hop_copies[q].start()

        ng_copies[q].start()

    @pl.when(s == last)
    def _():
        prepare_first()

    gf[...] = jnp.zeros_like(gf)
    for b in range(blocks):
        rhs = ds[:, b * blk : (b + 1) * blk]
        for t in range(9):
            dense = jnp.where(same, dot_nn(ft[t, b], rhs), 0.0)
            folded = jnp.sum(dense.reshape(blk // gw, gw, blk), axis=0)
            for j in range(n):
                gf[j, t * k : (t + 1) * k, b * blk : (b + 1) * blk] = folded[j * k : (j + 1) * k]
    g_send[...] = gf[...].astype(bf16)
    g_copies = dp_copies(3, lambda to: g_send.at[to], g_all.at[me])
    for copy in g_copies:
        copy.start()

    @pl.when(s == last)
    def _():
        sec_forward()
        bi_forward()

    def d_forward(step):
        for q in range(2):
            line_recv(d_moves[step][q])
            line_start(d_moves[step + 1][q])

    if n > 2:
        d_forward(0)
    for copy, share_copy in zip(ps_copies, ps_shares):
        copy.wait_recv()
        share_copy.start()
    for q in range(2):
        ng_copies[q].wait_recv()
    grads_ref[:, :half] = ng[0]
    grads_ref[:, half:] = ng[1]
    if n > 1:
        for q in range(2):
            line_recv(sec_moves[n - 2][q])
    for copy in ps_shares:
        copy.wait_recv()
    expand = dot_tn(sec_all[...].reshape(n * rows, width), ps_all[...].reshape(n * rows, share))
    expand_ref[...] = expand * norm
    for step in range(1, n - 2):
        d_forward(step)
    for copy in bi_shares:
        copy.wait_recv()
    for copy in g_copies:
        copy.wait_recv()
    g_all[me] = jnp.zeros(g_all.shape[1:], bf16)
    total = gf[me]
    for j in range(n):
        total = total + g_all[j].astype(f32)
    total = (total * norm)[: 9 * k]
    wide = jnp.broadcast_to(total[:, None, :], (9 * k, gw, width)).reshape(9 * k * gw, width)
    out_of = iota((9 * k * gw, width), 0) % gw == iota((9 * k * gw, width), 1) % gw
    wide = jnp.where(out_of, wide, 0.0)
    high = wide.astype(bf16)
    low = (wide - high.astype(f32)).astype(bf16)
    group_of = (iota((width, groups), 0) // gw == iota((width, groups), 1)).astype(f32).astype(bf16)
    group_ref[...] = dot_nn(high, group_of) + dot_nn(low, group_of)
    if n > 1:
        for q in range(2):
            line_recv(d_moves[n - 2][q])
    reduced = dot_tn(bi_all[...].reshape(n * rows, share), d_all[...].reshape(n * rows, width))
    reduce_ref[...] = reduced * norm

    for steps in (sec_moves, d_moves):
        for step_moves in steps:
            for move in step_moves:
                for copy, sends, _ in move:
                    pl.when(sends)(copy.wait_send)
    for copy in bi_shares + ps_shares + bi_copies + ps_copies + g_copies:
        copy.wait_send()
    for copy in [wr_copy] + dfx_copies + ng_copies:
        copy.wait_send()

    @pl.when(s == last)
    def _():
        for copy in cnt_copies:
            copy.wait_send()

    @pl.when(s > 0)
    def _():
        for copy in hop_copies:
            copy.wait_send()

    @pl.when(s < last)
    def _():
        for copy in fwd_copies:
            copy.wait_send()


def store_kernel(*refs):
    count = (len(refs) - 1) // 2
    copies = [pltpu.make_async_copy(refs[i], refs[count + i], refs[-1].at[i]) for i in range(count)]
    for copy in copies:
        copy.start()
    for copy in copies:
        copy.wait()


def on_device(
    block_inputs, out_pre, first_pre, second_pre, w_reduce, w_group, w_expand, w_lateral,
    teacher, top_grad, boxes, region_counts,
):
    n = lax.axis_size("dp")
    sections = lax.axis_size("section")
    crops, side, _, channels = top_grad.shape
    rows = crops * side * side
    width = first_pre.shape[4]
    lateral_width = w_lateral.shape[1]
    groups, gw = w_group.shape[2], w_group.shape[3]
    slots = boxes.shape[1]
    pixels = rows * n
    share = channels // n
    k = gw // n
    grows = -(-9 * k // 8) * 8
    half = channels // 2
    blk = min(256, width)
    hbm = pl.BlockSpec(memory_space=pltpu.HBM)
    vmem = pl.BlockSpec(memory_space=pltpu.VMEM)
    dma = pltpu.SemaphoreType.DMA
    peers = max(n - 1, 1)
    shapes = (
        ((rows, channels), bf16), ((share, width), f32),
        ((9 * k * gw, groups), f32), ((width, share), f32),
    )
    results = pl.pallas_call(
        functools.partial(kernel, (n, sections, crops, side, slots, pixels)),
        out_shape=tuple(pltpu.VMEM(shape, kind) for shape, kind in shapes),
        in_specs=[hbm] * 12,
        out_specs=(vmem,) * 4,
        scratch_shapes=[
            pltpu.SMEM((crops, 4, slots), jnp.int32),
            pltpu.SMEM((1, crops), jnp.int32),
            pltpu.VMEM((rows, channels), bf16),
            pltpu.VMEM((rows, channels), bf16),
            pltpu.VMEM((rows, width), bf16),
            pltpu.VMEM((rows, width), bf16),
            pltpu.VMEM((channels, width), bf16),
            pltpu.VMEM((9 * gw * gw, groups), bf16),
            pltpu.VMEM((2, width, half), bf16),
            pltpu.VMEM((channels, lateral_width), bf16),
            pltpu.VMEM((rows, lateral_width), bf16),
            pltpu.VMEM((rows, channels), bf16),
            dma((13,)),
            pltpu.VMEM((2, rows, half), bf16),
            pltpu.VMEM((2, rows, half), bf16),
            pltpu.VMEM((half, width), bf16),
            pltpu.VMEM((rows, width), bf16),
            pltpu.VMEM((2, rows, half), bf16),
            pltpu.VMEM((rows, width), bf16),
            pltpu.VMEM((n, rows, width), bf16),
            pltpu.VMEM((n, rows, width), bf16),
            pltpu.VMEM((n, rows, share), bf16),
            pltpu.VMEM((n, rows, share), bf16),
            pltpu.VMEM((n, rows, share), bf16),
            pltpu.VMEM((n, rows, share), bf16),
            pltpu.VMEM((n, grows, width), f32),
            pltpu.VMEM((n, grows, width), bf16),
            pltpu.VMEM((n, grows, width), bf16),
            pltpu.VMEM((n, 8, 128), f32),
            pltpu.VMEM((9, width, blk), bf16),
            pltpu.VMEM((9, width // blk, blk, rows), bf16),
            dma((4, peers)), dma((4, peers)), dma((5,)), dma((5,)),
            dma((2,)), dma((2,)), dma((2,)), dma((2,)),
            dma((2, peers, 2)), dma((2, peers, 2)), dma((2, peers, 2)), dma((2, peers, 2)),
            dma((2, peers)), dma((2, peers)),
        ],
        compiler_params=pltpu.CompilerParams(
            collective_id=0, has_side_effects=True, vmem_limit_bytes=44 << 20,
        ),
    )(*(pltpu.with_memory_space_constraint(x, pltpu.HBM) for x in (
        boxes.transpose(0, 2, 1), region_counts.reshape(1, crops),
        block_inputs.reshape(rows, channels), out_pre.reshape(rows, channels),
        first_pre.reshape(rows, width), second_pre.reshape(rows, width),
        w_reduce[0], w_group[0].transpose(0, 2, 3, 1).reshape(9 * gw * gw, groups), w_expand[0], w_lateral,
        teacher.reshape(rows, lateral_width), top_grad.reshape(rows, channels),
    )))
    grads, reduced, group, expand = pl.pallas_call(
        store_kernel,
        out_shape=tuple(jax.ShapeDtypeStruct(shape, kind) for shape, kind in shapes),
        in_specs=[vmem] * 4,
        out_specs=(hbm,) * 4,
        scratch_shapes=[dma((4,))],
    )(*(pltpu.with_memory_space_constraint(x, pltpu.VMEM) for x in results))
    group = group.reshape(9, k, gw, groups).transpose(0, 3, 1, 2)
    return (
        grads.reshape(1, crops, side, side, channels), reduced[None], group[None], expand[None],
    )


def solution(mesh):
    return jax.shard_map(
        on_device,
        mesh=mesh,
        in_specs=(
            P("section", ("parts", "dp"), None, None, None),
            P("section", ("parts", "dp"), None, None, None),
            P("section", ("parts", "dp"), None, None, "chan"),
            P("section", ("parts", "dp"), None, None, "chan"),
            P("section", None, "chan"),
            P("section", None, "chan", None, None),
            P("section", "chan", None),
            P(),
            P(("parts", "dp"), None, None, None),
            P(("parts", "dp"), None, None, None),
            P(("parts", "dp"), None, None),
            P(("parts", "dp")),
        ),
        out_specs=(
            P("section", ("parts", "dp"), None, None, None),
            P(("parts", "section"), "dp", "chan"),
            P(("parts", "section"), None, "chan", "dp", None),
            P(("parts", "section"), "chan", "dp"),
        ),
        check_vma=False,
    )
```

```python
import functools
import math

import jax
import jax.numpy as jnp
from jax import lax
from jax.experimental import pallas as pl
from jax.experimental.pallas import tpu as pltpu
from jax.sharding import PartitionSpec as P

imitation_weight = 0.5
tap_offsets = [(tap // 3 - 1, tap % 3 - 1) for tap in range(9)]
f32 = jnp.float32
bf16 = jnp.bfloat16


def dot_nn(a, b):
    return lax.dot_general(a, b, (((1,), (0,)), ((), ())), preferred_element_type=f32)


def dot_nt(a, b):
    return lax.dot_general(a, b, (((1,), (1,)), ((), ())), preferred_element_type=f32)


def dot_tn(a, b):
    return lax.dot_general(a, b, (((0,), (0,)), ((), ())), preferred_element_type=f32)


def kernel(
    dims,
    boxes_hbm, counts_hbm, bi_hbm, out_hbm, first_hbm, second_hbm, wr_hbm, wg_hbm, we_hbm,
    wl_hbm, teacher_hbm, top_hbm,
    grads_ref, reduce_ref, group_ref, expand_ref,
    boxes_ref, counts_ref,
    full_ref, part_ref, wr_ref, wg_ref, we_ref, wl_ref, teacher_ref, load_sem,
    inc, pas, wr_peer, dfx, ng, ds, d_all, sec_all, bi_send, bi_all, ps_send, ps_all,
    gf, g_send, g_recv, cnt, taps, ft,
    dp_send, dp_recv, core_send, core_recv, hop_send, hop_recv, fwd_send, fwd_recv,
    sec_send, sec_recv, d_send, d_recv, gs_send, gs_recv, share_send, share_recv,
):
    n, sections, crops, side, slots, pixels = dims
    bi_ref, out_ref, top_ref = (full_ref.at[i] for i in range(3))
    first_ref, second_ref = part_ref.at[0], part_ref.at[1]
    rows, channels = bi_ref.shape
    half = channels // 2
    quarter = half // 2
    width = first_ref.shape[1]
    cols = width // 2
    groups = wg_ref.shape[1]
    gw = width // groups
    blk = taps.shape[2]
    blocks = width // blk
    cells = side * side
    share = channels // n
    k = gw // n
    hrows = rows // 2
    me = lax.axis_index("dp")
    s = lax.axis_index("section")
    c = lax.axis_index("chan")
    other = 1 - c
    last = sections - 1
    norm = 1.0 / math.sqrt(pixels)

    def remote(src, dst, send, recv, where):
        return pltpu.make_async_remote_copy(
            src_ref=src, dst_ref=dst, send_sem=send, recv_sem=recv,
            device_id=where, device_id_type=pl.DeviceIdType.MESH,
        )

    class Spread:
        def __init__(self, what, src_of, dst, sent, received):
            self.copies = [
                remote(src_of(to), dst, dp_send.at[what], dp_recv.at[what], {"dp": to})
                for to in (lax.rem(me + step, n) for step in range(1, n))
            ]
            self.sent = pltpu.make_async_copy(sent, sent, dp_send.at[what])
            self.received = pltpu.make_async_copy(received, received, dp_recv.at[what])

        def start(self):
            for copy in self.copies:
                copy.start()

        def wait_recv(self):
            self.received.wait()

        def wait_send(self):
            self.sent.wait()

    mine = pl.ds(pl.multiple_of(c * hrows, hrows), hrows)
    peers = pl.ds(0, n - 1)

    def share_copy(which, buf):
        return remote(buf.at[:, mine], buf.at[:, mine], share_send.at[which],
                      share_recv.at[which], {"chan": other})

    def line(step, block, send, recv):
        ahead = block(lax.max(me - step, 0))
        behind = block(lax.min(me + step, n - 1))
        right = remote(ahead, ahead, send.at[0], recv.at[0], {"dp": lax.min(me + 1, n - 1)})
        left = remote(behind, behind, send.at[1], recv.at[1], {"dp": lax.max(me - 1, 0)})
        return (
            (right, (me - step >= 0) & (me + 1 < n), me - 1 - step >= 0),
            (left, (me + step < n) & (me >= 1), me + 1 + step < n),
        )

    def line_start(moves):
        for copy, sends, _ in moves:
            pl.when(sends)(copy.start)

    def line_recv(moves):
        for copy, _, receives in moves:
            pl.when(receives)(copy.wait_recv)

    barrier = pltpu.get_barrier_semaphore()
    mesh_type = pl.DeviceIdType.MESH
    for step in range(1, n):
        pl.semaphore_signal(barrier, inc=1, device_id={"dp": lax.rem(me + step, n)},
                            device_id_type=mesh_type)
    pl.semaphore_signal(barrier, inc=1, device_id={"chan": other}, device_id_type=mesh_type)

    @pl.when(s > 0)
    def _():
        pl.semaphore_signal(barrier, inc=1, device_id={"section": s - 1},
                            device_id_type=mesh_type)

    @pl.when(s < last)
    def _():
        pl.semaphore_signal(barrier, inc=1, device_id={"section": s + 1},
                            device_id_type=mesh_type)

    pairs = (
        ("boxes", boxes_hbm, boxes_ref), ("counts", counts_hbm, counts_ref),
        ("full", out_hbm, out_ref), ("wl", wl_hbm, wl_ref), ("teacher", teacher_hbm, teacher_ref),
        ("part", second_hbm, second_ref), ("full", bi_hbm, bi_ref), ("full", top_hbm, top_ref),
        ("wg", wg_hbm, wg_ref), ("we", we_hbm.at[:, :half], we_ref.at[0]),
        ("we", we_hbm.at[:, half:], we_ref.at[1]), ("part", first_hbm, first_ref),
        ("wr", wr_hbm, wr_ref),
    )
    whole = {
        "boxes": boxes_ref, "counts": counts_ref, "full": full_ref, "part": part_ref, "wl": wl_ref,
        "teacher": teacher_ref, "wg": wg_ref, "we": we_ref, "wr": wr_ref,
    }
    load_at = {name: load_sem.at[i] for i, name in enumerate(whole)}
    for name, a, b in pairs:
        pltpu.make_async_copy(a, b, load_at[name]).start()

    def loaded(*names):
        for name in names:
            pltpu.make_async_copy(whole[name], whole[name], load_at[name]).wait()

    loaded("boxes", "counts")
    row = lax.broadcasted_iota(jnp.int32, (cells, 128), 0)
    row_h, row_w = row // side, row % side
    masks = []
    for crop in range(crops):
        inside = jnp.zeros((cells, 128), f32)
        for r in range(slots):
            hit = ((row_h >= boxes_ref[crop, 0, r]) & (row_h < boxes_ref[crop, 1, r])
                   & (row_w >= boxes_ref[crop, 2, r]) & (row_w < boxes_ref[crop, 3, r])
                   & (counts_ref[0, crop] > r))
            inside = jnp.where(hit, 1.0, inside)
        masks.append(inside)
    mask = jnp.concatenate(masks, axis=0)
    cnt[me] = jnp.broadcast_to(jnp.sum(mask, axis=0, keepdims=True), (8, 128))

    pl.semaphore_wait(barrier, n + jnp.where(s > 0, 1, 0) + jnp.where(s < last, 1, 0))

    cnt_copies = Spread(0, lambda to: cnt.at[me], cnt.at[me], cnt.at[peers], cnt.at[peers])

    @pl.when(s == last)
    def _():
        cnt_copies.start()

    loaded("full", "part", "wr")
    sec_all[me] = jnp.maximum(second_ref[...], 0)
    for j in range(n):
        bi_send[j] = bi_ref[:, j * share : (j + 1) * share]
    bi_all[me, mine] = bi_send[me, mine]

    wr_copy = remote(wr_ref.at[pl.ds(pl.multiple_of(other * half, half), half)], wr_peer,
                     core_send.at[0], core_recv.at[0], {"chan": other})
    sec_moves = [line(step, lambda j: sec_all.at[j], sec_send.at[step], sec_recv.at[step])
                 for step in range(n - 1)]
    bi_copies = Spread(1, lambda to: bi_send.at[to, mine], bi_all.at[me, mine],
                       bi_all.at[peers, mine], bi_all.at[peers, mine])
    bi_share = share_copy(0, bi_all)

    def bulk_start():
        line_start(sec_moves[0])
        bi_copies.start()
        wr_copy.start()

    def sec_forward(step):
        line_recv(sec_moves[step])
        line_start(sec_moves[step + 1])

    def bi_forward():
        bi_copies.wait_recv()
        bi_share.start()

    pair = gw * gw
    iota = lambda shape, dim: lax.broadcasted_iota(jnp.int32, shape, dim)
    same = iota((blk, blk), 0) // gw == iota((blk, blk), 1) // gw

    def build_taps():
        same_out = iota((blk, pair), 0) % gw == iota((blk, pair), 1) % gw
        spread = (iota((pair, blk), 0) // gw == iota((pair, blk), 1) % gw).astype(f32).astype(bf16)
        for b in range(blocks):
            pick = (iota((blk, groups), 1) == b * (blk // gw) + iota((blk, groups), 0) // gw)
            pick = pick.astype(f32).astype(bf16)
            for t in range(9):
                values = dot_nt(pick, wg_ref[t * pair : (t + 1) * pair, :])
                values = jnp.where(same_out, values, 0.0).astype(bf16)
                dense = dot_nn(values, spread)
                taps[t, b * blk : (b + 1) * blk, :] = jnp.where(same, dense, 0.0).astype(bf16)

    def shifter(count):
        prow = lax.broadcasted_iota(jnp.int32, (count, blk), 0)
        p_w = prow % side
        p_h = (prow // side) % side

        def moved(x, a, b):
            shift = (side * a + b) % count
            if shift:
                x = pltpu.roll(x, shift, 0)
            if a:
                x = jnp.where(p_h >= 1 if a == 1 else p_h < side - 1, x, 0.0)
            if b:
                x = jnp.where(p_w >= 1 if b == 1 else p_w < side - 1, x, 0.0)
            return x

        return moved

    def prepare_first():
        moved = shifter(rows)
        for b in range(blocks):
            first = jnp.maximum(first_ref[:, b * blk : (b + 1) * blk], 0).astype(f32)
            for t, (da, db) in enumerate(tap_offsets):
                ft[t, b] = moved(first, -da, -db).T.astype(bf16)

    hop_copies = [
        remote(ng.at[c, q], inc.at[c, q],
               hop_send.at[q], hop_recv.at[q], {"section": lax.max(s - 1, 0)})
        for q in range(2)
    ]
    fwd_copies = [
        remote(inc.at[c, q], inc.at[c, q],
               fwd_send.at[q], fwd_recv.at[q], {"chan": other})
        for q in range(2)
    ]

    @pl.when(s == last)
    def _():
        loaded("wl", "teacher", "wg", "we")
        feature = jnp.maximum(out_ref[...], 0)
        lateral = dot_nn(feature, wl_ref[...])
        error = (mask[:, 0:1] * (lateral - teacher_ref[...].astype(f32))).astype(bf16)
        imitation = dot_nt(error, wl_ref[...])
        build_taps()
        cnt_copies.wait_recv()
        bulk_start()
        covered = cnt[0]
        for j in range(1, n):
            covered = covered + cnt[j]
        scale = (imitation_weight * pixels) / covered[0:1, 0:1]
        start = (top_ref[...].astype(f32) + imitation * scale).astype(bf16)
        start = jnp.where(out_ref[...] > 0, start, jnp.zeros_like(start))
        for p in range(4):
            pas[p // 2, p % 2] = start[:, p * quarter : (p + 1) * quarter]

    @pl.when(s < last)
    def _():
        bulk_start()
        loaded("wl", "teacher", "wg", "we")
        build_taps()
        prepare_first()
        for step in range(n - 2):
            sec_forward(step)
        bi_forward()

    ps_copies = Spread(2, lambda to: ps_send.at[to, mine], ps_all.at[me, mine],
                       ps_all.at[peers, mine], ps_all.at[peers, mine])
    ps_share = share_copy(1, ps_all)
    d_moves = [[line(step, lambda j, q=q: d_all.at[q, j], d_send.at[step, q], d_recv.at[step, q])
                for q in range(2)] for step in range(n - 1)]
    dfx_copies = [remote(d_all.at[q, me], dfx.at[q], core_send.at[1 + q], core_recv.at[1 + q],
                         {"chan": other}) for q in range(2)]
    ng_copy = remote(ng.at[c], ng.at[c], core_send.at[3], core_recv.at[3], {"chan": other})

    def gate_quarter(h, q):
        at = pl.ds(pl.multiple_of(h * half + q * quarter, quarter), quarter)
        value = inc[h, q]
        pas[h, q] = jnp.where(out_ref[:, at] > 0, value, jnp.zeros_like(value))

    second_full = None
    for h, copies in ((c, hop_copies), (other, fwd_copies)):
        for q in range(2):
            @pl.when(s < last)
            def _():
                copies[q].wait_recv()
                if copies is hop_copies:
                    fwd_copies[q].start()
                gate_quarter(h, q)

            if copies is fwd_copies and q == 1:
                for j in range(n):
                    at = (j * share) // quarter
                    lo = j * share - at * quarter
                    ps_send[j] = pas[at // 2, at % 2, :, lo : lo + share]
                ps_all[me, mine] = ps_send[me, mine]
                ps_copies.start()

            term = dot_nt(pas[h, q], we_ref[h, :, q * quarter : (q + 1) * quarter])
            second_full = term if second_full is None else second_full + term

    moved = shifter(rows)
    for q in range(2):
        for b in range(q * blocks // 2, (q + 1) * blocks // 2):
            lo, hi = b * blk, (b + 1) * blk
            lhs = jnp.where(second_ref[:, lo:hi] > 0, second_full[:, lo:hi], 0.0).astype(bf16)
            ds[:, lo:hi] = lhs
            total = None
            for db in (-1, 0, 1):
                column = None
                for da in (-1, 0, 1):
                    t = 3 * (da + 1) + db + 1
                    y = moved(dot_nn(lhs, taps[t, lo:hi, :]), da, 0)
                    column = y if column is None else column + y
                column = moved(column, 0, db)
                total = column if total is None else total + column
            d_all[q, me, :, lo - q * cols : hi - q * cols] = jnp.where(
                first_ref[:, lo:hi] > 0, total, 0.0).astype(bf16)
        dfx_copies[q].start()
        if n > 1:
            line_start(d_moves[0][q])

    own_rows = pl.ds(pl.multiple_of(c * half, half), half)
    grad = dot_nt(d_all[0, me], wr_ref[own_rows, :cols]) + dot_nt(d_all[1, me], wr_ref[own_rows, cols:])
    wr_copy.wait_recv()
    for q in range(2):
        dfx_copies[q].wait_recv()
    for q in range(2):
        at = slice(q * quarter, (q + 1) * quarter)
        piece = grad[:, at] + pas[c, q].astype(f32)
        for p in range(2):
            piece = piece + dot_nt(dfx[p], wr_peer[at, p * cols : (p + 1) * cols])
        ng[c, q] = piece.astype(bf16)

        @pl.when(s > 0)
        def _():
            hop_copies[q].start()

    ng_copy.start()

    @pl.when(s == last)
    def _():
        prepare_first()

    gf[...] = jnp.zeros_like(gf)
    for b in range(blocks):
        rhs = ds[:, b * blk : (b + 1) * blk]
        for t in range(9):
            dense = jnp.where(same, dot_nn(ft[t, b], rhs), 0.0)
            folded = jnp.sum(dense.reshape(blk // gw, gw, blk), axis=0)
            for j in range(n):
                gf[j, t * k : (t + 1) * k, b * blk : (b + 1) * blk] = folded[j * k : (j + 1) * k]

    g_moves = [[remote(g_send.at[way, e], g_recv.at[way, e], gs_send.at[way, e], gs_recv.at[way, e],
                       {"dp": lax.min(me + 1, n - 1) if way == 0 else lax.max(me - 1, 0)})
                for e in range(n - 1)] for way in range(2)]

    def g_target(way, e):
        return me + e if way == 0 else me - e

    def within(j):
        return (j >= 0) & (j < n)

    def g_start(way, e, add):
        j = g_target(way, e + 1)

        @pl.when(within(j))
        def _():
            value = gf[lax.clamp(0, j, n - 1)]
            if add:
                value = value + g_recv[way, e + 1].astype(f32)
            g_send[way, e] = value.astype(bf16)
            g_moves[way][e].start()

    def g_arrived(way):
        return me > 0 if way == 0 else me < n - 1

    def g_forward():
        for way in range(2):
            @pl.when(g_arrived(way))
            def _():
                for e in range(n - 1):
                    pl.when(within(g_target(way, e)))(g_moves[way][e].wait_recv)
                for e in range(n - 2):
                    g_start(way, e, True)

    for way in range(2):
        @pl.when(jnp.logical_not(g_arrived(way)))
        def _():
            for e in range(n - 1):
                g_start(way, e, False)
            g_recv[way, 0] = jnp.zeros(g_recv.shape[2:], bf16)

    ps_copies.wait_recv()
    ps_share.start()

    @pl.when(s == last)
    def _():
        if n > 2:
            sec_forward(0)
        bi_forward()

    def d_forward(step):
        for q in range(2):
            line_recv(d_moves[step][q])
            line_start(d_moves[step + 1][q])

    if n > 2:
        d_forward(0)
    g_forward()

    @pl.when(s == last)
    def _():
        for step in range(1, n - 2):
            sec_forward(step)

    ng_copy.wait_recv()
    for p in range(4):
        grads_ref[:, p * quarter : (p + 1) * quarter] = ng[p // 2, p % 2]
    for step in range(1, n - 2):
        d_forward(step)
    if n > 1:
        line_recv(sec_moves[n - 2])
    ps_share.wait_recv()
    expand = dot_tn(sec_all[...].reshape(n * rows, width), ps_all[...].reshape(n * rows, share))
    expand_ref[...] = expand * norm
    bi_share.wait_recv()

    total = gf[me] + g_recv[0, 0].astype(f32) + g_recv[1, 0].astype(f32)
    total = (total * norm)[: 9 * k]
    wide = jnp.broadcast_to(total[:, None, :], (9 * k, gw, width)).reshape(9 * k * gw, width)
    out_of = iota((9 * k * gw, width), 0) % gw == iota((9 * k * gw, width), 1) % gw
    wide = jnp.where(out_of, wide, 0.0)
    high = wide.astype(bf16)
    low = (wide - high.astype(f32)).astype(bf16)
    group_of = (iota((width, groups), 0) // gw == iota((width, groups), 1)).astype(f32).astype(bf16)
    group_ref[...] = dot_nn(high, group_of) + dot_nn(low, group_of)
    for q in range(2):
        if n > 1:
            line_recv(d_moves[n - 2][q])
        reduced = dot_tn(bi_all[...].reshape(n * rows, share), d_all[q].reshape(n * rows, cols))
        reduce_ref[:, q * cols : (q + 1) * cols] = reduced * norm

    for move in sec_moves + [move for step_moves in d_moves for move in step_moves]:
        for copy, sends, _ in move:
            pl.when(sends)(copy.wait_send)
    for way in range(2):
        for e in range(n - 1):
            pl.when(within(g_target(way, e + 1)))(g_moves[way][e].wait_send)
    for copy in [bi_share, ps_share, bi_copies, ps_copies, wr_copy, ng_copy] + dfx_copies:
        copy.wait_send()

    @pl.when(s == last)
    def _():
        cnt_copies.wait_send()

    @pl.when(s > 0)
    def _():
        for copy in hop_copies:
            copy.wait_send()

    @pl.when(s < last)
    def _():
        for copy in fwd_copies:
            copy.wait_send()


def store_kernel(*refs):
    count = (len(refs) - 1) // 2
    copies = [pltpu.make_async_copy(refs[i], refs[count + i], refs[-1].at[i]) for i in range(count)]
    for copy in copies:
        copy.start()
    for copy in copies:
        copy.wait()


def on_device(
    block_inputs, out_pre, first_pre, second_pre, w_reduce, w_group, w_expand, w_lateral,
    teacher, top_grad, boxes, region_counts,
):
    n = lax.axis_size("dp")
    sections = lax.axis_size("section")
    crops, side, _, channels = top_grad.shape
    rows = crops * side * side
    width = first_pre.shape[4]
    lateral_width = w_lateral.shape[1]
    groups, gw = w_group.shape[2], w_group.shape[3]
    slots = boxes.shape[1]
    pixels = rows * n
    share = channels // n
    k = gw // n
    grows = -(-9 * k // 8) * 8
    half = channels // 2
    blk = min(256, width)
    hbm = pl.BlockSpec(memory_space=pltpu.HBM)
    vmem = pl.BlockSpec(memory_space=pltpu.VMEM)
    dma = pltpu.SemaphoreType.DMA
    peers = max(n - 1, 1)
    shapes = (
        ((rows, channels), bf16), ((share, width), f32),
        ((9 * k * gw, groups), f32), ((width, share), f32),
    )
    results = pl.pallas_call(
        functools.partial(kernel, (n, sections, crops, side, slots, pixels)),
        out_shape=tuple(pltpu.VMEM(shape, kind) for shape, kind in shapes),
        in_specs=[hbm] * 12,
        out_specs=(vmem,) * 4,
        scratch_shapes=[
            pltpu.SMEM((crops, 4, slots), jnp.int32),
            pltpu.SMEM((1, crops), jnp.int32),
            pltpu.VMEM((3, rows, channels), bf16),
            pltpu.VMEM((2, rows, width), bf16),
            pltpu.VMEM((channels, width), bf16),
            pltpu.VMEM((9 * gw * gw, groups), bf16),
            pltpu.VMEM((2, width, half), bf16),
            pltpu.VMEM((channels, lateral_width), bf16),
            pltpu.VMEM((rows, lateral_width), bf16),
            dma((9,)),
            pltpu.VMEM((2, 2, rows, half // 2), bf16),
            pltpu.VMEM((2, 2, rows, half // 2), bf16),
            pltpu.VMEM((half, width), bf16),
            pltpu.VMEM((2, rows, width // 2), bf16),
            pltpu.VMEM((2, 2, rows, half // 2), bf16),
            pltpu.VMEM((rows, width), bf16),
            pltpu.VMEM((2, n, rows, width // 2), bf16),
            pltpu.VMEM((n, rows, width), bf16),
            pltpu.VMEM((n, rows, share), bf16),
            pltpu.VMEM((n, rows, share), bf16),
            pltpu.VMEM((n, rows, share), bf16),
            pltpu.VMEM((n, rows, share), bf16),
            pltpu.VMEM((n, grows, width), f32),
            pltpu.VMEM((2, peers, grows, width), bf16),
            pltpu.VMEM((2, peers, grows, width), bf16),
            pltpu.VMEM((n, 8, 128), f32),
            pltpu.VMEM((9, width, blk), bf16),
            pltpu.VMEM((9, width // blk, blk, rows), bf16),
            dma((3,)), dma((3,)), dma((4,)), dma((4,)),
            dma((2,)), dma((2,)), dma((2,)), dma((2,)),
            dma((peers, 2)), dma((peers, 2)), dma((peers, 2, 2)), dma((peers, 2, 2)),
            dma((2, peers)), dma((2, peers)), dma((2,)), dma((2,)),
        ],
        compiler_params=pltpu.CompilerParams(
            collective_id=0, has_side_effects=True, vmem_limit_bytes=44 << 20,
        ),
    )(*(pltpu.with_memory_space_constraint(x, pltpu.HBM) for x in (
        boxes.transpose(0, 2, 1), region_counts.reshape(1, crops),
        block_inputs.reshape(rows, channels), out_pre.reshape(rows, channels),
        first_pre.reshape(rows, width), second_pre.reshape(rows, width),
        w_reduce[0], w_group[0].transpose(0, 2, 3, 1).reshape(9 * gw * gw, groups), w_expand[0], w_lateral,
        teacher.reshape(rows, lateral_width), top_grad.reshape(rows, channels),
    )))
    grads, reduced, group, expand = pl.pallas_call(
        store_kernel,
        out_shape=tuple(jax.ShapeDtypeStruct(shape, kind) for shape, kind in shapes),
        in_specs=[vmem] * 4,
        out_specs=(hbm,) * 4,
        scratch_shapes=[dma((4,))],
    )(*(pltpu.with_memory_space_constraint(x, pltpu.VMEM) for x in results))
    group = group.reshape(9, k, gw, groups).transpose(0, 3, 1, 2)
    return (
        grads.reshape(1, crops, side, side, channels), reduced[None], group[None], expand[None],
    )


def solution(mesh):
    return jax.shard_map(
        on_device,
        mesh=mesh,
        in_specs=(
            P("section", ("parts", "dp"), None, None, None),
            P("section", ("parts", "dp"), None, None, None),
            P("section", ("parts", "dp"), None, None, "chan"),
            P("section", ("parts", "dp"), None, None, "chan"),
            P("section", None, "chan"),
            P("section", None, "chan", None, None),
            P("section", "chan", None),
            P(),
            P(("parts", "dp"), None, None, None),
            P(("parts", "dp"), None, None, None),
            P(("parts", "dp"), None, None),
            P(("parts", "dp")),
        ),
        out_specs=(
            P("section", ("parts", "dp"), None, None, None),
            P(("parts", "section"), "dp", "chan"),
            P(("parts", "section"), None, "chan", "dp", None),
            P(("parts", "section"), "chan", "dp"),
        ),
        check_vma=False,
    )
```

```python
import functools
import math

import jax
import jax.numpy as jnp
from jax import lax
from jax.experimental import pallas as pl
from jax.experimental.pallas import tpu as pltpu
from jax.sharding import PartitionSpec as P

imitation_weight = 0.5
tap_offsets = [(tap // 3 - 1, tap % 3 - 1) for tap in range(9)]
f32 = jnp.float32
bf16 = jnp.bfloat16


def dot_nn(a, b):
    return lax.dot_general(a, b, (((1,), (0,)), ((), ())), preferred_element_type=f32)


def dot_nt(a, b):
    return lax.dot_general(a, b, (((1,), (1,)), ((), ())), preferred_element_type=f32)


def dot_tn(a, b):
    return lax.dot_general(a, b, (((0,), (0,)), ((), ())), preferred_element_type=f32)


def kernel(
    dims,
    boxes_hbm, counts_hbm, bi_hbm, out_hbm, first_hbm, second_hbm, wr_hbm, wg_hbm, we_hbm,
    wl_hbm, teacher_hbm, top_hbm,
    grads_ref, reduce_ref, group_ref, expand_ref,
    boxes_ref, counts_ref,
    full_ref, part_ref, wr_ref, wg_ref, we_ref, wl_ref, teacher_ref, load_sem,
    inc, pas, wr_peer, dfx, ng, ds, d_all, sec_all, bi_send, bi_all, ps_send, ps_all,
    gf, g_send, g_recv, cnt, taps, ft,
    dp_send, dp_recv, core_send, core_recv, hop_send, hop_recv, fwd_send, fwd_recv,
    sec_send, sec_recv, d_send, d_recv, share_send, share_recv,
):
    n, sections, crops, side, slots, pixels = dims
    bi_ref, out_ref, top_ref = (full_ref.at[i] for i in range(3))
    first_ref, second_ref = part_ref.at[0], part_ref.at[1]
    rows, channels = bi_ref.shape
    half = channels // 2
    quarter = half // 2
    width = first_ref.shape[1]
    cols = width // 2
    groups = wg_ref.shape[1]
    gw = width // groups
    blk = taps.shape[2]
    blocks = width // blk
    cells = side * side
    share = channels // n
    k = gw // n
    hrows = rows // 2
    me = lax.axis_index("dp")
    s = lax.axis_index("section")
    c = lax.axis_index("chan")
    other = 1 - c
    last = sections - 1
    norm = 1.0 / math.sqrt(pixels)

    def remote(src, dst, send, recv, where):
        return pltpu.make_async_remote_copy(
            src_ref=src, dst_ref=dst, send_sem=send, recv_sem=recv,
            device_id=where, device_id_type=pl.DeviceIdType.MESH,
        )

    class Spread:
        def __init__(self, what, src_of, dst, sent, received):
            self.copies = [
                remote(src_of(to), dst, dp_send.at[what], dp_recv.at[what], {"dp": to})
                for to in (lax.rem(me + step, n) for step in range(1, n))
            ]
            self.sent = pltpu.make_async_copy(sent, sent, dp_send.at[what])
            self.received = pltpu.make_async_copy(received, received, dp_recv.at[what])

        def start(self):
            for copy in self.copies:
                copy.start()

        def wait_recv(self):
            self.received.wait()

        def wait_send(self):
            self.sent.wait()

    mine = pl.ds(pl.multiple_of(c * hrows, hrows), hrows)
    peers = pl.ds(0, n - 1)

    def share_copy(which, buf):
        return remote(buf.at[:, mine], buf.at[:, mine], share_send.at[which],
                      share_recv.at[which], {"chan": other})

    def line(step, block, send, recv):
        ahead = block(lax.max(me - step, 0))
        behind = block(lax.min(me + step, n - 1))
        right = remote(ahead, ahead, send.at[0], recv.at[0], {"dp": lax.min(me + 1, n - 1)})
        left = remote(behind, behind, send.at[1], recv.at[1], {"dp": lax.max(me - 1, 0)})
        return (
            (right, (me - step >= 0) & (me + 1 < n), me - 1 - step >= 0),
            (left, (me + step < n) & (me >= 1), me + 1 + step < n),
        )

    def line_start(moves):
        for copy, sends, _ in moves:
            pl.when(sends)(copy.start)

    def line_forward(moves, following):
        for (copy, _, receives), (onward, sends, _) in zip(moves, following):
            @pl.when(receives & sends)
            def _():
                copy.wait_recv()
                onward.start()

    def line_finish(moves):
        for step in range(n - 1):
            for way, (copy, _, receives) in enumerate(moves[step]):
                if step + 1 < n - 1:
                    receives = receives & jnp.logical_not(moves[step + 1][way][1])
                pl.when(receives)(copy.wait_recv)

    barrier = pltpu.get_barrier_semaphore()
    mesh_type = pl.DeviceIdType.MESH
    for step in range(1, n):
        pl.semaphore_signal(barrier, inc=1, device_id={"dp": lax.rem(me + step, n)},
                            device_id_type=mesh_type)
    pl.semaphore_signal(barrier, inc=1, device_id={"chan": other}, device_id_type=mesh_type)

    @pl.when(s > 0)
    def _():
        pl.semaphore_signal(barrier, inc=1, device_id={"section": s - 1},
                            device_id_type=mesh_type)

    @pl.when(s < last)
    def _():
        pl.semaphore_signal(barrier, inc=1, device_id={"section": s + 1},
                            device_id_type=mesh_type)

    pairs = (
        ("boxes", boxes_hbm, boxes_ref), ("counts", counts_hbm, counts_ref),
        ("full", out_hbm, out_ref), ("wl", wl_hbm, wl_ref), ("teacher", teacher_hbm, teacher_ref),
        ("part", second_hbm, second_ref), ("full", bi_hbm, bi_ref), ("full", top_hbm, top_ref),
        ("wg", wg_hbm, wg_ref), ("we", we_hbm.at[:, :half], we_ref.at[0]),
        ("we", we_hbm.at[:, half:], we_ref.at[1]), ("part", first_hbm, first_ref),
        ("wr", wr_hbm, wr_ref),
    )
    whole = {
        "boxes": boxes_ref, "counts": counts_ref, "full": full_ref, "part": part_ref, "wl": wl_ref,
        "teacher": teacher_ref, "wg": wg_ref, "we": we_ref, "wr": wr_ref,
    }
    load_at = {name: load_sem.at[i] for i, name in enumerate(whole)}
    for name, a, b in pairs:
        pltpu.make_async_copy(a, b, load_at[name]).start()

    def loaded(*names):
        for name in names:
            pltpu.make_async_copy(whole[name], whole[name], load_at[name]).wait()

    loaded("boxes", "counts")
    row = lax.broadcasted_iota(jnp.int32, (cells, 128), 0)
    row_h, row_w = row // side, row % side
    masks = []
    for crop in range(crops):
        inside = jnp.zeros((cells, 128), f32)
        for r in range(slots):
            hit = ((row_h >= boxes_ref[crop, 0, r]) & (row_h < boxes_ref[crop, 1, r])
                   & (row_w >= boxes_ref[crop, 2, r]) & (row_w < boxes_ref[crop, 3, r])
                   & (counts_ref[0, crop] > r))
            inside = jnp.where(hit, 1.0, inside)
        masks.append(inside)
    mask = jnp.concatenate(masks, axis=0)
    cnt[me] = jnp.broadcast_to(jnp.sum(mask, axis=0, keepdims=True), (8, 128))

    pl.semaphore_wait(barrier, n + jnp.where(s > 0, 1, 0) + jnp.where(s < last, 1, 0))

    cnt_copies = Spread(0, lambda to: cnt.at[me], cnt.at[me], cnt.at[peers], cnt.at[peers])

    @pl.when(s == last)
    def _():
        cnt_copies.start()

    loaded("full", "part", "wr")
    sec_all[me] = jnp.maximum(second_ref[...], 0)
    for j in range(n):
        bi_send[j] = bi_ref[:, j * share : (j + 1) * share]
    bi_all[me, mine] = bi_send[me, mine]

    wr_copy = remote(wr_ref.at[pl.ds(pl.multiple_of(other * half, half), half)], wr_peer,
                     core_send.at[0], core_recv.at[0], {"chan": other})
    sec_moves = [line(step, lambda j: sec_all.at[j], sec_send.at[step], sec_recv.at[step])
                 for step in range(n - 1)]
    bi_copies = Spread(1, lambda to: bi_send.at[to, mine], bi_all.at[me, mine],
                       bi_all.at[peers, mine], bi_all.at[peers, mine])
    bi_share = share_copy(0, bi_all)

    def sec_forward(step):
        line_forward(sec_moves[step], sec_moves[step + 1])

    def bi_forward():
        bi_copies.wait_recv()
        bi_share.start()

    pair = gw * gw
    iota = lambda shape, dim: lax.broadcasted_iota(jnp.int32, shape, dim)
    same = iota((blk, blk), 0) // gw == iota((blk, blk), 1) // gw

    def build_taps():
        same_out = iota((blk, pair), 0) % gw == iota((blk, pair), 1) % gw
        spread = (iota((pair, blk), 0) // gw == iota((pair, blk), 1) % gw).astype(f32).astype(bf16)
        for b in range(blocks):
            pick = (iota((blk, groups), 1) == b * (blk // gw) + iota((blk, groups), 0) // gw)
            pick = pick.astype(f32).astype(bf16)
            for t in range(9):
                values = dot_nt(pick, wg_ref[t * pair : (t + 1) * pair, :])
                values = jnp.where(same_out, values, 0.0).astype(bf16)
                dense = dot_nn(values, spread)
                taps[t, b * blk : (b + 1) * blk, :] = jnp.where(same, dense, 0.0).astype(bf16)

    def shifter(count):
        prow = lax.broadcasted_iota(jnp.int32, (count, blk), 0)
        p_w = prow % side
        p_h = (prow // side) % side

        def moved(x, a, b):
            shift = (side * a + b) % count
            if shift:
                x = pltpu.roll(x, shift, 0)
            if a:
                x = jnp.where(p_h >= 1 if a == 1 else p_h < side - 1, x, 0.0)
            if b:
                x = jnp.where(p_w >= 1 if b == 1 else p_w < side - 1, x, 0.0)
            return x

        return moved

    def prepare_first():
        moved = shifter(rows)
        for b in range(blocks):
            first = jnp.maximum(first_ref[:, b * blk : (b + 1) * blk], 0).astype(f32)
            for t, (da, db) in enumerate(tap_offsets):
                ft[t, b] = moved(first, -da, -db).T.astype(bf16)

    hop_copies = [
        remote(ng.at[c, q], inc.at[c, q],
               hop_send.at[q], hop_recv.at[q], {"section": lax.max(s - 1, 0)})
        for q in range(2)
    ]
    fwd_copies = [
        remote(inc.at[c, q], inc.at[c, q],
               fwd_send.at[q], fwd_recv.at[q], {"chan": other})
        for q in range(2)
    ]

    @pl.when(s == last)
    def _():
        loaded("wl", "teacher", "wg", "we")
        feature = jnp.maximum(out_ref[...], 0)
        lateral = dot_nn(feature, wl_ref[...])
        error = (mask[:, 0:1] * (lateral - teacher_ref[...].astype(f32))).astype(bf16)
        imitation = dot_nt(error, wl_ref[...])
        build_taps()
        cnt_copies.wait_recv()
        wr_copy.start()
        bi_copies.start()
        covered = cnt[0]
        for j in range(1, n):
            covered = covered + cnt[j]
        scale = (imitation_weight * pixels) / covered[0:1, 0:1]
        start = (top_ref[...].astype(f32) + imitation * scale).astype(bf16)
        start = jnp.where(out_ref[...] > 0, start, jnp.zeros_like(start))
        for p in range(4):
            pas[p // 2, p % 2] = start[:, p * quarter : (p + 1) * quarter]

    @pl.when(s < last)
    def _():
        if n > 1:
            line_start(sec_moves[0])
        bi_copies.start()
        wr_copy.start()
        loaded("wl", "teacher", "wg", "we")
        build_taps()
        prepare_first()
        for step in range(n - 2):
            sec_forward(step)
        bi_forward()

    ps_copies = Spread(2, lambda to: ps_send.at[to, mine], ps_all.at[me, mine],
                       ps_all.at[peers, mine], ps_all.at[peers, mine])
    ps_share = share_copy(1, ps_all)
    d_moves = [[line(step, lambda j, q=q: d_all.at[q, j], d_send.at[step, q], d_recv.at[step, q])
                for q in range(2)] for step in range(n - 1)]
    dfx_copies = [remote(d_all.at[q, me], dfx.at[q], core_send.at[1 + q], core_recv.at[1 + q],
                         {"chan": other}) for q in range(2)]
    ng_copy = remote(ng.at[c], ng.at[c], core_send.at[3], core_recv.at[3], {"chan": other})

    def gate_quarter(h, q):
        at = pl.ds(pl.multiple_of(h * half + q * quarter, quarter), quarter)
        value = inc[h, q]
        pas[h, q] = jnp.where(out_ref[:, at] > 0, value, jnp.zeros_like(value))

    second_full = None
    for h, copies in ((c, hop_copies), (other, fwd_copies)):
        for q in range(2):
            @pl.when(s < last)
            def _():
                copies[q].wait_recv()
                if copies is hop_copies:
                    fwd_copies[q].start()
                gate_quarter(h, q)

            if copies is fwd_copies and q == 1:
                for j in range(n):
                    at = (j * share) // quarter
                    lo = j * share - at * quarter
                    ps_send[j] = pas[at // 2, at % 2, :, lo : lo + share]
                ps_all[me, mine] = ps_send[me, mine]
                ps_copies.start()

            term = dot_nt(pas[h, q], we_ref[h, :, q * quarter : (q + 1) * quarter])
            second_full = term if second_full is None else second_full + term

    moved = shifter(rows)
    for q in range(2):
        for b in range(q * blocks // 2, (q + 1) * blocks // 2):
            lo, hi = b * blk, (b + 1) * blk
            lhs = jnp.where(second_ref[:, lo:hi] > 0, second_full[:, lo:hi], 0.0).astype(bf16)
            ds[:, lo:hi] = lhs
            total = None
            for db in (-1, 0, 1):
                column = None
                for da in (-1, 0, 1):
                    t = 3 * (da + 1) + db + 1
                    y = moved(dot_nn(lhs, taps[t, lo:hi, :]), da, 0)
                    column = y if column is None else column + y
                column = moved(column, 0, db)
                total = column if total is None else total + column
            d_all[q, me, :, lo - q * cols : hi - q * cols] = jnp.where(
                first_ref[:, lo:hi] > 0, total, 0.0).astype(bf16)
        dfx_copies[q].start()
        if n > 1:
            @pl.when(s < last)
            def _():
                line_start(d_moves[0][q])

    own_rows = pl.ds(pl.multiple_of(c * half, half), half)
    grad = dot_nt(d_all[0, me], wr_ref[own_rows, :cols]) + dot_nt(d_all[1, me], wr_ref[own_rows, cols:])
    wr_copy.wait_recv()
    for q in range(2):
        dfx_copies[q].wait_recv()
    for q in range(2):
        at = slice(q * quarter, (q + 1) * quarter)
        piece = grad[:, at] + pas[c, q].astype(f32)
        for p in range(2):
            piece = piece + dot_nt(dfx[p], wr_peer[at, p * cols : (p + 1) * cols])
        ng[c, q] = piece.astype(bf16)

        @pl.when(s > 0)
        def _():
            hop_copies[q].start()

    ng_copy.start()

    if n > 1:
        @pl.when(s == last)
        def _():
            line_start(sec_moves[0])

    @pl.when(s == last)
    def _():
        prepare_first()

    gf[...] = jnp.zeros_like(gf)
    for b in range(blocks):
        rhs = ds[:, b * blk : (b + 1) * blk]
        for t in range(9):
            dense = jnp.where(same, dot_nn(ft[t, b], rhs), 0.0)
            folded = jnp.sum(dense.reshape(blk // gw, gw, blk), axis=0)
            for j in range(n):
                gf[j, t * k : (t + 1) * k, b * blk : (b + 1) * blk] = folded[j * k : (j + 1) * k]
    g_send[...] = gf[...].astype(bf16)
    g_copies = Spread(3, lambda to: g_send.at[to], g_recv.at[me], g_recv.at[peers], g_recv.at[peers])

    if n > 1:
        @pl.when(s == last)
        def _():
            for q in range(2):
                line_start(d_moves[0][q])

    ps_copies.wait_recv()
    ps_share.start()

    def d_forward(step):
        for q in range(2):
            line_forward(d_moves[step][q], d_moves[step + 1][q])

    for step in range(n - 2):
        @pl.when(s == last)
        def _():
            sec_forward(step)
            if step == 0:
                bi_forward()

        d_forward(step)
        if step == 0:
            ng_copy.wait_recv()
            for p in range(4):
                grads_ref[:, p * quarter : (p + 1) * quarter] = ng[p // 2, p % 2]
    g_copies.start()
    line_finish(sec_moves)
    ps_share.wait_recv()
    expand = dot_tn(sec_all[...].reshape(n * rows, width), ps_all[...].reshape(n * rows, share))
    expand_ref[...] = expand * norm
    bi_share.wait_recv()
    g_copies.wait_recv()
    g_recv[me] = jnp.zeros(g_recv.shape[1:], bf16)
    total = gf[me]
    for j in range(n):
        total = total + g_recv[j].astype(f32)
    total = (total * norm)[: 9 * k]
    wide = jnp.broadcast_to(total[:, None, :], (9 * k, gw, width)).reshape(9 * k * gw, width)
    out_of = iota((9 * k * gw, width), 0) % gw == iota((9 * k * gw, width), 1) % gw
    wide = jnp.where(out_of, wide, 0.0)
    high = wide.astype(bf16)
    low = (wide - high.astype(f32)).astype(bf16)
    group_of = (iota((width, groups), 0) // gw == iota((width, groups), 1)).astype(f32).astype(bf16)
    group_ref[...] = dot_nn(high, group_of) + dot_nn(low, group_of)
    for q in range(2):
        line_finish([step_moves[q] for step_moves in d_moves])
        reduced = dot_tn(bi_all[...].reshape(n * rows, share), d_all[q].reshape(n * rows, cols))
        reduce_ref[:, q * cols : (q + 1) * cols] = reduced * norm

    for move in sec_moves + [move for step_moves in d_moves for move in step_moves]:
        for copy, sends, _ in move:
            pl.when(sends)(copy.wait_send)
    for copy in [bi_share, ps_share, bi_copies, ps_copies, g_copies, wr_copy, ng_copy] + dfx_copies:
        copy.wait_send()

    @pl.when(s == last)
    def _():
        cnt_copies.wait_send()

    @pl.when(s > 0)
    def _():
        for copy in hop_copies:
            copy.wait_send()

    @pl.when(s < last)
    def _():
        for copy in fwd_copies:
            copy.wait_send()


def store_kernel(*refs):
    count = (len(refs) - 1) // 2
    copies = [pltpu.make_async_copy(refs[i], refs[count + i], refs[-1].at[i]) for i in range(count)]
    for copy in copies:
        copy.start()
    for copy in copies:
        copy.wait()


def on_device(
    block_inputs, out_pre, first_pre, second_pre, w_reduce, w_group, w_expand, w_lateral,
    teacher, top_grad, boxes, region_counts,
):
    n = lax.axis_size("dp")
    sections = lax.axis_size("section")
    crops, side, _, channels = top_grad.shape
    rows = crops * side * side
    width = first_pre.shape[4]
    lateral_width = w_lateral.shape[1]
    groups, gw = w_group.shape[2], w_group.shape[3]
    slots = boxes.shape[1]
    pixels = rows * n
    share = channels // n
    k = gw // n
    grows = -(-9 * k // 8) * 8
    half = channels // 2
    blk = min(256, width)
    hbm = pl.BlockSpec(memory_space=pltpu.HBM)
    vmem = pl.BlockSpec(memory_space=pltpu.VMEM)
    dma = pltpu.SemaphoreType.DMA
    peers = max(n - 1, 1)
    shapes = (
        ((rows, channels), bf16), ((share, width), f32),
        ((9 * k * gw, groups), f32), ((width, share), f32),
    )
    results = pl.pallas_call(
        functools.partial(kernel, (n, sections, crops, side, slots, pixels)),
        out_shape=tuple(pltpu.VMEM(shape, kind) for shape, kind in shapes),
        in_specs=[hbm] * 12,
        out_specs=(vmem,) * 4,
        scratch_shapes=[
            pltpu.SMEM((crops, 4, slots), jnp.int32),
            pltpu.SMEM((1, crops), jnp.int32),
            pltpu.VMEM((3, rows, channels), bf16),
            pltpu.VMEM((2, rows, width), bf16),
            pltpu.VMEM((channels, width), bf16),
            pltpu.VMEM((9 * gw * gw, groups), bf16),
            pltpu.VMEM((2, width, half), bf16),
            pltpu.VMEM((channels, lateral_width), bf16),
            pltpu.VMEM((rows, lateral_width), bf16),
            dma((9,)),
            pltpu.VMEM((2, 2, rows, half // 2), bf16),
            pltpu.VMEM((2, 2, rows, half // 2), bf16),
            pltpu.VMEM((half, width), bf16),
            pltpu.VMEM((2, rows, width // 2), bf16),
            pltpu.VMEM((2, 2, rows, half // 2), bf16),
            pltpu.VMEM((rows, width), bf16),
            pltpu.VMEM((2, n, rows, width // 2), bf16),
            pltpu.VMEM((n, rows, width), bf16),
            pltpu.VMEM((n, rows, share), bf16),
            pltpu.VMEM((n, rows, share), bf16),
            pltpu.VMEM((n, rows, share), bf16),
            pltpu.VMEM((n, rows, share), bf16),
            pltpu.VMEM((n, grows, width), f32),
            pltpu.VMEM((n, grows, width), bf16),
            pltpu.VMEM((n, grows, width), bf16),
            pltpu.VMEM((n, 8, 128), f32),
            pltpu.VMEM((9, width, blk), bf16),
            pltpu.VMEM((9, width // blk, blk, rows), bf16),
            dma((4,)), dma((4,)), dma((4,)), dma((4,)),
            dma((2,)), dma((2,)), dma((2,)), dma((2,)),
            dma((peers, 2)), dma((peers, 2)), dma((peers, 2, 2)), dma((peers, 2, 2)),
            dma((2,)), dma((2,)),
        ],
        compiler_params=pltpu.CompilerParams(
            collective_id=0, has_side_effects=True, vmem_limit_bytes=44 << 20,
        ),
    )(*(pltpu.with_memory_space_constraint(x, pltpu.HBM) for x in (
        boxes.transpose(0, 2, 1), region_counts.reshape(1, crops),
        block_inputs.reshape(rows, channels), out_pre.reshape(rows, channels),
        first_pre.reshape(rows, width), second_pre.reshape(rows, width),
        w_reduce[0], w_group[0].transpose(0, 2, 3, 1).reshape(9 * gw * gw, groups), w_expand[0], w_lateral,
        teacher.reshape(rows, lateral_width), top_grad.reshape(rows, channels),
    )))
    grads, reduced, group, expand = pl.pallas_call(
        store_kernel,
        out_shape=tuple(jax.ShapeDtypeStruct(shape, kind) for shape, kind in shapes),
        in_specs=[vmem] * 4,
        out_specs=(hbm,) * 4,
        scratch_shapes=[dma((4,))],
    )(*(pltpu.with_memory_space_constraint(x, pltpu.VMEM) for x in results))
    group = group.reshape(9, k, gw, groups).transpose(0, 3, 1, 2)
    return (
        grads.reshape(1, crops, side, side, channels), reduced[None], group[None], expand[None],
    )


def solution(mesh):
    return jax.shard_map(
        on_device,
        mesh=mesh,
        in_specs=(
            P("section", ("parts", "dp"), None, None, None),
            P("section", ("parts", "dp"), None, None, None),
            P("section", ("parts", "dp"), None, None, "chan"),
            P("section", ("parts", "dp"), None, None, "chan"),
            P("section", None, "chan"),
            P("section", None, "chan", None, None),
            P("section", "chan", None),
            P(),
            P(("parts", "dp"), None, None, None),
            P(("parts", "dp"), None, None, None),
            P(("parts", "dp"), None, None),
            P(("parts", "dp")),
        ),
        out_specs=(
            P("section", ("parts", "dp"), None, None, None),
            P(("parts", "section"), "dp", "chan"),
            P(("parts", "section"), None, "chan", "dp", None),
            P(("parts", "section"), "chan", "dp"),
        ),
        check_vma=False,
    )
```

```python
import functools
import math

import jax
import jax.numpy as jnp
from jax import lax
from jax.experimental import pallas as pl
from jax.experimental.pallas import tpu as pltpu
from jax.sharding import PartitionSpec as P

imitation_weight = 0.5
tap_offsets = [(tap // 3 - 1, tap % 3 - 1) for tap in range(9)]
f32 = jnp.float32
bf16 = jnp.bfloat16


def dot_nn(a, b):
    return lax.dot_general(a, b, (((1,), (0,)), ((), ())), preferred_element_type=f32)


def dot_nt(a, b):
    return lax.dot_general(a, b, (((1,), (1,)), ((), ())), preferred_element_type=f32)


def dot_tn(a, b):
    return lax.dot_general(a, b, (((0,), (0,)), ((), ())), preferred_element_type=f32)


def kernel(
    dims,
    boxes_hbm, counts_hbm, bi_hbm, out_hbm, first_hbm, second_hbm, wr_hbm, wg_hbm, we_hbm,
    wl_hbm, teacher_hbm, top_hbm,
    grads_ref, reduce_ref, group_ref, expand_ref,
    boxes_ref, counts_ref,
    full_ref, part_ref, wr_ref, wg_ref, we_ref, wl_ref, teacher_ref, load_sem,
    inc, pas, wr_peer, dfx, ng, ds, d_all, sec_all, bi_send, bi_all, ps_send, ps_all,
    gf, g_send, g_recv, cnt, taps, ft,
    dp_send, dp_recv, core_send, core_recv, hop_send, hop_recv, fwd_send, fwd_recv,
    sec_send, sec_recv, d_send, d_recv, share_send, share_recv,
):
    n, sections, crops, side, slots, pixels = dims
    bi_ref, out_ref, top_ref = (full_ref.at[i] for i in range(3))
    first_ref, second_ref = part_ref.at[0], part_ref.at[1]
    rows, channels = bi_ref.shape
    half = channels // 2
    quarter = half // 2
    width = first_ref.shape[1]
    cols = width // 2
    groups = wg_ref.shape[1]
    gw = width // groups
    blk = taps.shape[2]
    blocks = width // blk
    cells = side * side
    share = channels // n
    k = gw // n
    hrows = rows // 2
    me = lax.axis_index("dp")
    s = lax.axis_index("section")
    c = lax.axis_index("chan")
    other = 1 - c
    last = sections - 1
    norm = 1.0 / math.sqrt(pixels)

    def remote(src, dst, send, recv, where):
        return pltpu.make_async_remote_copy(
            src_ref=src, dst_ref=dst, send_sem=send, recv_sem=recv,
            device_id=where, device_id_type=pl.DeviceIdType.MESH,
        )

    class Spread:
        def __init__(self, what, src_of, dst, moved, at=None, where={}):
            at = what if at is None else at
            self.copies = [
                remote(src_of(to), dst, dp_send.at[at], dp_recv.at[what], {"dp": to, **where})
                for to in (lax.rem(me + step, n) for step in range(1, n))
            ]
            self.sent = pltpu.make_async_copy(moved, moved, dp_send.at[at])
            self.received = pltpu.make_async_copy(moved, moved, dp_recv.at[what])

        def start(self):
            for copy in self.copies:
                copy.start()

        def wait_recv(self):
            self.received.wait()

        def wait_send(self):
            self.sent.wait()

    mine = pl.ds(pl.multiple_of(c * hrows, hrows), hrows)
    peers = pl.ds(0, n - 1)

    def share_copy(which, buf):
        return remote(buf.at[:, mine], buf.at[:, mine], share_send.at[which],
                      share_recv.at[which], {"chan": other})

    def line(step, block, send, recv):
        ahead = block(lax.max(me - step, 0))
        behind = block(lax.min(me + step, n - 1))
        right = remote(ahead, ahead, send.at[0], recv.at[0], {"dp": lax.min(me + 1, n - 1)})
        left = remote(behind, behind, send.at[1], recv.at[1], {"dp": lax.max(me - 1, 0)})
        return (
            (right, (me - step >= 0) & (me + 1 < n), me - 1 - step >= 0),
            (left, (me + step < n) & (me >= 1), me + 1 + step < n),
        )

    def line_start(moves):
        for copy, sends, _ in moves:
            pl.when(sends)(copy.start)

    def line_forward(moves, following):
        for (copy, _, receives), (onward, sends, _) in zip(moves, following):
            @pl.when(receives & sends)
            def _():
                copy.wait_recv()
                onward.start()

    def line_finish(moves):
        for step in range(n - 1):
            for way, (copy, _, receives) in enumerate(moves[step]):
                if step + 1 < n - 1:
                    receives = receives & jnp.logical_not(moves[step + 1][way][1])
                pl.when(receives)(copy.wait_recv)

    barrier = pltpu.get_barrier_semaphore()
    mesh_type = pl.DeviceIdType.MESH
    for step in range(1, n):
        pl.semaphore_signal(barrier, inc=1, device_id={"dp": lax.rem(me + step, n)},
                            device_id_type=mesh_type)
    pl.semaphore_signal(barrier, inc=1, device_id={"chan": other}, device_id_type=mesh_type)

    @pl.when((s == last) & (c == 0))
    def _():
        for step in range(1, n):
            pl.semaphore_signal(barrier, inc=1, device_id_type=mesh_type,
                                device_id={"dp": lax.rem(me + step, n), "chan": other})

    @pl.when(s > 0)
    def _():
        pl.semaphore_signal(barrier, inc=1, device_id={"section": s - 1},
                            device_id_type=mesh_type)

    @pl.when(s < last)
    def _():
        pl.semaphore_signal(barrier, inc=1, device_id={"section": s + 1},
                            device_id_type=mesh_type)

    pairs = (
        ("boxes", boxes_hbm, boxes_ref), ("counts", counts_hbm, counts_ref),
        ("full", out_hbm, out_ref), ("wl", wl_hbm, wl_ref), ("teacher", teacher_hbm, teacher_ref),
        ("part", second_hbm, second_ref), ("full", bi_hbm, bi_ref), ("full", top_hbm, top_ref),
        ("wg", wg_hbm, wg_ref), ("we", we_hbm.at[:, :half], we_ref.at[0]),
        ("we", we_hbm.at[:, half:], we_ref.at[1]), ("part", first_hbm, first_ref),
        ("wr", wr_hbm, wr_ref),
    )
    whole = {
        "boxes": boxes_ref, "counts": counts_ref, "full": full_ref, "part": part_ref, "wl": wl_ref,
        "teacher": teacher_ref, "wg": wg_ref, "we": we_ref, "wr": wr_ref,
    }
    load_at = {name: load_sem.at[i] for i, name in enumerate(whole)}
    for name, a, b in pairs:
        pltpu.make_async_copy(a, b, load_at[name]).start()

    def loaded(*names):
        for name in names:
            pltpu.make_async_copy(whole[name], whole[name], load_at[name]).wait()

    loaded("boxes", "counts")
    row = lax.broadcasted_iota(jnp.int32, (cells, 128), 0)
    row_h, row_w = row // side, row % side
    masks = []
    for crop in range(crops):
        inside = jnp.zeros((cells, 128), f32)
        for r in range(slots):
            hit = ((row_h >= boxes_ref[crop, 0, r]) & (row_h < boxes_ref[crop, 1, r])
                   & (row_w >= boxes_ref[crop, 2, r]) & (row_w < boxes_ref[crop, 3, r])
                   & (counts_ref[0, crop] > r))
            inside = jnp.where(hit, 1.0, inside)
        masks.append(inside)
    mask = jnp.concatenate(masks, axis=0)
    cnt[me] = jnp.broadcast_to(jnp.sum(mask, axis=0, keepdims=True), (8, 128))

    pl.semaphore_wait(barrier, n + jnp.where(s > 0, 1, 0) + jnp.where(s < last, 1, 0)
                      + jnp.where((s == last) & (c == 1), n - 1, 0))

    cnt_copies = [Spread(0, lambda to: cnt.at[me], cnt.at[me], cnt.at[peers], at, {"chan": core})
                  for core, at in ((0, 0), (1, 4))]

    @pl.when((s == last) & (c == 1))
    def _():
        for copies in cnt_copies:
            copies.start()

    loaded("full", "part", "wr")
    wr_copy = remote(wr_ref.at[pl.ds(pl.multiple_of(other * half, half), half)], wr_peer,
                     core_send.at[0], core_recv.at[0], {"chan": other})
    wr_copy.start()
    sec_all[me] = jnp.maximum(second_ref[...], 0)
    for j in range(n):
        bi_send[j] = bi_ref[:, j * share : (j + 1) * share]
    bi_all[me, mine] = bi_send[me, mine]

    sec_moves = [[line(step, lambda j, q=q: sec_all.at[j, pl.ds(q * hrows, hrows)],
                       sec_send.at[step, q], sec_recv.at[step, q])
                  for q in range(2)] for step in range(n - 1)]
    bi_copies = Spread(1, lambda to: bi_send.at[to, mine], bi_all.at[me, mine],
                       bi_all.at[peers, mine])
    bi_share = share_copy(0, bi_all)

    def sec_forward(step):
        for q in range(2):
            line_forward(sec_moves[step][q], sec_moves[step + 1][q])

    def bi_forward():
        bi_copies.wait_recv()
        bi_share.start()

    pair = gw * gw
    iota = lambda shape, dim: lax.broadcasted_iota(jnp.int32, shape, dim)
    same = iota((blk, blk), 0) // gw == iota((blk, blk), 1) // gw

    def build_taps():
        same_out = iota((width, pair), 0) % gw == iota((width, pair), 1) % gw
        spread = (iota((pair, blk), 0) // gw == iota((pair, blk), 1) % gw).astype(f32).astype(bf16)
        inside = iota((width, blk), 0) // gw % (blk // gw) == iota((width, blk), 1) // gw
        by_group = wg_ref[...].astype(f32).T
        for t in range(9):
            values = by_group[:, t * pair : (t + 1) * pair]
            values = jnp.broadcast_to(values[:, None, :], (groups, gw, pair)).reshape(width, pair)
            values = jnp.where(same_out, values, 0.0).astype(bf16)
            taps[t] = jnp.where(inside, dot_nn(values, spread), 0.0).astype(bf16)

    def shifter(count):
        prow = lax.broadcasted_iota(jnp.int32, (count, blk), 0)
        p_w = prow % side
        p_h = (prow // side) % side

        def moved(x, a, b):
            shift = (side * a + b) % count
            if shift:
                x = pltpu.roll(x, shift, 0)
            if a:
                x = jnp.where(p_h >= 1 if a == 1 else p_h < side - 1, x, 0.0)
            if b:
                x = jnp.where(p_w >= 1 if b == 1 else p_w < side - 1, x, 0.0)
            return x

        return moved

    def prepare_first():
        moved = shifter(rows)
        for b in range(blocks):
            first = jnp.maximum(first_ref[:, b * blk : (b + 1) * blk], 0).astype(f32)
            for t, (da, db) in enumerate(tap_offsets):
                ft[t, b] = moved(first, -da, -db).T.astype(bf16)

    hop_copies = [
        remote(ng.at[c, q], inc.at[c, q],
               hop_send.at[q], hop_recv.at[q], {"section": lax.max(s - 1, 0)})
        for q in range(2)
    ]
    fwd_copies = [
        remote(inc.at[c, q], inc.at[c, q],
               fwd_send.at[q], fwd_recv.at[q], {"chan": other})
        for q in range(2)
    ]

    @pl.when(s == last)
    def _():
        loaded("wl", "teacher", "wg", "we")
        feature = jnp.maximum(out_ref[...], 0)
        lateral = dot_nn(feature, wl_ref[...])
        error = (mask[:, 0:1] * (lateral - teacher_ref[...].astype(f32))).astype(bf16)
        imitation = dot_nt(error, wl_ref[...])
        build_taps()
        cnt_copies[0].wait_recv()
        bi_copies.start()
        covered = cnt[0]
        for j in range(1, n):
            covered = covered + cnt[j]
        scale = (imitation_weight * pixels) / covered[0:1, 0:1]
        start = (top_ref[...].astype(f32) + imitation * scale).astype(bf16)
        start = jnp.where(out_ref[...] > 0, start, jnp.zeros_like(start))
        for p in range(4):
            pas[p // 2, p % 2] = start[:, p * quarter : (p + 1) * quarter]

    @pl.when(s < last)
    def _():
        if n > 1:
            for q in range(2):
                line_start(sec_moves[0][q])
        loaded("wl", "teacher", "wg", "we")
        build_taps()
        prepare_first()
        if n > 2:
            sec_forward(0)
        bi_copies.start()
        for step in range(1, n - 2):
            sec_forward(step)

    ps_copies = Spread(2, lambda to: ps_send.at[to, mine], ps_all.at[me, mine],
                       ps_all.at[peers, mine])
    ps_share = share_copy(1, ps_all)
    d_moves = [[line(step, lambda j, q=q: d_all.at[q, j], d_send.at[step, q], d_recv.at[step, q])
                for q in range(2)] for step in range(n - 1)]
    dfx_copies = [remote(d_all.at[q, me], dfx.at[q], core_send.at[1 + q], core_recv.at[1 + q],
                         {"chan": other}) for q in range(2)]
    ng_copy = remote(ng.at[c], ng.at[c], core_send.at[3], core_recv.at[3], {"chan": other})

    def gate_quarter(h, q):
        at = pl.ds(pl.multiple_of(h * half + q * quarter, quarter), quarter)
        value = inc[h, q]
        pas[h, q] = jnp.where(out_ref[:, at] > 0, value, jnp.zeros_like(value))

    second_full = None
    for h, copies in ((c, hop_copies), (other, fwd_copies)):
        for q in range(2):
            @pl.when(s < last)
            def _():
                copies[q].wait_recv()
                if copies is hop_copies:
                    fwd_copies[q].start()
                gate_quarter(h, q)

            if copies is fwd_copies and q == 1:
                for j in range(n):
                    at = (j * share) // quarter
                    lo = j * share - at * quarter
                    ps_send[j] = pas[at // 2, at % 2, :, lo : lo + share]
                ps_all[me, mine] = ps_send[me, mine]
                ps_copies.start()

            term = dot_nt(pas[h, q], we_ref[h, :, q * quarter : (q + 1) * quarter])
            second_full = term if second_full is None else second_full + term

    moved = shifter(rows)
    for q in range(2):
        for b in range(q * blocks // 2, (q + 1) * blocks // 2):
            lo, hi = b * blk, (b + 1) * blk
            lhs = jnp.where(second_ref[:, lo:hi] > 0, second_full[:, lo:hi], 0.0).astype(bf16)
            ds[:, lo:hi] = lhs
            total = None
            for db in (-1, 0, 1):
                column = None
                for da in (-1, 0, 1):
                    t = 3 * (da + 1) + db + 1
                    y = moved(dot_nn(lhs, taps[t, lo:hi, :]), da, 0)
                    column = y if column is None else column + y
                column = moved(column, 0, db)
                total = column if total is None else total + column
            d_all[q, me, :, lo - q * cols : hi - q * cols] = jnp.where(
                first_ref[:, lo:hi] > 0, total, 0.0).astype(bf16)
        dfx_copies[q].start()
        if n > 1:
            @pl.when(s < last)
            def _():
                line_start(d_moves[0][q])

    own_rows = pl.ds(pl.multiple_of(c * half, half), half)
    grad = dot_nt(d_all[0, me], wr_ref[own_rows, :cols]) + dot_nt(d_all[1, me], wr_ref[own_rows, cols:])
    wr_copy.wait_recv()
    for q in range(2):
        dfx_copies[q].wait_recv()
    for q in range(2):
        at = slice(q * quarter, (q + 1) * quarter)
        piece = grad[:, at] + pas[c, q].astype(f32)
        for p in range(2):
            piece = piece + dot_nt(dfx[p], wr_peer[at, p * cols : (p + 1) * cols])
        ng[c, q] = piece.astype(bf16)

        @pl.when(s > 0)
        def _():
            hop_copies[q].start()

    ng_copy.start()

    if n > 1:
        @pl.when(s == last)
        def _():
            for q in range(2):
                line_start(sec_moves[0][q])

    @pl.when(s == last)
    def _():
        prepare_first()

    gf[...] = jnp.zeros_like(gf)
    for b in range(blocks):
        rhs = ds[:, b * blk : (b + 1) * blk]
        for t in range(9):
            dense = jnp.where(same, dot_nn(ft[t, b], rhs), 0.0)
            folded = jnp.sum(dense.reshape(blk // gw, gw, blk), axis=0)
            for j in range(n):
                gf[j, t * k : (t + 1) * k, b * blk : (b + 1) * blk] = folded[j * k : (j + 1) * k]
    g_send[...] = gf[...].astype(bf16)
    g_copies = Spread(3, lambda to: g_send.at[to], g_recv.at[me], g_recv.at[peers])

    if n > 1:
        @pl.when(s == last)
        def _():
            for q in range(2):
                line_start(d_moves[0][q])

    @pl.when(s < last)
    def _():
        bi_forward()

    ps_copies.wait_recv()
    ps_share.start()

    def d_forward(step):
        for q in range(2):
            line_forward(d_moves[step][q], d_moves[step + 1][q])

    for step in range(n - 2):
        @pl.when(s == last)
        def _():
            sec_forward(step)
            if step == 0:
                bi_forward()

        d_forward(step)
        if step == 0:
            ng_copy.wait_recv()
            for p in range(4):
                grads_ref[:, p * quarter : (p + 1) * quarter] = ng[p // 2, p % 2]
    g_copies.start()
    for q in range(2):
        line_finish([step_moves[q] for step_moves in sec_moves])
    ps_share.wait_recv()
    expand = dot_tn(sec_all[...].reshape(n * rows, width), ps_all[...].reshape(n * rows, share))
    expand_ref[...] = expand * norm
    bi_share.wait_recv()

    def reduce_columns(q):
        line_finish([step_moves[q] for step_moves in d_moves])
        reduced = dot_tn(bi_all[...].reshape(n * rows, share), d_all[q].reshape(n * rows, cols))
        reduce_ref[:, q * cols : (q + 1) * cols] = reduced * norm

    reduce_columns(0)
    reduce_columns(1)
    g_copies.wait_recv()
    g_recv[me] = jnp.zeros(g_recv.shape[1:], bf16)
    total = gf[me]
    for j in range(n):
        total = total + g_recv[j].astype(f32)
    total = (total * norm)[: 9 * k]
    wide = jnp.broadcast_to(total[:, None, :], (9 * k, gw, width)).reshape(9 * k * gw, width)
    out_of = iota((9 * k * gw, width), 0) % gw == iota((9 * k * gw, width), 1) % gw
    wide = jnp.where(out_of, wide, 0.0)
    high = wide.astype(bf16)
    low = (wide - high.astype(f32)).astype(bf16)
    group_of = (iota((width, groups), 0) // gw == iota((width, groups), 1)).astype(f32).astype(bf16)
    group_ref[...] = dot_nn(high, group_of) + dot_nn(low, group_of)

    for move in [move for step_moves in sec_moves + d_moves for move in step_moves]:
        for copy, sends, _ in move:
            pl.when(sends)(copy.wait_send)
    for copy in [bi_share, ps_share, bi_copies, ps_copies, g_copies, wr_copy, ng_copy] + dfx_copies:
        copy.wait_send()

    @pl.when((s == last) & (c == 1))
    def _():
        for copies in cnt_copies:
            copies.wait_send()

    @pl.when(s > 0)
    def _():
        for copy in hop_copies:
            copy.wait_send()

    @pl.when(s < last)
    def _():
        for copy in fwd_copies:
            copy.wait_send()


def store_kernel(*refs):
    count = (len(refs) - 1) // 2
    copies = [pltpu.make_async_copy(refs[i], refs[count + i], refs[-1].at[i]) for i in range(count)]
    for copy in copies:
        copy.start()
    for copy in copies:
        copy.wait()


def on_device(
    block_inputs, out_pre, first_pre, second_pre, w_reduce, w_group, w_expand, w_lateral,
    teacher, top_grad, boxes, region_counts,
):
    n = lax.axis_size("dp")
    sections = lax.axis_size("section")
    crops, side, _, channels = top_grad.shape
    rows = crops * side * side
    width = first_pre.shape[4]
    lateral_width = w_lateral.shape[1]
    groups, gw = w_group.shape[2], w_group.shape[3]
    slots = boxes.shape[1]
    pixels = rows * n
    share = channels // n
    k = gw // n
    grows = -(-9 * k // 8) * 8
    half = channels // 2
    blk = min(256, width)
    hbm = pl.BlockSpec(memory_space=pltpu.HBM)
    vmem = pl.BlockSpec(memory_space=pltpu.VMEM)
    dma = pltpu.SemaphoreType.DMA
    peers = max(n - 1, 1)
    shapes = (
        ((rows, channels), bf16), ((share, width), f32),
        ((9 * k * gw, groups), f32), ((width, share), f32),
    )
    results = pl.pallas_call(
        functools.partial(kernel, (n, sections, crops, side, slots, pixels)),
        out_shape=tuple(pltpu.VMEM(shape, kind) for shape, kind in shapes),
        in_specs=[hbm] * 12,
        out_specs=(vmem,) * 4,
        scratch_shapes=[
            pltpu.SMEM((crops, 4, slots), jnp.int32),
            pltpu.SMEM((1, crops), jnp.int32),
            pltpu.VMEM((3, rows, channels), bf16),
            pltpu.VMEM((2, rows, width), bf16),
            pltpu.VMEM((channels, width), bf16),
            pltpu.VMEM((9 * gw * gw, groups), bf16),
            pltpu.VMEM((2, width, half), bf16),
            pltpu.VMEM((channels, lateral_width), bf16),
            pltpu.VMEM((rows, lateral_width), bf16),
            dma((9,)),
            pltpu.VMEM((2, 2, rows, half // 2), bf16),
            pltpu.VMEM((2, 2, rows, half // 2), bf16),
            pltpu.VMEM((half, width), bf16),
            pltpu.VMEM((2, rows, width // 2), bf16),
            pltpu.VMEM((2, 2, rows, half // 2), bf16),
            pltpu.VMEM((rows, width), bf16),
            pltpu.VMEM((2, n, rows, width // 2), bf16),
            pltpu.VMEM((n, rows, width), bf16),
            pltpu.VMEM((n, rows, share), bf16),
            pltpu.VMEM((n, rows, share), bf16),
            pltpu.VMEM((n, rows, share), bf16),
            pltpu.VMEM((n, rows, share), bf16),
            pltpu.VMEM((n, grows, width), f32),
            pltpu.VMEM((n, grows, width), bf16),
            pltpu.VMEM((n, grows, width), bf16),
            pltpu.VMEM((n, 8, 128), f32),
            pltpu.VMEM((9, width, blk), bf16),
            pltpu.VMEM((9, width // blk, blk, rows), bf16),
            dma((5,)), dma((4,)), dma((4,)), dma((4,)),
            dma((2,)), dma((2,)), dma((2,)), dma((2,)),
            dma((peers, 2, 2)), dma((peers, 2, 2)), dma((peers, 2, 2)), dma((peers, 2, 2)),
            dma((2,)), dma((2,)),
        ],
        compiler_params=pltpu.CompilerParams(
            collective_id=0, has_side_effects=True, vmem_limit_bytes=44 << 20,
        ),
    )(*(pltpu.with_memory_space_constraint(x, pltpu.HBM) for x in (
        boxes.transpose(0, 2, 1), region_counts.reshape(1, crops),
        block_inputs.reshape(rows, channels), out_pre.reshape(rows, channels),
        first_pre.reshape(rows, width), second_pre.reshape(rows, width),
        w_reduce[0], w_group[0].transpose(0, 2, 3, 1).reshape(9 * gw * gw, groups), w_expand[0], w_lateral,
        teacher.reshape(rows, lateral_width), top_grad.reshape(rows, channels),
    )))
    grads, reduced, group, expand = pl.pallas_call(
        store_kernel,
        out_shape=tuple(jax.ShapeDtypeStruct(shape, kind) for shape, kind in shapes),
        in_specs=[vmem] * 4,
        out_specs=(hbm,) * 4,
        scratch_shapes=[dma((4,))],
    )(*(pltpu.with_memory_space_constraint(x, pltpu.VMEM) for x in results))
    group = group.reshape(9, k, gw, groups).transpose(0, 3, 1, 2)
    return (
        grads.reshape(1, crops, side, side, channels), reduced[None], group[None], expand[None],
    )


def solution(mesh):
    return jax.shard_map(
        on_device,
        mesh=mesh,
        in_specs=(
            P("section", ("parts", "dp"), None, None, None),
            P("section", ("parts", "dp"), None, None, None),
            P("section", ("parts", "dp"), None, None, "chan"),
            P("section", ("parts", "dp"), None, None, "chan"),
            P("section", None, "chan"),
            P("section", None, "chan", None, None),
            P("section", "chan", None),
            P(),
            P(("parts", "dp"), None, None, None),
            P(("parts", "dp"), None, None, None),
            P(("parts", "dp"), None, None),
            P(("parts", "dp")),
        ),
        out_specs=(
            P("section", ("parts", "dp"), None, None, None),
            P(("parts", "section"), "dp", "chan"),
            P(("parts", "section"), None, "chan", "dp", None),
            P(("parts", "section"), "chan", "dp"),
        ),
        check_vma=False,
    )
```

```python
import functools
import math

import jax
import jax.numpy as jnp
from jax import lax
from jax.experimental import pallas as pl
from jax.experimental.pallas import tpu as pltpu
from jax.sharding import PartitionSpec as P

imitation_weight = 0.5
tap_offsets = [(tap // 3 - 1, tap % 3 - 1) for tap in range(9)]
f32 = jnp.float32
bf16 = jnp.bfloat16


def dot_nn(a, b):
    return lax.dot_general(a, b, (((1,), (0,)), ((), ())), preferred_element_type=f32)


def dot_nt(a, b):
    return lax.dot_general(a, b, (((1,), (1,)), ((), ())), preferred_element_type=f32)


def dot_tn(a, b):
    return lax.dot_general(a, b, (((0,), (0,)), ((), ())), preferred_element_type=f32)


def kernel(
    dims,
    boxes_hbm, counts_hbm, bi_hbm, out_hbm, first_hbm, second_hbm, wr_hbm, wg_hbm, we_hbm,
    wl_hbm, teacher_hbm, top_hbm,
    grads_ref, reduce_ref, group_ref, expand_ref,
    boxes_ref, counts_ref,
    full_ref, part_ref, wr_ref, wg_ref, we_ref, wl_ref, teacher_ref, load_sem,
    inc, pas, wr_peer, dfx, ng, ds, d_all, sec_all, bi_send, bi_all, ps_send, ps_all,
    gf, g_send, g_recv, cnt, taps, ft,
    dp_send, dp_recv, core_send, core_recv, hop_send, hop_recv, fwd_send, fwd_recv,
    sec_send, sec_recv, d_send, d_recv, share_send, share_recv,
):
    n, sections, crops, side, slots, pixels = dims
    out_ref, bi_ref, top_ref = (full_ref.at[i] for i in range(3))
    first_ref, second_ref = part_ref.at[0], part_ref.at[1]
    rows, channels = bi_ref.shape
    half = channels // 2
    quarter = half // 2
    width = first_ref.shape[1]
    cols = width // 2
    groups = wg_ref.shape[1]
    gw = width // groups
    blk = taps.shape[2]
    blocks = width // blk
    cells = side * side
    share = channels // n
    k = gw // n
    hrows = rows // 2
    me = lax.axis_index("dp")
    s = lax.axis_index("section")
    c = lax.axis_index("chan")
    other = 1 - c
    last = sections - 1
    norm = 1.0 / math.sqrt(pixels)

    def remote(src, dst, send, recv, where):
        return pltpu.make_async_remote_copy(
            src_ref=src, dst_ref=dst, send_sem=send, recv_sem=recv,
            device_id=where, device_id_type=pl.DeviceIdType.MESH,
        )

    class Spread:
        def __init__(self, what, src_of, dst, moved, at=None, where={}):
            at = what if at is None else at
            self.copies = [
                remote(src_of(to), dst, dp_send.at[at], dp_recv.at[what], {"dp": to, **where})
                for to in (lax.rem(me + step, n) for step in range(1, n))
            ]
            self.sent = pltpu.make_async_copy(moved, moved, dp_send.at[at])
            self.received = pltpu.make_async_copy(moved, moved, dp_recv.at[what])

        def start(self):
            for copy in self.copies:
                copy.start()

        def wait_recv(self):
            self.received.wait()

        def wait_send(self):
            self.sent.wait()

    mine = pl.ds(pl.multiple_of(c * hrows, hrows), hrows)
    peers = pl.ds(0, n - 1)

    def share_copy(which, buf):
        return remote(buf.at[:, mine], buf.at[:, mine], share_send.at[which],
                      share_recv.at[which], {"chan": other})

    def line(step, block, send, recv):
        ahead = block(lax.max(me - step, 0))
        behind = block(lax.min(me + step, n - 1))
        right = remote(ahead, ahead, send.at[0], recv.at[0], {"dp": lax.min(me + 1, n - 1)})
        left = remote(behind, behind, send.at[1], recv.at[1], {"dp": lax.max(me - 1, 0)})
        return (
            (right, (me - step >= 0) & (me + 1 < n), me - 1 - step >= 0),
            (left, (me + step < n) & (me >= 1), me + 1 + step < n),
        )

    def line_start(moves):
        for copy, sends, _ in moves:
            pl.when(sends)(copy.start)

    def line_forward(moves, following):
        for (copy, _, receives), (onward, sends, _) in zip(moves, following):
            @pl.when(receives & sends)
            def _():
                copy.wait_recv()
                onward.start()

    def line_settle(moves, following):
        for (copy, _, receives), (_, sends, _) in zip(moves, following):
            pl.when(receives & jnp.logical_not(sends))(copy.wait_recv)

    def line_finish(moves, settled):
        for step in range(n - 1):
            if step == n - 2:
                for copy, _, receives in moves[step]:
                    pl.when(receives)(copy.wait_recv)
            elif step != settled:
                line_settle(moves[step], moves[step + 1])

    barrier = pltpu.get_barrier_semaphore()
    mesh_type = pl.DeviceIdType.MESH
    for step in range(1, n):
        pl.semaphore_signal(barrier, inc=1, device_id={"dp": lax.rem(me + step, n)},
                            device_id_type=mesh_type)
    pl.semaphore_signal(barrier, inc=1, device_id={"chan": other}, device_id_type=mesh_type)

    @pl.when((s == last) & (c == 0))
    def _():
        for step in range(1, n):
            pl.semaphore_signal(barrier, inc=1, device_id_type=mesh_type,
                                device_id={"dp": lax.rem(me + step, n), "chan": other})

    @pl.when(s > 0)
    def _():
        pl.semaphore_signal(barrier, inc=1, device_id={"section": s - 1},
                            device_id_type=mesh_type)

    @pl.when(s < last)
    def _():
        pl.semaphore_signal(barrier, inc=1, device_id={"section": s + 1},
                            device_id_type=mesh_type)

    pairs = (
        ("boxes", boxes_hbm, boxes_ref), ("counts", counts_hbm, counts_ref),
        ("second", second_hbm, second_ref), ("pair", out_hbm, out_ref), ("wl", wl_hbm, wl_ref),
        ("teacher", teacher_hbm, teacher_ref), ("pair", bi_hbm, bi_ref),
        ("wg", wg_hbm, wg_ref), ("top", top_hbm, top_ref), ("we", we_hbm.at[:, :half], we_ref.at[0]),
        ("we", we_hbm.at[:, half:], we_ref.at[1]), ("first", first_hbm, first_ref),
        ("wr", wr_hbm, wr_ref),
    )
    whole = {
        "boxes": boxes_ref, "counts": counts_ref, "pair": full_ref.at[0:2], "top": top_ref,
        "first": first_ref, "second": second_ref, "wl": wl_ref, "teacher": teacher_ref,
        "wg": wg_ref, "we": we_ref, "wr": wr_ref,
    }
    load_at = {name: load_sem.at[i] for i, name in enumerate(whole)}

    def load_start(some):
        for name, a, b in some:
            pltpu.make_async_copy(a, b, load_at[name]).start()

    def loaded(*names):
        for name in names:
            pltpu.make_async_copy(whole[name], whole[name], load_at[name]).wait()

    counting = (s == last) & (c == 1)
    load_start(pairs[:7])

    @pl.when(jnp.logical_not(counting))
    def _():
        load_start(pairs[7:])

    loaded("boxes", "counts")
    row = lax.broadcasted_iota(jnp.int32, (cells, 128), 0)
    row_h, row_w = row // side, row % side
    masks = []
    for crop in range(crops):
        inside = jnp.zeros((cells, 128), f32)
        for r in range(slots):
            hit = ((row_h >= boxes_ref[crop, 0, r]) & (row_h < boxes_ref[crop, 1, r])
                   & (row_w >= boxes_ref[crop, 2, r]) & (row_w < boxes_ref[crop, 3, r])
                   & (counts_ref[0, crop] > r))
            inside = jnp.where(hit, 1.0, inside)
        masks.append(inside)
    mask = jnp.concatenate(masks, axis=0)
    cnt[me] = jnp.broadcast_to(jnp.sum(mask, axis=0, keepdims=True), (8, 128))

    pl.semaphore_wait(barrier, n + jnp.where(s > 0, 1, 0) + jnp.where(s < last, 1, 0)
                      + jnp.where(counting, n - 1, 0))

    cnt_copies = [Spread(0, lambda to: cnt.at[me], cnt.at[me], cnt.at[peers], at, {"chan": core})
                  for core, at in ((0, 0), (1, 4))]

    @pl.when(counting)
    def _():
        for copies in cnt_copies:
            copies.start()
        load_start(pairs[7:])

    wr_copy = remote(wr_ref.at[pl.ds(pl.multiple_of(other * half, half), half)], wr_peer,
                     core_send.at[0], core_recv.at[0], {"chan": other})
    loaded("second")
    sec_all[me] = jnp.maximum(second_ref[...], 0)
    sec_moves = [[line(step, lambda j, q=q: sec_all.at[j, pl.ds(q * hrows, hrows)],
                       sec_send.at[step, q], sec_recv.at[step, q])
                  for q in range(2)] for step in range(n - 1)]
    if n > 1:
        for q in range(2):
            line_start(sec_moves[0][q])
    loaded("pair")
    for j in range(n):
        bi_send[j] = bi_ref[:, j * share : (j + 1) * share]
    bi_all[me, mine] = bi_send[me, mine]

    bi_copies = Spread(1, lambda to: bi_send.at[to, mine], bi_all.at[me, mine],
                       bi_all.at[peers, mine])
    bi_share = share_copy(0, bi_all)

    def sec_forward(step):
        for q in range(2):
            line_forward(sec_moves[step][q], sec_moves[step + 1][q])

    def bi_forward():
        bi_copies.wait_recv()
        bi_share.start()

    pair = gw * gw
    iota = lambda shape, dim: lax.broadcasted_iota(jnp.int32, shape, dim)
    same = iota((blk, blk), 0) // gw == iota((blk, blk), 1) // gw

    def build_taps():
        same_out = iota((width, pair), 0) % gw == iota((width, pair), 1) % gw
        spread = (iota((pair, blk), 0) // gw == iota((pair, blk), 1) % gw).astype(f32).astype(bf16)
        inside = iota((width, blk), 0) // gw % (blk // gw) == iota((width, blk), 1) // gw
        by_group = wg_ref[...].astype(f32).T
        for t in range(9):
            values = by_group[:, t * pair : (t + 1) * pair]
            values = jnp.broadcast_to(values[:, None, :], (groups, gw, pair)).reshape(width, pair)
            values = jnp.where(same_out, values, 0.0).astype(bf16)
            taps[t] = jnp.where(inside, dot_nn(values, spread), 0.0).astype(bf16)

    def shifter(count):
        prow = lax.broadcasted_iota(jnp.int32, (count, blk), 0)
        p_w = prow % side
        p_h = (prow // side) % side

        def moved(x, a, b):
            shift = (side * a + b) % count
            if shift:
                x = pltpu.roll(x, shift, 0)
            if a:
                x = jnp.where(p_h >= 1 if a == 1 else p_h < side - 1, x, 0.0)
            if b:
                x = jnp.where(p_w >= 1 if b == 1 else p_w < side - 1, x, 0.0)
            return x

        return moved

    def prepare_first():
        moved = shifter(rows)
        for b in range(blocks):
            first = jnp.maximum(first_ref[:, b * blk : (b + 1) * blk], 0).astype(f32)
            for t, (da, db) in enumerate(tap_offsets):
                ft[t, b] = moved(first, -da, -db).T.astype(bf16)

    hop_copies = [
        remote(ng.at[c, q], inc.at[c, q],
               hop_send.at[q], hop_recv.at[q], {"section": lax.max(s - 1, 0)})
        for q in range(2)
    ]
    fwd_copies = [
        remote(inc.at[c, q], inc.at[c, q],
               fwd_send.at[q], fwd_recv.at[q], {"chan": other})
        for q in range(2)
    ]

    @pl.when(s == last)
    def _():
        loaded("wl", "teacher")
        feature = jnp.maximum(out_ref[...], 0)
        lateral = dot_nn(feature, wl_ref[...])
        error = (mask[:, 0:1] * (lateral - teacher_ref[...].astype(f32))).astype(bf16)
        imitation = dot_nt(error, wl_ref[...])
        loaded("wg")
        build_taps()
        loaded("top", "first", "we", "wr")
        wr_copy.start()
        cnt_copies[0].wait_recv()
        bi_copies.start()
        covered = cnt[0]
        for j in range(1, n):
            covered = covered + cnt[j]
        scale = (imitation_weight * pixels) / covered[0:1, 0:1]
        start = (top_ref[...].astype(f32) + imitation * scale).astype(bf16)
        start = jnp.where(out_ref[...] > 0, start, jnp.zeros_like(start))
        for p in range(4):
            pas[p // 2, p % 2] = start[:, p * quarter : (p + 1) * quarter]

    @pl.when(s < last)
    def _():
        loaded("wl", "teacher", "wg", "top", "first", "we", "wr")
        wr_copy.start()
        build_taps()
        prepare_first()
        for step in range(n - 2):
            sec_forward(step)
        if n > 2:
            for q in range(2):
                line_settle(sec_moves[n - 3][q], sec_moves[n - 2][q])
        bi_copies.start()

    ps_copies = Spread(2, lambda to: ps_send.at[to, mine], ps_all.at[me, mine],
                       ps_all.at[peers, mine])
    ps_share = share_copy(1, ps_all)
    d_moves = [[line(step, lambda j, q=q: d_all.at[q, j], d_send.at[step, q], d_recv.at[step, q])
                for q in range(2)] for step in range(n - 1)]
    dfx_copies = [remote(d_all.at[q, me], dfx.at[q], core_send.at[1 + q], core_recv.at[1 + q],
                         {"chan": other}) for q in range(2)]
    ng_copy = remote(ng.at[c], ng.at[c], core_send.at[3], core_recv.at[3], {"chan": other})

    def gate_quarter(h, q):
        at = pl.ds(pl.multiple_of(h * half + q * quarter, quarter), quarter)
        value = inc[h, q]
        pas[h, q] = jnp.where(out_ref[:, at] > 0, value, jnp.zeros_like(value))

    second_full = None
    for h, copies in ((c, hop_copies), (other, fwd_copies)):
        for q in range(2):
            @pl.when(s < last)
            def _():
                copies[q].wait_recv()
                if copies is hop_copies:
                    fwd_copies[q].start()
                gate_quarter(h, q)

            if copies is fwd_copies and q == 1:
                for j in range(n):
                    at = (j * share) // quarter
                    lo = j * share - at * quarter
                    ps_send[j] = pas[at // 2, at % 2, :, lo : lo + share]
                ps_all[me, mine] = ps_send[me, mine]
                ps_copies.start()

            term = dot_nt(pas[h, q], we_ref[h, :, q * quarter : (q + 1) * quarter])
            second_full = term if second_full is None else second_full + term

    moved = shifter(rows)
    for q in range(2):
        for b in range(q * blocks // 2, (q + 1) * blocks // 2):
            lo, hi = b * blk, (b + 1) * blk
            lhs = jnp.where(second_ref[:, lo:hi] > 0, second_full[:, lo:hi], 0.0).astype(bf16)
            ds[:, lo:hi] = lhs
            total = None
            for db in (-1, 0, 1):
                column = None
                for da in (-1, 0, 1):
                    t = 3 * (da + 1) + db + 1
                    y = moved(dot_nn(lhs, taps[t, lo:hi, :]), da, 0)
                    column = y if column is None else column + y
                column = moved(column, 0, db)
                total = column if total is None else total + column
            d_all[q, me, :, lo - q * cols : hi - q * cols] = jnp.where(
                first_ref[:, lo:hi] > 0, total, 0.0).astype(bf16)
        dfx_copies[q].start()
        if n > 1:
            @pl.when(s < last)
            def _():
                line_start(d_moves[0][q])

    own_rows = pl.ds(pl.multiple_of(c * half, half), half)
    grad = dot_nt(d_all[0, me], wr_ref[own_rows, :cols]) + dot_nt(d_all[1, me], wr_ref[own_rows, cols:])
    wr_copy.wait_recv()
    for q in range(2):
        dfx_copies[q].wait_recv()
    for q in range(2):
        at = slice(q * quarter, (q + 1) * quarter)
        piece = grad[:, at] + pas[c, q].astype(f32)
        for p in range(2):
            piece = piece + dot_nt(dfx[p], wr_peer[at, p * cols : (p + 1) * cols])
        ng[c, q] = piece.astype(bf16)

        @pl.when(s > 0)
        def _():
            hop_copies[q].start()

    ng_copy.start()

    @pl.when(s == last)
    def _():
        prepare_first()

    gf[...] = jnp.zeros_like(gf)
    for b in range(blocks):
        rhs = ds[:, b * blk : (b + 1) * blk]
        for t in range(9):
            dense = jnp.where(same, dot_nn(ft[t, b], rhs), 0.0)
            folded = jnp.sum(dense.reshape(blk // gw, gw, blk), axis=0)
            for j in range(n):
                gf[j, t * k : (t + 1) * k, b * blk : (b + 1) * blk] = folded[j * k : (j + 1) * k]
    g_send[...] = gf[...].astype(bf16)
    g_copies = Spread(3, lambda to: g_send.at[to], g_recv.at[me], g_recv.at[peers])

    if n > 1:
        @pl.when(s == last)
        def _():
            for q in range(2):
                line_start(d_moves[0][q])

    @pl.when(s < last)
    def _():
        bi_forward()

    ps_copies.wait_recv()
    ps_share.start()

    def d_forward(step):
        for q in range(2):
            line_forward(d_moves[step][q], d_moves[step + 1][q])

    for step in range(n - 2):
        @pl.when(s == last)
        def _():
            sec_forward(step)
            if step == 0:
                bi_forward()

        d_forward(step)

        @pl.when(s == last)
        def _():
            if step == 0:
                g_copies.start()

        if step == 0:
            ng_copy.wait_recv()
            for p in range(4):
                grads_ref[:, p * quarter : (p + 1) * quarter] = ng[p // 2, p % 2]
    if n > 2:
        for q in range(2):
            line_settle(d_moves[n - 3][q], d_moves[n - 2][q])

    @pl.when(s < last)
    def _():
        g_copies.start()

    for q in range(2):
        @pl.when(s == last)
        def _():
            if n > 2:
                line_settle(sec_moves[n - 3][q], sec_moves[n - 2][q])

        line_finish([step_moves[q] for step_moves in sec_moves], n - 3)
    ps_share.wait_recv()
    expand = dot_tn(sec_all[...].reshape(n * rows, width), ps_all[...].reshape(n * rows, share))
    expand_ref[...] = expand * norm
    bi_share.wait_recv()

    def reduce_columns(q):
        line_finish([step_moves[q] for step_moves in d_moves], n - 3)
        reduced = dot_tn(bi_all[...].reshape(n * rows, share), d_all[q].reshape(n * rows, cols))
        reduce_ref[:, q * cols : (q + 1) * cols] = reduced * norm

    reduce_columns(0)
    reduce_columns(1)
    g_copies.wait_recv()
    g_recv[me] = jnp.zeros(g_recv.shape[1:], bf16)
    total = gf[me]
    for j in range(n):
        total = total + g_recv[j].astype(f32)
    total = (total * norm)[: 9 * k]
    wide = jnp.broadcast_to(total[:, None, :], (9 * k, gw, width)).reshape(9 * k * gw, width)
    out_of = iota((9 * k * gw, width), 0) % gw == iota((9 * k * gw, width), 1) % gw
    wide = jnp.where(out_of, wide, 0.0)
    high = wide.astype(bf16)
    low = (wide - high.astype(f32)).astype(bf16)
    group_of = (iota((width, groups), 0) // gw == iota((width, groups), 1)).astype(f32).astype(bf16)
    group_ref[...] = dot_nn(high, group_of) + dot_nn(low, group_of)

    for move in [move for step_moves in sec_moves + d_moves for move in step_moves]:
        for copy, sends, _ in move:
            pl.when(sends)(copy.wait_send)
    for copy in [bi_share, ps_share, bi_copies, ps_copies, g_copies, wr_copy, ng_copy] + dfx_copies:
        copy.wait_send()

    @pl.when(counting)
    def _():
        for copies in cnt_copies:
            copies.wait_send()

    @pl.when(s > 0)
    def _():
        for copy in hop_copies:
            copy.wait_send()

    @pl.when(s < last)
    def _():
        for copy in fwd_copies:
            copy.wait_send()


def store_kernel(*refs):
    count = (len(refs) - 1) // 2
    copies = [pltpu.make_async_copy(refs[i], refs[count + i], refs[-1].at[i]) for i in range(count)]
    for copy in copies:
        copy.start()
    for copy in copies:
        copy.wait()


def on_device(
    block_inputs, out_pre, first_pre, second_pre, w_reduce, w_group, w_expand, w_lateral,
    teacher, top_grad, boxes, region_counts,
):
    n = lax.axis_size("dp")
    sections = lax.axis_size("section")
    crops, side, _, channels = top_grad.shape
    rows = crops * side * side
    width = first_pre.shape[4]
    lateral_width = w_lateral.shape[1]
    groups, gw = w_group.shape[2], w_group.shape[3]
    slots = boxes.shape[1]
    pixels = rows * n
    share = channels // n
    k = gw // n
    grows = -(-9 * k // 8) * 8
    half = channels // 2
    blk = min(256, width)
    hbm = pl.BlockSpec(memory_space=pltpu.HBM)
    vmem = pl.BlockSpec(memory_space=pltpu.VMEM)
    dma = pltpu.SemaphoreType.DMA
    peers = max(n - 1, 1)
    shapes = (
        ((rows, channels), bf16), ((share, width), f32),
        ((9 * k * gw, groups), f32), ((width, share), f32),
    )
    results = pl.pallas_call(
        functools.partial(kernel, (n, sections, crops, side, slots, pixels)),
        out_shape=tuple(pltpu.VMEM(shape, kind) for shape, kind in shapes),
        in_specs=[hbm] * 12,
        out_specs=(vmem,) * 4,
        scratch_shapes=[
            pltpu.SMEM((crops, 4, slots), jnp.int32),
            pltpu.SMEM((1, crops), jnp.int32),
            pltpu.VMEM((3, rows, channels), bf16),
            pltpu.VMEM((2, rows, width), bf16),
            pltpu.VMEM((channels, width), bf16),
            pltpu.VMEM((9 * gw * gw, groups), bf16),
            pltpu.VMEM((2, width, half), bf16),
            pltpu.VMEM((channels, lateral_width), bf16),
            pltpu.VMEM((rows, lateral_width), bf16),
            dma((11,)),
            pltpu.VMEM((2, 2, rows, half // 2), bf16),
            pltpu.VMEM((2, 2, rows, half // 2), bf16),
            pltpu.VMEM((half, width), bf16),
            pltpu.VMEM((2, rows, width // 2), bf16),
            pltpu.VMEM((2, 2, rows, half // 2), bf16),
            pltpu.VMEM((rows, width), bf16),
            pltpu.VMEM((2, n, rows, width // 2), bf16),
            pltpu.VMEM((n, rows, width), bf16),
            pltpu.VMEM((n, rows, share), bf16),
            pltpu.VMEM((n, rows, share), bf16),
            pltpu.VMEM((n, rows, share), bf16),
            pltpu.VMEM((n, rows, share), bf16),
            pltpu.VMEM((n, grows, width), f32),
            pltpu.VMEM((n, grows, width), bf16),
            pltpu.VMEM((n, grows, width), bf16),
            pltpu.VMEM((n, 8, 128), f32),
            pltpu.VMEM((9, width, blk), bf16),
            pltpu.VMEM((9, width // blk, blk, rows), bf16),
            dma((5,)), dma((4,)), dma((4,)), dma((4,)),
            dma((2,)), dma((2,)), dma((2,)), dma((2,)),
            dma((peers, 2, 2)), dma((peers, 2, 2)), dma((peers, 2, 2)), dma((peers, 2, 2)),
            dma((2,)), dma((2,)),
        ],
        compiler_params=pltpu.CompilerParams(
            collective_id=0, has_side_effects=True, vmem_limit_bytes=44 << 20,
        ),
    )(*(pltpu.with_memory_space_constraint(x, pltpu.HBM) for x in (
        boxes.transpose(0, 2, 1), region_counts.reshape(1, crops),
        block_inputs.reshape(rows, channels), out_pre.reshape(rows, channels),
        first_pre.reshape(rows, width), second_pre.reshape(rows, width),
        w_reduce[0], w_group[0].transpose(0, 2, 3, 1).reshape(9 * gw * gw, groups), w_expand[0], w_lateral,
        teacher.reshape(rows, lateral_width), top_grad.reshape(rows, channels),
    )))
    grads, reduced, group, expand = pl.pallas_call(
        store_kernel,
        out_shape=tuple(jax.ShapeDtypeStruct(shape, kind) for shape, kind in shapes),
        in_specs=[vmem] * 4,
        out_specs=(hbm,) * 4,
        scratch_shapes=[dma((4,))],
    )(*(pltpu.with_memory_space_constraint(x, pltpu.VMEM) for x in results))
    group = group.reshape(9, k, gw, groups).transpose(0, 3, 1, 2)
    return (
        grads.reshape(1, crops, side, side, channels), reduced[None], group[None], expand[None],
    )


def solution(mesh):
    return jax.shard_map(
        on_device,
        mesh=mesh,
        in_specs=(
            P("section", ("parts", "dp"), None, None, None),
            P("section", ("parts", "dp"), None, None, None),
            P("section", ("parts", "dp"), None, None, "chan"),
            P("section", ("parts", "dp"), None, None, "chan"),
            P("section", None, "chan"),
            P("section", None, "chan", None, None),
            P("section", "chan", None),
            P(),
            P(("parts", "dp"), None, None, None),
            P(("parts", "dp"), None, None, None),
            P(("parts", "dp"), None, None),
            P(("parts", "dp")),
        ),
        out_specs=(
            P("section", ("parts", "dp"), None, None, None),
            P(("parts", "section"), "dp", "chan"),
            P(("parts", "section"), None, "chan", "dp", None),
            P(("parts", "section"), "chan", "dp"),
        ),
        check_vma=False,
    )
```

```python
import functools
import math

import jax
import jax.numpy as jnp
from jax import lax
from jax.experimental import pallas as pl
from jax.experimental.pallas import tpu as pltpu
from jax.sharding import PartitionSpec as P

imitation_weight = 0.5
tap_offsets = [(tap // 3 - 1, tap % 3 - 1) for tap in range(9)]
f32 = jnp.float32
bf16 = jnp.bfloat16


def dot_nn(a, b):
    return lax.dot_general(a, b, (((1,), (0,)), ((), ())), preferred_element_type=f32)


def dot_nt(a, b):
    return lax.dot_general(a, b, (((1,), (1,)), ((), ())), preferred_element_type=f32)


def dot_tn(a, b):
    return lax.dot_general(a, b, (((0,), (0,)), ((), ())), preferred_element_type=f32)


def kernel(
    dims,
    boxes_hbm, counts_hbm, bi_hbm, out_hbm, first_hbm, second_hbm, wr_hbm, wg_hbm, we_hbm,
    wl_hbm, teacher_hbm, top_hbm,
    grads_ref, reduce_ref, group_ref, expand_ref,
    boxes_ref, counts_ref,
    full_ref, part_ref, wr_ref, wg_ref, we_ref, wl_ref, teacher_ref, load_sem,
    inc, pas, wr_peer, dfx, ng, ds, d_all, sec_all, bi_send, bi_all, ps_send, ps_all,
    gf, g_send, g_recv, cnt, taps, ft,
    dp_send, dp_recv, core_send, core_recv, hop_send, hop_recv, fwd_send, fwd_recv,
    sec_send, sec_recv, d_send, d_recv, share_send, share_recv,
):
    n, sections, crops, side, slots, pixels = dims
    out_ref, bi_ref, top_ref = (full_ref.at[i] for i in range(3))
    first_ref, second_ref = part_ref.at[0], part_ref.at[1]
    rows, channels = bi_ref.shape
    half = channels // 2
    width = first_ref.shape[1]
    groups = wg_ref.shape[1]
    gw = width // groups
    blk = taps.shape[2]
    blocks = width // blk
    cells = side * side
    share = channels // n
    k = gw // n
    hrows = rows // 2
    me = lax.axis_index("dp")
    s = lax.axis_index("section")
    c = lax.axis_index("chan")
    other = 1 - c
    last = sections - 1
    norm = 1.0 / math.sqrt(pixels)

    def remote(src, dst, send, recv, where):
        return pltpu.make_async_remote_copy(
            src_ref=src, dst_ref=dst, send_sem=send, recv_sem=recv,
            device_id=where, device_id_type=pl.DeviceIdType.MESH,
        )

    class Spread:
        def __init__(self, what, src_of, dst, moved, at=None, where={}):
            at = what if at is None else at
            self.copies = [
                remote(src_of(to), dst, dp_send.at[at], dp_recv.at[what], {"dp": to, **where})
                for to in (lax.rem(me + step, n) for step in range(1, n))
            ]
            self.sent = pltpu.make_async_copy(moved, moved, dp_send.at[at])
            self.received = pltpu.make_async_copy(moved, moved, dp_recv.at[what])

        def start(self):
            for copy in self.copies:
                copy.start()

        def wait_recv(self):
            self.received.wait()

        def wait_send(self):
            self.sent.wait()

    mine = pl.ds(pl.multiple_of(c * hrows, hrows), hrows)
    peers = pl.ds(0, n - 1)
    crop_rows = [pl.ds(q * hrows, hrows) for q in range(2)]

    def share_copy(which, buf):
        return remote(buf.at[:, mine], buf.at[:, mine], share_send.at[which],
                      share_recv.at[which], {"chan": other})

    def line(step, block, send, recv):
        ahead = block(lax.max(me - step, 0))
        behind = block(lax.min(me + step, n - 1))
        right = remote(ahead, ahead, send.at[0], recv.at[0], {"dp": lax.min(me + 1, n - 1)})
        left = remote(behind, behind, send.at[1], recv.at[1], {"dp": lax.max(me - 1, 0)})
        return (
            (right, (me - step >= 0) & (me + 1 < n), me - 1 - step >= 0),
            (left, (me + step < n) & (me >= 1), me + 1 + step < n),
        )

    def line_start(moves):
        for copy, sends, _ in moves:
            pl.when(sends)(copy.start)

    def line_forward(moves, following):
        for (copy, _, receives), (onward, sends, _) in zip(moves, following):
            @pl.when(receives & sends)
            def _():
                copy.wait_recv()
                onward.start()

    def line_settle(moves, following):
        for (copy, _, receives), (_, sends, _) in zip(moves, following):
            pl.when(receives & jnp.logical_not(sends))(copy.wait_recv)

    def line_finish(moves, settled):
        for step in range(n - 1):
            if step == n - 2:
                for copy, _, receives in moves[step]:
                    pl.when(receives)(copy.wait_recv)
            elif step != settled:
                line_settle(moves[step], moves[step + 1])

    barrier = pltpu.get_barrier_semaphore()
    mesh_type = pl.DeviceIdType.MESH
    for step in range(1, n):
        pl.semaphore_signal(barrier, inc=1, device_id={"dp": lax.rem(me + step, n)},
                            device_id_type=mesh_type)
    pl.semaphore_signal(barrier, inc=1, device_id={"chan": other}, device_id_type=mesh_type)

    @pl.when((s == last) & (c == 0))
    def _():
        for step in range(1, n):
            pl.semaphore_signal(barrier, inc=1, device_id_type=mesh_type,
                                device_id={"dp": lax.rem(me + step, n), "chan": other})

    @pl.when(s > 0)
    def _():
        pl.semaphore_signal(barrier, inc=1, device_id={"section": s - 1},
                            device_id_type=mesh_type)

    @pl.when(s < last)
    def _():
        pl.semaphore_signal(barrier, inc=1, device_id={"section": s + 1},
                            device_id_type=mesh_type)

    pairs = (
        ("boxes", boxes_hbm, boxes_ref), ("counts", counts_hbm, counts_ref),
        ("second", second_hbm, second_ref), ("pair", out_hbm, out_ref), ("wl", wl_hbm, wl_ref),
        ("teacher", teacher_hbm, teacher_ref), ("pair", bi_hbm, bi_ref),
        ("wg", wg_hbm, wg_ref), ("top", top_hbm, top_ref), ("we", we_hbm.at[:, :half], we_ref.at[0]),
        ("we", we_hbm.at[:, half:], we_ref.at[1]), ("first", first_hbm, first_ref),
        ("wr", wr_hbm, wr_ref),
    )
    whole = {
        "boxes": boxes_ref, "counts": counts_ref, "pair": full_ref.at[0:2], "top": top_ref,
        "first": first_ref, "second": second_ref, "wl": wl_ref, "teacher": teacher_ref,
        "wg": wg_ref, "we": we_ref, "wr": wr_ref,
    }
    load_at = {name: load_sem.at[i] for i, name in enumerate(whole)}

    def load_start(some):
        for name, a, b in some:
            pltpu.make_async_copy(a, b, load_at[name]).start()

    def loaded(*names):
        for name in names:
            pltpu.make_async_copy(whole[name], whole[name], load_at[name]).wait()

    counting = (s == last) & (c == 1)
    load_start(pairs[:7])

    @pl.when(jnp.logical_not(counting))
    def _():
        load_start(pairs[7:])

    loaded("boxes", "counts")
    row = lax.broadcasted_iota(jnp.int32, (cells, 128), 0)
    row_h, row_w = row // side, row % side
    masks = []
    for crop in range(crops):
        inside = jnp.zeros((cells, 128), f32)
        for r in range(slots):
            hit = ((row_h >= boxes_ref[crop, 0, r]) & (row_h < boxes_ref[crop, 1, r])
                   & (row_w >= boxes_ref[crop, 2, r]) & (row_w < boxes_ref[crop, 3, r])
                   & (counts_ref[0, crop] > r))
            inside = jnp.where(hit, 1.0, inside)
        masks.append(inside)
    mask = jnp.concatenate(masks, axis=0)
    cnt[me] = jnp.broadcast_to(jnp.sum(mask, axis=0, keepdims=True), (8, 128))

    pl.semaphore_wait(barrier, n + jnp.where(s > 0, 1, 0) + jnp.where(s < last, 1, 0)
                      + jnp.where(counting, n - 1, 0))

    cnt_copies = [Spread(0, lambda to: cnt.at[me], cnt.at[me], cnt.at[peers], at, {"chan": core})
                  for core, at in ((0, 0), (1, 4))]

    @pl.when(counting)
    def _():
        for copies in cnt_copies:
            copies.start()
        load_start(pairs[7:])

    wr_copy = remote(wr_ref.at[pl.ds(pl.multiple_of(other * half, half), half)], wr_peer,
                     core_send.at[0], core_recv.at[0], {"chan": other})
    loaded("second")
    sec_all[me] = jnp.maximum(second_ref[...], 0)
    sec_moves = [[line(step, lambda j, q=q: sec_all.at[j, pl.ds(q * hrows, hrows)],
                       sec_send.at[step, q], sec_recv.at[step, q])
                  for q in range(2)] for step in range(n - 1)]
    if n > 1:
        for q in range(2):
            line_start(sec_moves[0][q])
    loaded("pair")
    for j in range(n):
        bi_send[j] = bi_ref[:, j * share : (j + 1) * share]
    bi_all[me, mine] = bi_send[me, mine]

    bi_copies = Spread(1, lambda to: bi_send.at[to, mine], bi_all.at[me, mine],
                       bi_all.at[peers, mine])
    bi_share = share_copy(0, bi_all)

    def sec_forward(step):
        for q in range(2):
            line_forward(sec_moves[step][q], sec_moves[step + 1][q])

    def bi_forward():
        bi_copies.wait_recv()
        bi_share.start()

    pair = gw * gw
    iota = lambda shape, dim: lax.broadcasted_iota(jnp.int32, shape, dim)
    same = iota((blk, blk), 0) // gw == iota((blk, blk), 1) // gw

    def build_taps():
        same_out = iota((width, pair), 0) % gw == iota((width, pair), 1) % gw
        spread = (iota((pair, blk), 0) // gw == iota((pair, blk), 1) % gw).astype(f32).astype(bf16)
        inside = iota((width, blk), 0) // gw % (blk // gw) == iota((width, blk), 1) // gw
        by_group = wg_ref[...].astype(f32).T
        for t in range(9):
            values = by_group[:, t * pair : (t + 1) * pair]
            values = jnp.broadcast_to(values[:, None, :], (groups, gw, pair)).reshape(width, pair)
            values = jnp.where(same_out, values, 0.0).astype(bf16)
            taps[t] = jnp.where(inside, dot_nn(values, spread), 0.0).astype(bf16)

    def shifter(count):
        prow = lax.broadcasted_iota(jnp.int32, (count, blk), 0)
        p_w = prow % side
        p_h = (prow // side) % side

        def moved(x, a, b):
            shift = (side * a + b) % count
            if shift:
                x = pltpu.roll(x, shift, 0)
            if a:
                x = jnp.where(p_h >= 1 if a == 1 else p_h < side - 1, x, 0.0)
            if b:
                x = jnp.where(p_w >= 1 if b == 1 else p_w < side - 1, x, 0.0)
            return x

        return moved

    def prepare_first():
        moved = shifter(rows)
        for b in range(blocks):
            first = jnp.maximum(first_ref[:, b * blk : (b + 1) * blk], 0).astype(f32)
            for t, (da, db) in enumerate(tap_offsets):
                ft[t, b] = moved(first, -da, -db).T.astype(bf16)

    hop_copies = [
        remote(ng.at[c, crop_rows[q]], inc.at[c, crop_rows[q]],
               hop_send.at[q], hop_recv.at[q], {"section": lax.max(s - 1, 0)})
        for q in range(2)
    ]
    fwd_copies = [
        remote(inc.at[c, crop_rows[q]], inc.at[c, crop_rows[q]],
               fwd_send.at[q], fwd_recv.at[q], {"chan": other})
        for q in range(2)
    ]

    @pl.when(s == last)
    def _():
        loaded("wl", "teacher")
        feature = jnp.maximum(out_ref[...], 0)
        lateral = dot_nn(feature, wl_ref[...])
        error = (mask[:, 0:1] * (lateral - teacher_ref[...].astype(f32))).astype(bf16)
        imitation = dot_nt(error, wl_ref[...])
        loaded("wg")
        build_taps()
        loaded("top", "first", "we", "wr")
        wr_copy.start()
        cnt_copies[0].wait_recv()
        bi_copies.start()
        covered = cnt[0]
        for j in range(1, n):
            covered = covered + cnt[j]
        scale = (imitation_weight * pixels) / covered[0:1, 0:1]
        start = (top_ref[...].astype(f32) + imitation * scale).astype(bf16)
        start = jnp.where(out_ref[...] > 0, start, jnp.zeros_like(start))
        pas[0] = start[:, :half]
        pas[1] = start[:, half:]

    @pl.when(s < last)
    def _():
        loaded("wl", "teacher", "wg", "top", "first", "we", "wr")
        wr_copy.start()
        build_taps()
        prepare_first()
        for step in range(n - 2):
            sec_forward(step)
        if n > 2:
            for q in range(2):
                line_settle(sec_moves[n - 3][q], sec_moves[n - 2][q])
        bi_copies.start()

    ps_copies = Spread(2, lambda to: ps_send.at[to, mine], ps_all.at[me, mine],
                       ps_all.at[peers, mine])
    ps_share = share_copy(1, ps_all)
    d_moves = [[line(step, lambda j, q=q: d_all.at[j, crop_rows[q]], d_send.at[step, q],
                     d_recv.at[step, q]) for q in range(2)] for step in range(n - 1)]
    dfx_copies = [remote(d_all.at[me, crop_rows[q]], dfx.at[crop_rows[q]], core_send.at[1 + q],
                         core_recv.at[1 + q], {"chan": other}) for q in range(2)]
    ng_copy = remote(ng.at[c], ng.at[c], core_send.at[3], core_recv.at[3], {"chan": other})
    at_end = (me == 0) | (me == n - 1)

    def gate_half(h, q):
        at = pl.ds(pl.multiple_of(h * half, half), half)
        value = inc[h, crop_rows[q]]
        gate = out_ref[q * hrows : (q + 1) * hrows, at] > 0
        pas[h, crop_rows[q]] = jnp.where(gate, value, jnp.zeros_like(value))

    def own_arrives(q):
        @pl.when(s < last)
        def _():
            hop_copies[q].wait_recv()
            fwd_copies[q].start()
            gate_half(c, q)

    def other_arrives(q):
        @pl.when(s < last)
        def _():
            fwd_copies[q].wait_recv()
            gate_half(other, q)

    moved = shifter(hrows)
    own_arrives(0)
    for q in range(2):
        top, end = q * hrows, (q + 1) * hrows
        second_full = dot_nt(pas[c, top:end], we_ref[c])
        other_arrives(q)
        for j in range(n):
            at = (j * share) // half
            ps_send[j, top:end] = pas[at, top:end, j * share - at * half : (j + 1) * share - at * half]

        @pl.when(c == q)
        def _():
            ps_all[me, top:end] = ps_send[me, top:end]
            pl.when(jnp.logical_not(at_end))(ps_copies.start)

        second_full = second_full + dot_nt(pas[other, top:end], we_ref[other])
        for b in range(blocks):
            lo, hi = b * blk, (b + 1) * blk
            lhs = jnp.where(second_ref[top:end, lo:hi] > 0, second_full[:, lo:hi], 0.0).astype(bf16)
            ds[top:end, lo:hi] = lhs
            total = None
            for db in (-1, 0, 1):
                column = None
                for da in (-1, 0, 1):
                    t = 3 * (da + 1) + db + 1
                    y = moved(dot_nn(lhs, taps[t, lo:hi, :]), da, 0)
                    column = y if column is None else column + y
                column = moved(column, 0, db)
                total = column if total is None else total + column
            d_all[me, top:end, lo:hi] = jnp.where(
                first_ref[top:end, lo:hi] > 0, total, 0.0).astype(bf16)
            if q == 0 and b == 0:
                own_arrives(1)
        dfx_copies[q].start()
        if n > 1:
            @pl.when(s < last)
            def _():
                line_start(d_moves[0][q])

    @pl.when(at_end)
    def _():
        ps_copies.start()

    own_rows = pl.ds(pl.multiple_of(c * half, half), half)
    wr_copy.wait_recv()
    for q in range(2):
        top, end = q * hrows, (q + 1) * hrows
        grad = dot_nt(d_all[me, top:end], wr_ref[own_rows, :]) + pas[c, top:end].astype(f32)
        dfx_copies[q].wait_recv()
        ng[c, top:end] = (grad + dot_nt(dfx[top:end], wr_peer[...])).astype(bf16)

        @pl.when(s > 0)
        def _():
            hop_copies[q].start()

    ng_copy.start()

    @pl.when(s == last)
    def _():
        prepare_first()

    gf[...] = jnp.zeros_like(gf)
    for b in range(blocks):
        rhs = ds[:, b * blk : (b + 1) * blk]
        for t in range(9):
            dense = jnp.where(same, dot_nn(ft[t, b], rhs), 0.0)
            folded = jnp.sum(dense.reshape(blk // gw, gw, blk), axis=0)
            for j in range(n):
                gf[j, t * k : (t + 1) * k, b * blk : (b + 1) * blk] = folded[j * k : (j + 1) * k]
    g_send[...] = gf[...].astype(bf16)
    g_copies = Spread(3, lambda to: g_send.at[to], g_recv.at[me], g_recv.at[peers])

    if n > 1:
        @pl.when(s == last)
        def _():
            for q in range(2):
                line_start(d_moves[0][q])

    @pl.when(s < last)
    def _():
        bi_forward()

    ps_copies.wait_recv()
    ps_share.start()

    def d_forward(step):
        for q in range(2):
            line_forward(d_moves[step][q], d_moves[step + 1][q])

    for step in range(n - 2):
        @pl.when(s == last)
        def _():
            sec_forward(step)
            if step == 0:
                bi_forward()

        d_forward(step)

        @pl.when(s == last)
        def _():
            if step == 0:
                g_copies.start()

        if step == 0:
            ng_copy.wait_recv()
            grads_ref[:, :half] = ng[0]
            grads_ref[:, half:] = ng[1]
    if n > 2:
        for q in range(2):
            line_settle(d_moves[n - 3][q], d_moves[n - 2][q])

    @pl.when(s < last)
    def _():
        g_copies.start()

    for q in range(2):
        @pl.when(s == last)
        def _():
            if n > 2:
                line_settle(sec_moves[n - 3][q], sec_moves[n - 2][q])

        line_finish([step_moves[q] for step_moves in sec_moves], n - 3)
    ps_share.wait_recv()
    expand = dot_tn(sec_all[...].reshape(n * rows, width), ps_all[...].reshape(n * rows, share))
    expand_ref[...] = expand * norm
    bi_share.wait_recv()

    def reduce_crop(q):
        line_finish([step_moves[q] for step_moves in d_moves], n - 3)
        bi_rows = bi_all[:, q * hrows : (q + 1) * hrows].reshape(n * hrows, share)
        d_rows = d_all[:, q * hrows : (q + 1) * hrows].reshape(n * hrows, width)
        reduced = dot_tn(bi_rows, d_rows) * norm
        reduce_ref[...] = reduced if q == 0 else reduce_ref[...] + reduced

    reduce_crop(0)
    reduce_crop(1)
    g_copies.wait_recv()
    g_recv[me] = jnp.zeros(g_recv.shape[1:], bf16)
    total = gf[me]
    for j in range(n):
        total = total + g_recv[j].astype(f32)
    total = (total * norm)[: 9 * k]
    wide = jnp.broadcast_to(total[:, None, :], (9 * k, gw, width)).reshape(9 * k * gw, width)
    out_of = iota((9 * k * gw, width), 0) % gw == iota((9 * k * gw, width), 1) % gw
    wide = jnp.where(out_of, wide, 0.0)
    high = wide.astype(bf16)
    low = (wide - high.astype(f32)).astype(bf16)
    group_of = (iota((width, groups), 0) // gw == iota((width, groups), 1)).astype(f32).astype(bf16)
    group_ref[...] = dot_nn(high, group_of) + dot_nn(low, group_of)

    for move in [move for step_moves in sec_moves + d_moves for move in step_moves]:
        for copy, sends, _ in move:
            pl.when(sends)(copy.wait_send)
    for copy in [bi_share, ps_share, bi_copies, ps_copies, g_copies, wr_copy, ng_copy] + dfx_copies:
        copy.wait_send()

    @pl.when(counting)
    def _():
        for copies in cnt_copies:
            copies.wait_send()

    @pl.when(s > 0)
    def _():
        for copy in hop_copies:
            copy.wait_send()

    @pl.when(s < last)
    def _():
        for copy in fwd_copies:
            copy.wait_send()


def store_kernel(*refs):
    count = (len(refs) - 1) // 2
    copies = [pltpu.make_async_copy(refs[i], refs[count + i], refs[-1].at[i]) for i in range(count)]
    for copy in copies:
        copy.start()
    for copy in copies:
        copy.wait()


def on_device(
    block_inputs, out_pre, first_pre, second_pre, w_reduce, w_group, w_expand, w_lateral,
    teacher, top_grad, boxes, region_counts,
):
    n = lax.axis_size("dp")
    sections = lax.axis_size("section")
    crops, side, _, channels = top_grad.shape
    rows = crops * side * side
    width = first_pre.shape[4]
    lateral_width = w_lateral.shape[1]
    groups, gw = w_group.shape[2], w_group.shape[3]
    slots = boxes.shape[1]
    pixels = rows * n
    share = channels // n
    k = gw // n
    grows = -(-9 * k // 8) * 8
    half = channels // 2
    blk = min(256, width)
    hbm = pl.BlockSpec(memory_space=pltpu.HBM)
    vmem = pl.BlockSpec(memory_space=pltpu.VMEM)
    dma = pltpu.SemaphoreType.DMA
    peers = max(n - 1, 1)
    shapes = (
        ((rows, channels), bf16), ((share, width), f32),
        ((9 * k * gw, groups), f32), ((width, share), f32),
    )
    results = pl.pallas_call(
        functools.partial(kernel, (n, sections, crops, side, slots, pixels)),
        out_shape=tuple(pltpu.VMEM(shape, kind) for shape, kind in shapes),
        in_specs=[hbm] * 12,
        out_specs=(vmem,) * 4,
        scratch_shapes=[
            pltpu.SMEM((crops, 4, slots), jnp.int32),
            pltpu.SMEM((1, crops), jnp.int32),
            pltpu.VMEM((3, rows, channels), bf16),
            pltpu.VMEM((2, rows, width), bf16),
            pltpu.VMEM((channels, width), bf16),
            pltpu.VMEM((9 * gw * gw, groups), bf16),
            pltpu.VMEM((2, width, half), bf16),
            pltpu.VMEM((channels, lateral_width), bf16),
            pltpu.VMEM((rows, lateral_width), bf16),
            dma((11,)),
            pltpu.VMEM((2, rows, half), bf16),
            pltpu.VMEM((2, rows, half), bf16),
            pltpu.VMEM((half, width), bf16),
            pltpu.VMEM((rows, width), bf16),
            pltpu.VMEM((2, rows, half), bf16),
            pltpu.VMEM((rows, width), bf16),
            pltpu.VMEM((n, rows, width), bf16),
            pltpu.VMEM((n, rows, width), bf16),
            pltpu.VMEM((n, rows, share), bf16),
            pltpu.VMEM((n, rows, share), bf16),
            pltpu.VMEM((n, rows, share), bf16),
            pltpu.VMEM((n, rows, share), bf16),
            pltpu.VMEM((n, grows, width), f32),
            pltpu.VMEM((n, grows, width), bf16),
            pltpu.VMEM((n, grows, width), bf16),
            pltpu.VMEM((n, 8, 128), f32),
            pltpu.VMEM((9, width, blk), bf16),
            pltpu.VMEM((9, width // blk, blk, rows), bf16),
            dma((5,)), dma((4,)), dma((4,)), dma((4,)),
            dma((2,)), dma((2,)), dma((2,)), dma((2,)),
            dma((peers, 2, 2)), dma((peers, 2, 2)), dma((peers, 2, 2)), dma((peers, 2, 2)),
            dma((2,)), dma((2,)),
        ],
        compiler_params=pltpu.CompilerParams(
            collective_id=0, has_side_effects=True, vmem_limit_bytes=44 << 20,
        ),
    )(*(pltpu.with_memory_space_constraint(x, pltpu.HBM) for x in (
        boxes.transpose(0, 2, 1), region_counts.reshape(1, crops),
        block_inputs.reshape(rows, channels), out_pre.reshape(rows, channels),
        first_pre.reshape(rows, width), second_pre.reshape(rows, width),
        w_reduce[0], w_group[0].transpose(0, 2, 3, 1).reshape(9 * gw * gw, groups), w_expand[0], w_lateral,
        teacher.reshape(rows, lateral_width), top_grad.reshape(rows, channels),
    )))
    grads, reduced, group, expand = pl.pallas_call(
        store_kernel,
        out_shape=tuple(jax.ShapeDtypeStruct(shape, kind) for shape, kind in shapes),
        in_specs=[vmem] * 4,
        out_specs=(hbm,) * 4,
        scratch_shapes=[dma((4,))],
    )(*(pltpu.with_memory_space_constraint(x, pltpu.VMEM) for x in results))
    group = group.reshape(9, k, gw, groups).transpose(0, 3, 1, 2)
    return (
        grads.reshape(1, crops, side, side, channels), reduced[None], group[None], expand[None],
    )


def solution(mesh):
    return jax.shard_map(
        on_device,
        mesh=mesh,
        in_specs=(
            P("section", ("parts", "dp"), None, None, None),
            P("section", ("parts", "dp"), None, None, None),
            P("section", ("parts", "dp"), None, None, "chan"),
            P("section", ("parts", "dp"), None, None, "chan"),
            P("section", None, "chan"),
            P("section", None, "chan", None, None),
            P("section", "chan", None),
            P(),
            P(("parts", "dp"), None, None, None),
            P(("parts", "dp"), None, None, None),
            P(("parts", "dp"), None, None),
            P(("parts", "dp")),
        ),
        out_specs=(
            P("section", ("parts", "dp"), None, None, None),
            P(("parts", "section"), "dp", "chan"),
            P(("parts", "section"), None, "chan", "dp", None),
            P(("parts", "section"), "chan", "dp"),
        ),
        check_vma=False,
    )
```

```python
import functools
import math

import jax
import jax.numpy as jnp
from jax import lax
from jax.experimental import pallas as pl
from jax.experimental.pallas import tpu as pltpu
from jax.sharding import PartitionSpec as P

imitation_weight = 0.5
tap_offsets = [(tap // 3 - 1, tap % 3 - 1) for tap in range(9)]
f32 = jnp.float32
bf16 = jnp.bfloat16


def dot_nn(a, b):
    return lax.dot_general(a, b, (((1,), (0,)), ((), ())), preferred_element_type=f32)


def dot_nt(a, b):
    return lax.dot_general(a, b, (((1,), (1,)), ((), ())), preferred_element_type=f32)


def dot_tn(a, b):
    return lax.dot_general(a, b, (((0,), (0,)), ((), ())), preferred_element_type=f32)


def kernel(
    dims,
    boxes_hbm, counts_hbm, bi_hbm, out_hbm, first_hbm, second_hbm, wr_hbm, wg_hbm, we_hbm,
    wl_hbm, teacher_hbm, top_hbm,
    grads_ref, reduce_ref, group_ref, expand_ref,
    boxes_ref, counts_ref,
    full_ref, part_ref, wr_ref, wg_ref, we_ref, wl_ref, teacher_ref, load_sem,
    inc, pas, wr_peer, dfx, ng, ds, d_all, sec_all, bi_send, bi_all, ps_send, ps_all,
    gf, g_send, g_recv, cnt, taps, ft,
    dp_send, dp_recv, core_send, core_recv, hop_send, hop_recv, fwd_send, fwd_recv,
    sec_send, sec_recv, d_send, d_recv, share_send, share_recv,
):
    n, sections, crops, side, slots, pixels = dims
    out_ref, bi_ref, top_ref = (full_ref.at[i] for i in range(3))
    first_ref, second_ref = part_ref.at[0], part_ref.at[1]
    rows, channels = bi_ref.shape
    half = channels // 2
    width = first_ref.shape[1]
    groups = wg_ref.shape[1]
    gw = width // groups
    blk = taps.shape[2]
    blocks = width // blk
    cells = side * side
    share = channels // n
    k = gw // n
    hrows = rows // 2
    me = lax.axis_index("dp")
    s = lax.axis_index("section")
    c = lax.axis_index("chan")
    other = 1 - c
    last = sections - 1
    norm = 1.0 / math.sqrt(pixels)

    def remote(src, dst, send, recv, where):
        return pltpu.make_async_remote_copy(
            src_ref=src, dst_ref=dst, send_sem=send, recv_sem=recv,
            device_id=where, device_id_type=pl.DeviceIdType.MESH,
        )

    class Spread:
        def __init__(self, what, src_of, dst, moved, at=None, where={}):
            at = what if at is None else at
            self.copies = [
                remote(src_of(to), dst, dp_send.at[at], dp_recv.at[what], {"dp": to, **where})
                for to in (lax.rem(me + step, n) for step in range(1, n))
            ]
            self.sent = pltpu.make_async_copy(moved, moved, dp_send.at[at])
            self.received = pltpu.make_async_copy(moved, moved, dp_recv.at[what])

        def start(self):
            for copy in self.copies:
                copy.start()

        def wait_recv(self):
            self.received.wait()

        def wait_send(self):
            self.sent.wait()

    mine = pl.ds(pl.multiple_of(c * hrows, hrows), hrows)
    peers = pl.ds(0, n - 1)
    crop_rows = [pl.ds(q * hrows, hrows) for q in range(2)]

    def share_copy(which, buf):
        return remote(buf.at[:, mine], buf.at[:, mine], share_send.at[which],
                      share_recv.at[which], {"chan": other})

    def line(step, block, send, recv):
        ahead = block(lax.max(me - step, 0))
        behind = block(lax.min(me + step, n - 1))
        right = remote(ahead, ahead, send.at[0], recv.at[0], {"dp": lax.min(me + 1, n - 1)})
        left = remote(behind, behind, send.at[1], recv.at[1], {"dp": lax.max(me - 1, 0)})
        return (
            (right, (me - step >= 0) & (me + 1 < n), me - 1 - step >= 0),
            (left, (me + step < n) & (me >= 1), me + 1 + step < n),
        )

    def line_start(moves):
        for copy, sends, _ in moves:
            pl.when(sends)(copy.start)

    def line_forward(moves, following):
        for (copy, _, receives), (onward, sends, _) in zip(moves, following):
            @pl.when(receives & sends)
            def _():
                copy.wait_recv()
                onward.start()

    def line_settle(moves, following):
        for (copy, _, receives), (_, sends, _) in zip(moves, following):
            pl.when(receives & jnp.logical_not(sends))(copy.wait_recv)

    def line_finish(moves):
        for step in range(n - 1):
            if step == n - 2:
                for copy, _, receives in moves[step]:
                    pl.when(receives)(copy.wait_recv)
            else:
                line_settle(moves[step], moves[step + 1])

    barrier = pltpu.get_barrier_semaphore()
    mesh_type = pl.DeviceIdType.MESH
    for step in range(1, n):
        pl.semaphore_signal(barrier, inc=1, device_id={"dp": lax.rem(me + step, n)},
                            device_id_type=mesh_type)
    pl.semaphore_signal(barrier, inc=1, device_id={"chan": other}, device_id_type=mesh_type)

    @pl.when((s == last) & (c == 0))
    def _():
        for step in range(1, n):
            pl.semaphore_signal(barrier, inc=1, device_id_type=mesh_type,
                                device_id={"dp": lax.rem(me + step, n), "chan": other})

    @pl.when(s > 0)
    def _():
        pl.semaphore_signal(barrier, inc=1, device_id={"section": s - 1},
                            device_id_type=mesh_type)

    @pl.when(s < last)
    def _():
        pl.semaphore_signal(barrier, inc=1, device_id={"section": s + 1},
                            device_id_type=mesh_type)

    pairs = (
        ("boxes", boxes_hbm, boxes_ref), ("counts", counts_hbm, counts_ref),
        ("second", second_hbm, second_ref), ("pair", out_hbm, out_ref), ("wl", wl_hbm, wl_ref),
        ("teacher", teacher_hbm, teacher_ref), ("pair", bi_hbm, bi_ref),
        ("wg", wg_hbm, wg_ref), ("top", top_hbm, top_ref), ("we", we_hbm.at[:, :half], we_ref.at[0]),
        ("we", we_hbm.at[:, half:], we_ref.at[1]), ("first", first_hbm, first_ref),
        ("wr", wr_hbm, wr_ref),
    )
    whole = {
        "boxes": boxes_ref, "counts": counts_ref, "pair": full_ref.at[0:2], "top": top_ref,
        "first": first_ref, "second": second_ref, "wl": wl_ref, "teacher": teacher_ref,
        "wg": wg_ref, "we": we_ref, "wr": wr_ref,
    }
    load_at = {name: load_sem.at[i] for i, name in enumerate(whole)}

    def load_start(some):
        for name, a, b in some:
            pltpu.make_async_copy(a, b, load_at[name]).start()

    def loaded(*names):
        for name in names:
            pltpu.make_async_copy(whole[name], whole[name], load_at[name]).wait()

    counting = (s == last) & (c == 1)
    at_end = (me == 0) | (me == n - 1)
    load_start(pairs[:8])

    @pl.when(jnp.logical_not(counting))
    def _():
        load_start(pairs[8:])

    loaded("boxes", "counts")
    row = lax.broadcasted_iota(jnp.int32, (cells, 128), 0)
    row_h, row_w = row // side, row % side
    masks = []
    for crop in range(crops):
        inside = jnp.zeros((cells, 128), f32)
        for r in range(slots):
            hit = ((row_h >= boxes_ref[crop, 0, r]) & (row_h < boxes_ref[crop, 1, r])
                   & (row_w >= boxes_ref[crop, 2, r]) & (row_w < boxes_ref[crop, 3, r])
                   & (counts_ref[0, crop] > r))
            inside = jnp.where(hit, 1.0, inside)
        masks.append(inside)
    mask = jnp.concatenate(masks, axis=0)
    cnt[me] = jnp.broadcast_to(jnp.sum(mask, axis=0, keepdims=True), (8, 128))

    pl.semaphore_wait(barrier, n + jnp.where(s > 0, 1, 0) + jnp.where(s < last, 1, 0)
                      + jnp.where(counting, n - 1, 0))

    cnt_copies = [Spread(0, lambda to: cnt.at[me], cnt.at[me], cnt.at[peers], at, {"chan": core})
                  for core, at in ((0, 0), (1, 4))]

    @pl.when(counting)
    def _():
        for copies in cnt_copies:
            copies.start()
        load_start(pairs[8:])

    wr_copy = remote(wr_ref.at[pl.ds(pl.multiple_of(other * half, half), half)], wr_peer,
                     core_send.at[0], core_recv.at[0], {"chan": other})
    loaded("second")
    sec_all[me] = jnp.maximum(second_ref[...], 0)
    sec_moves = [[line(step, lambda j, q=q: sec_all.at[j, pl.ds(q * hrows, hrows)],
                       sec_send.at[step, q], sec_recv.at[step, q])
                  for q in range(2)] for step in range(n - 1)]
    if n > 1:
        for q in range(2):
            line_start(sec_moves[0][q])
    loaded("pair")
    for j in range(n):
        bi_send[j] = bi_ref[:, j * share : (j + 1) * share]
    bi_all[me, mine] = bi_send[me, mine]

    bi_copies = Spread(1, lambda to: bi_send.at[to, mine], bi_all.at[me, mine],
                       bi_all.at[peers, mine])
    bi_share = share_copy(0, bi_all)

    def sec_forward(step):
        for q in range(2):
            line_forward(sec_moves[step][q], sec_moves[step + 1][q])

    def bi_forward():
        bi_copies.wait_recv()
        bi_share.start()

    pair = gw * gw
    iota = lambda shape, dim: lax.broadcasted_iota(jnp.int32, shape, dim)
    same = iota((blk, blk), 0) // gw == iota((blk, blk), 1) // gw

    def build_taps():
        same_out = iota((width, pair), 0) % gw == iota((width, pair), 1) % gw
        spread = (iota((pair, blk), 0) // gw == iota((pair, blk), 1) % gw).astype(f32).astype(bf16)
        inside = iota((width, blk), 0) // gw % (blk // gw) == iota((width, blk), 1) // gw
        by_group = wg_ref[...].astype(f32).T
        for t in range(9):
            values = by_group[:, t * pair : (t + 1) * pair]
            values = jnp.broadcast_to(values[:, None, :], (groups, gw, pair)).reshape(width, pair)
            values = jnp.where(same_out, values, 0.0).astype(bf16)
            taps[t] = jnp.where(inside, dot_nn(values, spread), 0.0).astype(bf16)

    def shifter(count):
        prow = lax.broadcasted_iota(jnp.int32, (count, blk), 0)
        p_w = prow % side
        p_h = (prow // side) % side

        def moved(x, a, b):
            shift = (side * a + b) % count
            if shift:
                x = pltpu.roll(x, shift, 0)
            if a:
                x = jnp.where(p_h >= 1 if a == 1 else p_h < side - 1, x, 0.0)
            if b:
                x = jnp.where(p_w >= 1 if b == 1 else p_w < side - 1, x, 0.0)
            return x

        return moved

    def prepare_first():
        moved = shifter(rows)
        for b in range(blocks):
            first = jnp.maximum(first_ref[:, b * blk : (b + 1) * blk], 0).astype(f32)
            for t, (da, db) in enumerate(tap_offsets):
                ft[t, b] = moved(first, -da, -db).T.astype(bf16)

    hop_copies = [
        remote(ng.at[c, crop_rows[q]], inc.at[c, crop_rows[q]],
               hop_send.at[q], hop_recv.at[q], {"section": lax.max(s - 1, 0)})
        for q in range(2)
    ]
    fwd_copies = [
        remote(inc.at[c, crop_rows[q]], inc.at[c, crop_rows[q]],
               fwd_send.at[q], fwd_recv.at[q], {"chan": other})
        for q in range(2)
    ]

    @pl.when(s == last)
    def _():
        loaded("wl", "teacher")
        feature = jnp.maximum(out_ref[...], 0)
        lateral = dot_nn(feature, wl_ref[...])
        error = (mask[:, 0:1] * (lateral - teacher_ref[...].astype(f32))).astype(bf16)
        imitation = dot_nt(error, wl_ref[...])
        loaded("wg")
        build_taps()
        loaded("top", "first", "we", "wr")
        wr_copy.start()
        cnt_copies[0].wait_recv()
        bi_copies.start()
        covered = cnt[0]
        for j in range(1, n):
            covered = covered + cnt[j]
        scale = (imitation_weight * pixels) / covered[0:1, 0:1]
        start = (top_ref[...].astype(f32) + imitation * scale).astype(bf16)
        start = jnp.where(out_ref[...] > 0, start, jnp.zeros_like(start))
        pas[0] = start[:, :half]
        pas[1] = start[:, half:]

    @pl.when(s < last)
    def _():
        loaded("wl", "teacher", "wg", "top", "first", "we", "wr")
        wr_copy.start()
        build_taps()
        prepare_first()
        for step in range(n - 2):
            sec_forward(step)
        pl.when(jnp.logical_not(at_end))(bi_copies.start)

    ps_copies = Spread(2, lambda to: ps_send.at[to, mine], ps_all.at[me, mine],
                       ps_all.at[peers, mine])
    ps_share = share_copy(1, ps_all)
    d_moves = [[line(step, lambda j, q=q: d_all.at[j, crop_rows[q]], d_send.at[step, q],
                     d_recv.at[step, q]) for q in range(2)] for step in range(n - 1)]
    dfx_copies = [remote(d_all.at[me, crop_rows[q]], dfx.at[crop_rows[q]], core_send.at[1 + q],
                         core_recv.at[1 + q], {"chan": other}) for q in range(2)]
    ng_copy = remote(ng.at[c], ng.at[c], core_send.at[3], core_recv.at[3], {"chan": other})

    def gate_half(h, q):
        at = pl.ds(pl.multiple_of(h * half, half), half)
        value = inc[h, crop_rows[q]]
        gate = out_ref[q * hrows : (q + 1) * hrows, at] > 0
        pas[h, crop_rows[q]] = jnp.where(gate, value, jnp.zeros_like(value))

    def own_arrives(q):
        @pl.when(s < last)
        def _():
            hop_copies[q].wait_recv()
            fwd_copies[q].start()
            if q == 0:
                pl.when(at_end)(bi_copies.start)
            gate_half(c, q)

    def other_arrives(q):
        @pl.when(s < last)
        def _():
            fwd_copies[q].wait_recv()
            gate_half(other, q)

    moved = shifter(hrows)
    own_arrives(0)
    for q in range(2):
        top, end = q * hrows, (q + 1) * hrows
        second_full = dot_nt(pas[c, top:end], we_ref[c])
        other_arrives(q)
        for j in range(n):
            at = (j * share) // half
            ps_send[j, top:end] = pas[at, top:end, j * share - at * half : (j + 1) * share - at * half]

        @pl.when(c == q)
        def _():
            ps_all[me, top:end] = ps_send[me, top:end]
            pl.when(jnp.logical_not(at_end))(ps_copies.start)

        second_full = second_full + dot_nt(pas[other, top:end], we_ref[other])
        for b in range(blocks):
            lo, hi = b * blk, (b + 1) * blk
            lhs = jnp.where(second_ref[top:end, lo:hi] > 0, second_full[:, lo:hi], 0.0).astype(bf16)
            ds[top:end, lo:hi] = lhs
            total = None
            for db in (-1, 0, 1):
                column = None
                for da in (-1, 0, 1):
                    t = 3 * (da + 1) + db + 1
                    y = moved(dot_nn(lhs, taps[t, lo:hi, :]), da, 0)
                    column = y if column is None else column + y
                column = moved(column, 0, db)
                total = column if total is None else total + column
            d_all[me, top:end, lo:hi] = jnp.where(
                first_ref[top:end, lo:hi] > 0, total, 0.0).astype(bf16)
            if q == 0 and b == 0:
                own_arrives(1)
        dfx_copies[q].start()
        if n > 1:
            @pl.when(s < last)
            def _():
                line_start(d_moves[0][q])

    @pl.when(at_end)
    def _():
        ps_copies.start()

    own_rows = pl.ds(pl.multiple_of(c * half, half), half)
    wr_copy.wait_recv()
    for q in range(2):
        top, end = q * hrows, (q + 1) * hrows
        grad = dot_nt(d_all[me, top:end], wr_ref[own_rows, :]) + pas[c, top:end].astype(f32)
        dfx_copies[q].wait_recv()
        ng[c, top:end] = (grad + dot_nt(dfx[top:end], wr_peer[...])).astype(bf16)

        @pl.when(s > 0)
        def _():
            hop_copies[q].start()

    ng_copy.start()

    @pl.when(s == last)
    def _():
        prepare_first()

    gf[...] = jnp.zeros_like(gf)
    for b in range(blocks):
        rhs = ds[:, b * blk : (b + 1) * blk]
        for t in range(9):
            dense = jnp.where(same, dot_nn(ft[t, b], rhs), 0.0)
            folded = jnp.sum(dense.reshape(blk // gw, gw, blk), axis=0)
            for j in range(n):
                gf[j, t * k : (t + 1) * k, b * blk : (b + 1) * blk] = folded[j * k : (j + 1) * k]
    g_send[...] = gf[...].astype(bf16)
    g_copies = Spread(3, lambda to: g_send.at[to], g_recv.at[me], g_recv.at[peers])

    if n > 1:
        @pl.when(s == last)
        def _():
            for q in range(2):
                line_start(d_moves[0][q])

    def d_forward(step):
        for q in range(2):
            line_forward(d_moves[step][q], d_moves[step + 1][q])

    for step in range(n - 2):
        @pl.when(s == last)
        def _():
            sec_forward(step)
            if step == 0:
                bi_forward()

        d_forward(step)

        @pl.when(s == last)
        def _():
            if step == 0:
                g_copies.start()

        if step == 0:
            @pl.when((s < last) & at_end)
            def _():
                g_copies.start()

            @pl.when(s < last)
            def _():
                bi_forward()

            ps_copies.wait_recv()
            ps_share.start()
            ng_copy.wait_recv()
            grads_ref[:, :half] = ng[0]
            grads_ref[:, half:] = ng[1]
    @pl.when((s < last) & jnp.logical_not(at_end))
    def _():
        g_copies.start()

    for q in range(2):
        line_finish([step_moves[q] for step_moves in sec_moves])
    ps_share.wait_recv()
    expand = dot_tn(sec_all[...].reshape(n * rows, width), ps_all[...].reshape(n * rows, share))
    expand_ref[...] = expand * norm
    bi_share.wait_recv()

    def reduce_crop(q):
        line_finish([step_moves[q] for step_moves in d_moves])
        bi_rows = bi_all[:, q * hrows : (q + 1) * hrows].reshape(n * hrows, share)
        d_rows = d_all[:, q * hrows : (q + 1) * hrows].reshape(n * hrows, width)
        reduced = dot_tn(bi_rows, d_rows) * norm
        reduce_ref[...] = reduced if q == 0 else reduce_ref[...] + reduced

    reduce_crop(0)
    reduce_crop(1)
    g_copies.wait_recv()
    g_recv[me] = jnp.zeros(g_recv.shape[1:], bf16)
    total = gf[me]
    for j in range(n):
        total = total + g_recv[j].astype(f32)
    total = (total * norm)[: 9 * k]
    wide = jnp.broadcast_to(total[:, None, :], (9 * k, gw, width)).reshape(9 * k * gw, width)
    out_of = iota((9 * k * gw, width), 0) % gw == iota((9 * k * gw, width), 1) % gw
    wide = jnp.where(out_of, wide, 0.0)
    high = wide.astype(bf16)
    low = (wide - high.astype(f32)).astype(bf16)
    group_of = (iota((width, groups), 0) // gw == iota((width, groups), 1)).astype(f32).astype(bf16)
    group_ref[...] = dot_nn(high, group_of) + dot_nn(low, group_of)

    for move in [move for step_moves in sec_moves + d_moves for move in step_moves]:
        for copy, sends, _ in move:
            pl.when(sends)(copy.wait_send)
    for copy in [bi_share, ps_share, bi_copies, ps_copies, g_copies, wr_copy, ng_copy] + dfx_copies:
        copy.wait_send()

    @pl.when(counting)
    def _():
        for copies in cnt_copies:
            copies.wait_send()

    @pl.when(s > 0)
    def _():
        for copy in hop_copies:
            copy.wait_send()

    @pl.when(s < last)
    def _():
        for copy in fwd_copies:
            copy.wait_send()


def store_kernel(*refs):
    count = (len(refs) - 1) // 2
    copies = [pltpu.make_async_copy(refs[i], refs[count + i], refs[-1].at[i]) for i in range(count)]
    for copy in copies:
        copy.start()
    for copy in copies:
        copy.wait()


def on_device(
    block_inputs, out_pre, first_pre, second_pre, w_reduce, w_group, w_expand, w_lateral,
    teacher, top_grad, boxes, region_counts,
):
    n = lax.axis_size("dp")
    sections = lax.axis_size("section")
    crops, side, _, channels = top_grad.shape
    rows = crops * side * side
    width = first_pre.shape[4]
    lateral_width = w_lateral.shape[1]
    groups, gw = w_group.shape[2], w_group.shape[3]
    slots = boxes.shape[1]
    pixels = rows * n
    share = channels // n
    k = gw // n
    grows = -(-9 * k // 8) * 8
    half = channels // 2
    blk = min(256, width)
    hbm = pl.BlockSpec(memory_space=pltpu.HBM)
    vmem = pl.BlockSpec(memory_space=pltpu.VMEM)
    dma = pltpu.SemaphoreType.DMA
    peers = max(n - 1, 1)
    shapes = (
        ((rows, channels), bf16), ((share, width), f32),
        ((9 * k * gw, groups), f32), ((width, share), f32),
    )
    results = pl.pallas_call(
        functools.partial(kernel, (n, sections, crops, side, slots, pixels)),
        out_shape=tuple(pltpu.VMEM(shape, kind) for shape, kind in shapes),
        in_specs=[hbm] * 12,
        out_specs=(vmem,) * 4,
        scratch_shapes=[
            pltpu.SMEM((crops, 4, slots), jnp.int32),
            pltpu.SMEM((1, crops), jnp.int32),
            pltpu.VMEM((3, rows, channels), bf16),
            pltpu.VMEM((2, rows, width), bf16),
            pltpu.VMEM((channels, width), bf16),
            pltpu.VMEM((9 * gw * gw, groups), bf16),
            pltpu.VMEM((2, width, half), bf16),
            pltpu.VMEM((channels, lateral_width), bf16),
            pltpu.VMEM((rows, lateral_width), bf16),
            dma((11,)),
            pltpu.VMEM((2, rows, half), bf16),
            pltpu.VMEM((2, rows, half), bf16),
            pltpu.VMEM((half, width), bf16),
            pltpu.VMEM((rows, width), bf16),
            pltpu.VMEM((2, rows, half), bf16),
            pltpu.VMEM((rows, width), bf16),
            pltpu.VMEM((n, rows, width), bf16),
            pltpu.VMEM((n, rows, width), bf16),
            pltpu.VMEM((n, rows, share), bf16),
            pltpu.VMEM((n, rows, share), bf16),
            pltpu.VMEM((n, rows, share), bf16),
            pltpu.VMEM((n, rows, share), bf16),
            pltpu.VMEM((n, grows, width), f32),
            pltpu.VMEM((n, grows, width), bf16),
            pltpu.VMEM((n, grows, width), bf16),
            pltpu.VMEM((n, 8, 128), f32),
            pltpu.VMEM((9, width, blk), bf16),
            pltpu.VMEM((9, width // blk, blk, rows), bf16),
            dma((5,)), dma((4,)), dma((4,)), dma((4,)),
            dma((2,)), dma((2,)), dma((2,)), dma((2,)),
            dma((peers, 2, 2)), dma((peers, 2, 2)), dma((peers, 2, 2)), dma((peers, 2, 2)),
            dma((2,)), dma((2,)),
        ],
        compiler_params=pltpu.CompilerParams(
            collective_id=0, has_side_effects=True, vmem_limit_bytes=44 << 20,
        ),
    )(*(pltpu.with_memory_space_constraint(x, pltpu.HBM) for x in (
        boxes.transpose(0, 2, 1), region_counts.reshape(1, crops),
        block_inputs.reshape(rows, channels), out_pre.reshape(rows, channels),
        first_pre.reshape(rows, width), second_pre.reshape(rows, width),
        w_reduce[0], w_group[0].transpose(0, 2, 3, 1).reshape(9 * gw * gw, groups), w_expand[0], w_lateral,
        teacher.reshape(rows, lateral_width), top_grad.reshape(rows, channels),
    )))
    grads, reduced, group, expand = pl.pallas_call(
        store_kernel,
        out_shape=tuple(jax.ShapeDtypeStruct(shape, kind) for shape, kind in shapes),
        in_specs=[vmem] * 4,
        out_specs=(hbm,) * 4,
        scratch_shapes=[dma((4,))],
    )(*(pltpu.with_memory_space_constraint(x, pltpu.VMEM) for x in results))
    group = group.reshape(9, k, gw, groups).transpose(0, 3, 1, 2)
    return (
        grads.reshape(1, crops, side, side, channels), reduced[None], group[None], expand[None],
    )


def solution(mesh):
    return jax.shard_map(
        on_device,
        mesh=mesh,
        in_specs=(
            P("section", ("parts", "dp"), None, None, None),
            P("section", ("parts", "dp"), None, None, None),
            P("section", ("parts", "dp"), None, None, "chan"),
            P("section", ("parts", "dp"), None, None, "chan"),
            P("section", None, "chan"),
            P("section", None, "chan", None, None),
            P("section", "chan", None),
            P(),
            P(("parts", "dp"), None, None, None),
            P(("parts", "dp"), None, None, None),
            P(("parts", "dp"), None, None),
            P(("parts", "dp")),
        ),
        out_specs=(
            P("section", ("parts", "dp"), None, None, None),
            P(("parts", "section"), "dp", "chan"),
            P(("parts", "section"), None, "chan", "dp", None),
            P(("parts", "section"), "chan", "dp"),
        ),
        check_vma=False,
    )
```

```python
import functools
import math

import jax
import jax.numpy as jnp
from jax import lax
from jax.experimental import pallas as pl
from jax.experimental.pallas import tpu as pltpu
from jax.sharding import PartitionSpec as P

imitation_weight = 0.5
tap_offsets = [(tap // 3 - 1, tap % 3 - 1) for tap in range(9)]
f32 = jnp.float32
bf16 = jnp.bfloat16


def dot_nn(a, b):
    return lax.dot_general(a, b, (((1,), (0,)), ((), ())), preferred_element_type=f32)


def dot_nt(a, b):
    return lax.dot_general(a, b, (((1,), (1,)), ((), ())), preferred_element_type=f32)


def dot_tn(a, b):
    return lax.dot_general(a, b, (((0,), (0,)), ((), ())), preferred_element_type=f32)


def kernel(
    dims,
    boxes_hbm, counts_hbm, bi_hbm, out_hbm, first_hbm, second_hbm, wr_hbm, wg_hbm, we_hbm,
    wl_hbm, teacher_hbm, top_hbm,
    grads_ref, reduce_ref, group_ref, expand_ref,
    boxes_ref, counts_ref,
    full_ref, part_ref, wr_ref, wg_ref, we_ref, wl_ref, teacher_ref, load_sem,
    inc, pas, wr_peer, dfx, ng, ds, d_all, sec_all, bi_send, bi_all, ps_send, ps_all,
    gf, g_send, g_recv, cnt, taps, ft,
    dp_send, dp_recv, core_send, core_recv, hop_send, hop_recv, fwd_send, fwd_recv,
    sec_send, sec_recv, d_send, d_recv, share_send, share_recv,
):
    n, sections, crops, side, slots, pixels = dims
    out_ref, bi_ref, top_ref = (full_ref.at[i] for i in range(3))
    first_ref, second_ref = part_ref.at[0], part_ref.at[1]
    rows, channels = bi_ref.shape
    half = channels // 2
    width = first_ref.shape[1]
    groups = wg_ref.shape[1]
    gw = width // groups
    blk = taps.shape[2]
    blocks = width // blk
    cells = side * side
    share = channels // n
    k = gw // n
    hrows = rows // 2
    me = lax.axis_index("dp")
    s = lax.axis_index("section")
    c = lax.axis_index("chan")
    other = 1 - c
    last = sections - 1
    norm = 1.0 / math.sqrt(pixels)

    def remote(src, dst, send, recv, where):
        return pltpu.make_async_remote_copy(
            src_ref=src, dst_ref=dst, send_sem=send, recv_sem=recv,
            device_id=where, device_id_type=pl.DeviceIdType.MESH,
        )

    class Spread:
        def __init__(self, what, src_of, dst, moved, at=None, where={}):
            at = what if at is None else at
            self.copies = [
                remote(src_of(to), dst, dp_send.at[at], dp_recv.at[what], {"dp": to, **where})
                for to in (lax.rem(me + step, n) for step in range(1, n))
            ]
            self.sent = pltpu.make_async_copy(moved, moved, dp_send.at[at])
            self.received = pltpu.make_async_copy(moved, moved, dp_recv.at[what])

        def start(self):
            for copy in self.copies:
                copy.start()

        def wait_recv(self):
            self.received.wait()

        def wait_send(self):
            self.sent.wait()

    mine = pl.ds(pl.multiple_of(c * hrows, hrows), hrows)
    peers = pl.ds(0, n - 1)
    crop_rows = [pl.ds(q * hrows, hrows) for q in range(2)]

    def share_copy(which, buf):
        return remote(buf.at[:, mine], buf.at[:, mine], share_send.at[which],
                      share_recv.at[which], {"chan": other})

    def line(step, block, send, recv):
        ahead = block(lax.max(me - step, 0))
        behind = block(lax.min(me + step, n - 1))
        right = remote(ahead, ahead, send.at[0], recv.at[0], {"dp": lax.min(me + 1, n - 1)})
        left = remote(behind, behind, send.at[1], recv.at[1], {"dp": lax.max(me - 1, 0)})
        return (
            (right, (me - step >= 0) & (me + 1 < n), me - 1 - step >= 0),
            (left, (me + step < n) & (me >= 1), me + 1 + step < n),
        )

    def line_start(moves):
        for copy, sends, _ in moves:
            pl.when(sends)(copy.start)

    def line_forward(moves, following):
        for (copy, _, receives), (onward, sends, _) in zip(moves, following):
            @pl.when(receives & sends)
            def _():
                copy.wait_recv()
                onward.start()

    def line_settle(moves, following):
        for (copy, _, receives), (_, sends, _) in zip(moves, following):
            pl.when(receives & jnp.logical_not(sends))(copy.wait_recv)

    def line_finish(moves):
        for step in range(n - 1):
            if step == n - 2:
                for copy, _, receives in moves[step]:
                    pl.when(receives)(copy.wait_recv)
            else:
                line_settle(moves[step], moves[step + 1])

    barrier = pltpu.get_barrier_semaphore()
    mesh_type = pl.DeviceIdType.MESH
    for step in range(1, n):
        pl.semaphore_signal(barrier, inc=1, device_id={"dp": lax.rem(me + step, n)},
                            device_id_type=mesh_type)
    pl.semaphore_signal(barrier, inc=1, device_id={"chan": other}, device_id_type=mesh_type)

    @pl.when((s == last) & (c == 0))
    def _():
        for step in range(1, n):
            pl.semaphore_signal(barrier, inc=1, device_id_type=mesh_type,
                                device_id={"dp": lax.rem(me + step, n), "chan": other})

    @pl.when(s > 0)
    def _():
        pl.semaphore_signal(barrier, inc=1, device_id={"section": s - 1},
                            device_id_type=mesh_type)

    @pl.when(s < last)
    def _():
        pl.semaphore_signal(barrier, inc=1, device_id={"section": s + 1},
                            device_id_type=mesh_type)

    pairs = (
        ("boxes", boxes_hbm, boxes_ref), ("counts", counts_hbm, counts_ref),
        ("second", second_hbm, second_ref), ("pair", out_hbm, out_ref), ("wl", wl_hbm, wl_ref),
        ("teacher", teacher_hbm, teacher_ref), ("pair", bi_hbm, bi_ref),
        ("wg", wg_hbm, wg_ref), ("top", top_hbm, top_ref), ("we", we_hbm.at[:, :half], we_ref.at[0]),
        ("we", we_hbm.at[:, half:], we_ref.at[1]), ("first", first_hbm, first_ref),
        ("wr", wr_hbm, wr_ref),
    )
    whole = {
        "boxes": boxes_ref, "counts": counts_ref, "pair": full_ref.at[0:2], "top": top_ref,
        "first": first_ref, "second": second_ref, "wl": wl_ref, "teacher": teacher_ref,
        "wg": wg_ref, "we": we_ref, "wr": wr_ref,
    }
    load_at = {name: load_sem.at[i] for i, name in enumerate(whole)}

    def load_start(some):
        for name, a, b in some:
            pltpu.make_async_copy(a, b, load_at[name]).start()

    def loaded(*names):
        for name in names:
            pltpu.make_async_copy(whole[name], whole[name], load_at[name]).wait()

    counting = (s == last) & (c == 1)
    at_end = (me == 0) | (me == n - 1)
    load_start(pairs[:8])

    @pl.when(jnp.logical_not(counting))
    def _():
        load_start(pairs[8:])

    loaded("boxes", "counts")
    row = lax.broadcasted_iota(jnp.int32, (cells, 128), 0)
    row_h, row_w = row // side, row % side
    masks = []
    for crop in range(crops):
        inside = jnp.zeros((cells, 128), f32)
        for r in range(slots):
            hit = ((row_h >= boxes_ref[crop, 0, r]) & (row_h < boxes_ref[crop, 1, r])
                   & (row_w >= boxes_ref[crop, 2, r]) & (row_w < boxes_ref[crop, 3, r])
                   & (counts_ref[0, crop] > r))
            inside = jnp.where(hit, 1.0, inside)
        masks.append(inside)
    mask = jnp.concatenate(masks, axis=0)
    cnt[me] = jnp.broadcast_to(jnp.sum(mask, axis=0, keepdims=True), (8, 128))

    pl.semaphore_wait(barrier, n + jnp.where(s > 0, 1, 0) + jnp.where(s < last, 1, 0)
                      + jnp.where(counting, n - 1, 0))

    cnt_copies = [Spread(0, lambda to: cnt.at[me], cnt.at[me], cnt.at[peers], at, {"chan": core})
                  for core, at in ((0, 0), (1, 4))]

    @pl.when(counting)
    def _():
        for copies in cnt_copies:
            copies.start()
        load_start(pairs[8:])

    wr_copy = remote(wr_ref.at[pl.ds(pl.multiple_of(other * half, half), half)], wr_peer,
                     core_send.at[0], core_recv.at[0], {"chan": other})
    loaded("second")
    sec_all[me] = jnp.maximum(second_ref[...], 0)
    sec_moves = [[line(step, lambda j, q=q: sec_all.at[j, pl.ds(q * hrows, hrows)],
                       sec_send.at[step, q], sec_recv.at[step, q])
                  for q in range(2)] for step in range(n - 1)]
    if n > 1:
        for q in range(2):
            line_start(sec_moves[0][q])
    loaded("pair")
    for j in range(n):
        bi_send[j] = bi_ref[:, j * share : (j + 1) * share]
    bi_all[me, mine] = bi_send[me, mine]

    bi_copies = Spread(1, lambda to: bi_send.at[to, mine], bi_all.at[me, mine],
                       bi_all.at[peers, mine])
    bi_share = share_copy(0, bi_all)

    def sec_forward(step):
        for q in range(2):
            line_forward(sec_moves[step][q], sec_moves[step + 1][q])

    def bi_forward():
        bi_copies.wait_recv()
        bi_share.start()

    pair = gw * gw
    iota = lambda shape, dim: lax.broadcasted_iota(jnp.int32, shape, dim)
    same = iota((blk, blk), 0) // gw == iota((blk, blk), 1) // gw

    def build_taps():
        same_out = iota((width, pair), 0) % gw == iota((width, pair), 1) % gw
        spread = (iota((pair, blk), 0) // gw == iota((pair, blk), 1) % gw).astype(f32).astype(bf16)
        inside = iota((width, blk), 0) // gw % (blk // gw) == iota((width, blk), 1) // gw
        by_group = wg_ref[...].astype(f32).T
        for t in range(9):
            values = by_group[:, t * pair : (t + 1) * pair]
            values = jnp.broadcast_to(values[:, None, :], (groups, gw, pair)).reshape(width, pair)
            values = jnp.where(same_out, values, 0.0).astype(bf16)
            taps[t] = jnp.where(inside, dot_nn(values, spread), 0.0).astype(bf16)

    def shifter(count):
        prow = lax.broadcasted_iota(jnp.int32, (count, blk), 0)
        p_w = prow % side
        p_h = (prow // side) % side

        def moved(x, a, b):
            shift = (side * a + b) % count
            if shift:
                x = pltpu.roll(x, shift, 0)
            if a:
                x = jnp.where(p_h >= 1 if a == 1 else p_h < side - 1, x, 0.0)
            if b:
                x = jnp.where(p_w >= 1 if b == 1 else p_w < side - 1, x, 0.0)
            return x

        return moved

    def prepare_first():
        moved = shifter(rows)
        for b in range(blocks):
            first = jnp.maximum(first_ref[:, b * blk : (b + 1) * blk], 0).astype(f32)
            for t, (da, db) in enumerate(tap_offsets):
                ft[t, b] = moved(first, -da, -db).T.astype(bf16)

    hop_copies = [
        remote(ng.at[c, crop_rows[q]], inc.at[c, crop_rows[q]],
               hop_send.at[q], hop_recv.at[q], {"section": lax.max(s - 1, 0)})
        for q in range(2)
    ]
    fwd_copies = [
        remote(inc.at[c, crop_rows[q]], inc.at[c, crop_rows[q]],
               fwd_send.at[q], fwd_recv.at[q], {"chan": other})
        for q in range(2)
    ]

    @pl.when(s == last)
    def _():
        loaded("wl", "teacher")
        feature = jnp.maximum(out_ref[...], 0)
        lateral = dot_nn(feature, wl_ref[...])
        error = (mask[:, 0:1] * (lateral - teacher_ref[...].astype(f32))).astype(bf16)
        imitation = dot_nt(error, wl_ref[...])
        loaded("wg")
        build_taps()
        loaded("top", "first", "we", "wr")
        wr_copy.start()
        cnt_copies[0].wait_recv()
        bi_copies.start()
        covered = cnt[0]
        for j in range(1, n):
            covered = covered + cnt[j]
        scale = (imitation_weight * pixels) / covered[0:1, 0:1]
        start = (top_ref[...].astype(f32) + imitation * scale).astype(bf16)
        start = jnp.where(out_ref[...] > 0, start, jnp.zeros_like(start))
        pas[0] = start[:, :half]
        pas[1] = start[:, half:]

    @pl.when(s < last)
    def _():
        loaded("wl", "teacher", "wg", "top", "first", "we", "wr")
        wr_copy.start()
        build_taps()
        prepare_first()
        for step in range(n - 2):
            sec_forward(step)
        pl.when(jnp.logical_not(at_end))(bi_copies.start)

    ps_copies = Spread(2, lambda to: ps_send.at[to, mine], ps_all.at[me, mine],
                       ps_all.at[peers, mine])
    ps_share = share_copy(1, ps_all)
    d_moves = [[line(step, lambda j, q=q: d_all.at[j, crop_rows[q]], d_send.at[step, q],
                     d_recv.at[step, q]) for q in range(2)] for step in range(n - 1)]
    dfx_copies = [remote(d_all.at[me, crop_rows[q]], dfx.at[crop_rows[q]], core_send.at[1 + q],
                         core_recv.at[1 + q], {"chan": other}) for q in range(2)]
    ng_copy = remote(ng.at[c], ng.at[c], core_send.at[3], core_recv.at[3], {"chan": other})

    def gate_half(h, q):
        at = pl.ds(pl.multiple_of(h * half, half), half)
        value = inc[h, crop_rows[q]]
        gate = out_ref[q * hrows : (q + 1) * hrows, at] > 0
        pas[h, crop_rows[q]] = jnp.where(gate, value, jnp.zeros_like(value))

    def own_arrives(q, where=None):
        @pl.when((s < last) & where if where is not None else s < last)
        def _():
            hop_copies[q].wait_recv()
            fwd_copies[q].start()
            if q == 0:
                pl.when(at_end)(bi_copies.start)
            gate_half(c, q)

    def other_arrives(q):
        @pl.when(s < last)
        def _():
            fwd_copies[q].wait_recv()
            gate_half(other, q)

    moved = shifter(hrows)
    own_arrives(0)
    for q in range(2):
        top, end = q * hrows, (q + 1) * hrows
        second_full = dot_nt(pas[c, top:end], we_ref[c])
        if q == 0:
            own_arrives(1, c == 1)
        other_arrives(q)
        for j in range(n):
            at = (j * share) // half
            ps_send[j, top:end] = pas[at, top:end, j * share - at * half : (j + 1) * share - at * half]

        @pl.when(c == q)
        def _():
            ps_all[me, top:end] = ps_send[me, top:end]
            pl.when(jnp.logical_not(at_end))(ps_copies.start)

        second_full = second_full + dot_nt(pas[other, top:end], we_ref[other])
        for b in range(blocks):
            lo, hi = b * blk, (b + 1) * blk
            lhs = jnp.where(second_ref[top:end, lo:hi] > 0, second_full[:, lo:hi], 0.0).astype(bf16)
            ds[top:end, lo:hi] = lhs
            total = None
            for db in (-1, 0, 1):
                column = None
                for da in (-1, 0, 1):
                    t = 3 * (da + 1) + db + 1
                    y = moved(dot_nn(lhs, taps[t, lo:hi, :]), da, 0)
                    column = y if column is None else column + y
                column = moved(column, 0, db)
                total = column if total is None else total + column
            d_all[me, top:end, lo:hi] = jnp.where(
                first_ref[top:end, lo:hi] > 0, total, 0.0).astype(bf16)
            if q == 0 and b == 0:
                own_arrives(1, c == 0)
        dfx_copies[q].start()
        if n > 1:
            @pl.when(s < last)
            def _():
                line_start(d_moves[0][q])

    @pl.when(at_end)
    def _():
        ps_copies.start()

    own_rows = pl.ds(pl.multiple_of(c * half, half), half)
    wr_copy.wait_recv()
    for q in range(2):
        top, end = q * hrows, (q + 1) * hrows
        grad = dot_nt(d_all[me, top:end], wr_ref[own_rows, :]) + pas[c, top:end].astype(f32)
        dfx_copies[q].wait_recv()
        ng[c, top:end] = (grad + dot_nt(dfx[top:end], wr_peer[...])).astype(bf16)

        @pl.when(s > 0)
        def _():
            hop_copies[q].start()

    ng_copy.start()

    @pl.when(s == last)
    def _():
        prepare_first()

    gf[...] = jnp.zeros_like(gf)
    for b in range(blocks):
        rhs = ds[:, b * blk : (b + 1) * blk]
        for t in range(9):
            dense = jnp.where(same, dot_nn(ft[t, b], rhs), 0.0)
            folded = jnp.sum(dense.reshape(blk // gw, gw, blk), axis=0)
            for j in range(n):
                gf[j, t * k : (t + 1) * k, b * blk : (b + 1) * blk] = folded[j * k : (j + 1) * k]
    g_send[...] = gf[...].astype(bf16)
    g_copies = Spread(3, lambda to: g_send.at[to], g_recv.at[me], g_recv.at[peers])

    if n > 1:
        @pl.when(s == last)
        def _():
            for q in range(2):
                line_start(d_moves[0][q])

    def d_forward(step):
        for q in range(2):
            line_forward(d_moves[step][q], d_moves[step + 1][q])

    for step in range(n - 2):
        @pl.when(s == last)
        def _():
            sec_forward(step)
            if step == 0:
                bi_forward()

        d_forward(step)

        @pl.when(s == last)
        def _():
            if step == 0:
                g_copies.start()

        if step == 0:
            @pl.when(s < last)
            def _():
                bi_forward()

            ps_copies.wait_recv()
            ps_share.start()

            @pl.when((s < last) & at_end)
            def _():
                g_copies.start()

            ng_copy.wait_recv()
            grads_ref[:, :half] = ng[0]
            grads_ref[:, half:] = ng[1]
    @pl.when((s < last) & jnp.logical_not(at_end))
    def _():
        g_copies.start()

    for q in range(2):
        line_finish([step_moves[q] for step_moves in sec_moves])
    ps_share.wait_recv()
    expand = dot_tn(sec_all[...].reshape(n * rows, width), ps_all[...].reshape(n * rows, share))
    expand_ref[...] = expand * norm
    bi_share.wait_recv()

    def reduce_crop(q):
        line_finish([step_moves[q] for step_moves in d_moves])
        bi_rows = bi_all[:, q * hrows : (q + 1) * hrows].reshape(n * hrows, share)
        d_rows = d_all[:, q * hrows : (q + 1) * hrows].reshape(n * hrows, width)
        reduced = dot_tn(bi_rows, d_rows) * norm
        reduce_ref[...] = reduced if q == 0 else reduce_ref[...] + reduced

    reduce_crop(0)
    reduce_crop(1)
    g_copies.wait_recv()
    g_recv[me] = jnp.zeros(g_recv.shape[1:], bf16)
    total = gf[me]
    for j in range(n):
        total = total + g_recv[j].astype(f32)
    total = (total * norm)[: 9 * k]
    wide = jnp.broadcast_to(total[:, None, :], (9 * k, gw, width)).reshape(9 * k * gw, width)
    out_of = iota((9 * k * gw, width), 0) % gw == iota((9 * k * gw, width), 1) % gw
    wide = jnp.where(out_of, wide, 0.0)
    high = wide.astype(bf16)
    low = (wide - high.astype(f32)).astype(bf16)
    group_of = (iota((width, groups), 0) // gw == iota((width, groups), 1)).astype(f32).astype(bf16)
    group_ref[...] = dot_nn(high, group_of) + dot_nn(low, group_of)

    for move in [move for step_moves in sec_moves + d_moves for move in step_moves]:
        for copy, sends, _ in move:
            pl.when(sends)(copy.wait_send)
    for copy in [bi_share, ps_share, bi_copies, ps_copies, g_copies, wr_copy, ng_copy] + dfx_copies:
        copy.wait_send()

    @pl.when(counting)
    def _():
        for copies in cnt_copies:
            copies.wait_send()

    @pl.when(s > 0)
    def _():
        for copy in hop_copies:
            copy.wait_send()

    @pl.when(s < last)
    def _():
        for copy in fwd_copies:
            copy.wait_send()


def store_kernel(*refs):
    count = (len(refs) - 1) // 2
    copies = [pltpu.make_async_copy(refs[i], refs[count + i], refs[-1].at[i]) for i in range(count)]
    for copy in copies:
        copy.start()
    for copy in copies:
        copy.wait()


def on_device(
    block_inputs, out_pre, first_pre, second_pre, w_reduce, w_group, w_expand, w_lateral,
    teacher, top_grad, boxes, region_counts,
):
    n = lax.axis_size("dp")
    sections = lax.axis_size("section")
    crops, side, _, channels = top_grad.shape
    rows = crops * side * side
    width = first_pre.shape[4]
    lateral_width = w_lateral.shape[1]
    groups, gw = w_group.shape[2], w_group.shape[3]
    slots = boxes.shape[1]
    pixels = rows * n
    share = channels // n
    k = gw // n
    grows = -(-9 * k // 8) * 8
    half = channels // 2
    blk = min(256, width)
    hbm = pl.BlockSpec(memory_space=pltpu.HBM)
    vmem = pl.BlockSpec(memory_space=pltpu.VMEM)
    dma = pltpu.SemaphoreType.DMA
    peers = max(n - 1, 1)
    shapes = (
        ((rows, channels), bf16), ((share, width), f32),
        ((9 * k * gw, groups), f32), ((width, share), f32),
    )
    results = pl.pallas_call(
        functools.partial(kernel, (n, sections, crops, side, slots, pixels)),
        out_shape=tuple(pltpu.VMEM(shape, kind) for shape, kind in shapes),
        in_specs=[hbm] * 12,
        out_specs=(vmem,) * 4,
        scratch_shapes=[
            pltpu.SMEM((crops, 4, slots), jnp.int32),
            pltpu.SMEM((1, crops), jnp.int32),
            pltpu.VMEM((3, rows, channels), bf16),
            pltpu.VMEM((2, rows, width), bf16),
            pltpu.VMEM((channels, width), bf16),
            pltpu.VMEM((9 * gw * gw, groups), bf16),
            pltpu.VMEM((2, width, half), bf16),
            pltpu.VMEM((channels, lateral_width), bf16),
            pltpu.VMEM((rows, lateral_width), bf16),
            dma((11,)),
            pltpu.VMEM((2, rows, half), bf16),
            pltpu.VMEM((2, rows, half), bf16),
            pltpu.VMEM((half, width), bf16),
            pltpu.VMEM((rows, width), bf16),
            pltpu.VMEM((2, rows, half), bf16),
            pltpu.VMEM((rows, width), bf16),
            pltpu.VMEM((n, rows, width), bf16),
            pltpu.VMEM((n, rows, width), bf16),
            pltpu.VMEM((n, rows, share), bf16),
            pltpu.VMEM((n, rows, share), bf16),
            pltpu.VMEM((n, rows, share), bf16),
            pltpu.VMEM((n, rows, share), bf16),
            pltpu.VMEM((n, grows, width), f32),
            pltpu.VMEM((n, grows, width), bf16),
            pltpu.VMEM((n, grows, width), bf16),
            pltpu.VMEM((n, 8, 128), f32),
            pltpu.VMEM((9, width, blk), bf16),
            pltpu.VMEM((9, width // blk, blk, rows), bf16),
            dma((5,)), dma((4,)), dma((4,)), dma((4,)),
            dma((2,)), dma((2,)), dma((2,)), dma((2,)),
            dma((peers, 2, 2)), dma((peers, 2, 2)), dma((peers, 2, 2)), dma((peers, 2, 2)),
            dma((2,)), dma((2,)),
        ],
        compiler_params=pltpu.CompilerParams(
            collective_id=0, has_side_effects=True, vmem_limit_bytes=44 << 20,
        ),
    )(*(pltpu.with_memory_space_constraint(x, pltpu.HBM) for x in (
        boxes.transpose(0, 2, 1), region_counts.reshape(1, crops),
        block_inputs.reshape(rows, channels), out_pre.reshape(rows, channels),
        first_pre.reshape(rows, width), second_pre.reshape(rows, width),
        w_reduce[0], w_group[0].transpose(0, 2, 3, 1).reshape(9 * gw * gw, groups), w_expand[0], w_lateral,
        teacher.reshape(rows, lateral_width), top_grad.reshape(rows, channels),
    )))
    grads, reduced, group, expand = pl.pallas_call(
        store_kernel,
        out_shape=tuple(jax.ShapeDtypeStruct(shape, kind) for shape, kind in shapes),
        in_specs=[vmem] * 4,
        out_specs=(hbm,) * 4,
        scratch_shapes=[dma((4,))],
    )(*(pltpu.with_memory_space_constraint(x, pltpu.VMEM) for x in results))
    group = group.reshape(9, k, gw, groups).transpose(0, 3, 1, 2)
    return (
        grads.reshape(1, crops, side, side, channels), reduced[None], group[None], expand[None],
    )


def solution(mesh):
    return jax.shard_map(
        on_device,
        mesh=mesh,
        in_specs=(
            P("section", ("parts", "dp"), None, None, None),
            P("section", ("parts", "dp"), None, None, None),
            P("section", ("parts", "dp"), None, None, "chan"),
            P("section", ("parts", "dp"), None, None, "chan"),
            P("section", None, "chan"),
            P("section", None, "chan", None, None),
            P("section", "chan", None),
            P(),
            P(("parts", "dp"), None, None, None),
            P(("parts", "dp"), None, None, None),
            P(("parts", "dp"), None, None),
            P(("parts", "dp")),
        ),
        out_specs=(
            P("section", ("parts", "dp"), None, None, None),
            P(("parts", "section"), "dp", "chan"),
            P(("parts", "section"), None, "chan", "dp", None),
            P(("parts", "section"), "chan", "dp"),
        ),
        check_vma=False,
    )
```

```python
import functools
import math

import jax
import jax.numpy as jnp
from jax import lax
from jax.experimental import pallas as pl
from jax.experimental.pallas import tpu as pltpu
from jax.sharding import PartitionSpec as P

imitation_weight = 0.5
tap_offsets = [(tap // 3 - 1, tap % 3 - 1) for tap in range(9)]
f32 = jnp.float32
bf16 = jnp.bfloat16


def dot_nn(a, b):
    return lax.dot_general(a, b, (((1,), (0,)), ((), ())), preferred_element_type=f32)


def dot_nt(a, b):
    return lax.dot_general(a, b, (((1,), (1,)), ((), ())), preferred_element_type=f32)


def dot_tn(a, b):
    return lax.dot_general(a, b, (((0,), (0,)), ((), ())), preferred_element_type=f32)


def kernel(
    dims,
    boxes_hbm, counts_hbm, bi_hbm, out_hbm, first_hbm, second_hbm, wr_hbm, wg_hbm, we_hbm,
    wl_hbm, teacher_hbm, top_hbm,
    grads_ref, reduce_ref, group_ref, expand_ref,
    boxes_ref, counts_ref,
    full_ref, part_ref, wr_ref, wg_ref, we_ref, wl_ref, teacher_ref, load_sem,
    inc, pas, wr_peer, dfx, ng, ds, d_all, sec_all, bi_send, bi_all, ps_send, ps_all,
    gf, g_send, g_recv, g_far, far_recv, cnt, taps, ft,
    dp_send, dp_recv, core_send, core_recv, hop_send, hop_recv, fwd_send, fwd_recv,
    sec_send, sec_recv, d_send, d_recv, share_send, share_recv,
):
    n, sections, crops, side, slots, pixels = dims
    out_ref, bi_ref, top_ref = (full_ref.at[i] for i in range(3))
    first_ref, second_ref = part_ref.at[0], part_ref.at[1]
    rows, channels = bi_ref.shape
    half = channels // 2
    width = first_ref.shape[1]
    groups = wg_ref.shape[1]
    gw = width // groups
    blk = taps.shape[2]
    blocks = width // blk
    cells = side * side
    share = channels // n
    k = gw // n
    hrows = rows // 2
    me = lax.axis_index("dp")
    s = lax.axis_index("section")
    c = lax.axis_index("chan")
    other = 1 - c
    last = sections - 1
    norm = 1.0 / math.sqrt(pixels)

    def remote(src, dst, send, recv, where):
        return pltpu.make_async_remote_copy(
            src_ref=src, dst_ref=dst, send_sem=send, recv_sem=recv,
            device_id=where, device_id_type=pl.DeviceIdType.MESH,
        )

    class Spread:
        def __init__(self, what, src_of, dst, moved, at=None, where={}):
            at = what if at is None else at
            self.copies = [
                remote(src_of(to), dst, dp_send.at[at], dp_recv.at[what], {"dp": to, **where})
                for to in (lax.rem(me + step, n) for step in range(1, n))
            ]
            self.sent = pltpu.make_async_copy(moved, moved, dp_send.at[at])
            self.received = pltpu.make_async_copy(moved, moved, dp_recv.at[what])

        def start(self):
            for copy in self.copies:
                copy.start()

        def wait_recv(self):
            self.received.wait()

        def wait_send(self):
            self.sent.wait()

    mine = pl.ds(pl.multiple_of(c * hrows, hrows), hrows)
    peers = pl.ds(0, n - 1)
    crop_rows = [pl.ds(q * hrows, hrows) for q in range(2)]

    def share_copy(which, buf):
        return remote(buf.at[:, mine], buf.at[:, mine], share_send.at[which],
                      share_recv.at[which], {"chan": other})

    def line(step, block, send, recv):
        ahead = block(lax.max(me - step, 0))
        behind = block(lax.min(me + step, n - 1))
        right = remote(ahead, ahead, send.at[0], recv.at[0], {"dp": lax.min(me + 1, n - 1)})
        left = remote(behind, behind, send.at[1], recv.at[1], {"dp": lax.max(me - 1, 0)})
        return (
            (right, (me - step >= 0) & (me + 1 < n), me - 1 - step >= 0),
            (left, (me + step < n) & (me >= 1), me + 1 + step < n),
        )

    def line_start(moves):
        for copy, sends, _ in moves:
            pl.when(sends)(copy.start)

    def line_forward(moves, following):
        for (copy, _, receives), (onward, sends, _) in zip(moves, following):
            @pl.when(receives & sends)
            def _():
                copy.wait_recv()
                onward.start()

    def line_settle(moves, following):
        for (copy, _, receives), (_, sends, _) in zip(moves, following):
            pl.when(receives & jnp.logical_not(sends))(copy.wait_recv)

    def line_finish(moves):
        for step in range(n - 1):
            if step == n - 2:
                for copy, _, receives in moves[step]:
                    pl.when(receives)(copy.wait_recv)
            else:
                line_settle(moves[step], moves[step + 1])

    barrier = pltpu.get_barrier_semaphore()
    mesh_type = pl.DeviceIdType.MESH
    for step in range(1, n):
        pl.semaphore_signal(barrier, inc=1, device_id={"dp": lax.rem(me + step, n)},
                            device_id_type=mesh_type)
    pl.semaphore_signal(barrier, inc=1, device_id={"chan": other}, device_id_type=mesh_type)

    @pl.when((s == last) & (c == 0))
    def _():
        for step in range(1, n):
            pl.semaphore_signal(barrier, inc=1, device_id_type=mesh_type,
                                device_id={"dp": lax.rem(me + step, n), "chan": other})

    @pl.when(s > 0)
    def _():
        pl.semaphore_signal(barrier, inc=1, device_id={"section": s - 1},
                            device_id_type=mesh_type)

    @pl.when(s < last)
    def _():
        pl.semaphore_signal(barrier, inc=1, device_id={"section": s + 1},
                            device_id_type=mesh_type)

    pairs = (
        ("boxes", boxes_hbm, boxes_ref), ("counts", counts_hbm, counts_ref),
        ("second", second_hbm, second_ref), ("pair", out_hbm, out_ref), ("wl", wl_hbm, wl_ref),
        ("teacher", teacher_hbm, teacher_ref), ("pair", bi_hbm, bi_ref),
        ("wg", wg_hbm, wg_ref), ("top", top_hbm, top_ref), ("we", we_hbm.at[:, :half], we_ref.at[0]),
        ("we", we_hbm.at[:, half:], we_ref.at[1]), ("first", first_hbm, first_ref),
        ("wr", wr_hbm, wr_ref),
    )
    whole = {
        "boxes": boxes_ref, "counts": counts_ref, "pair": full_ref.at[0:2], "top": top_ref,
        "first": first_ref, "second": second_ref, "wl": wl_ref, "teacher": teacher_ref,
        "wg": wg_ref, "we": we_ref, "wr": wr_ref,
    }
    load_at = {name: load_sem.at[i] for i, name in enumerate(whole)}

    def load_start(some):
        for name, a, b in some:
            pltpu.make_async_copy(a, b, load_at[name]).start()

    def loaded(*names):
        for name in names:
            pltpu.make_async_copy(whole[name], whole[name], load_at[name]).wait()

    counting = (s == last) & (c == 1)
    at_end = (me == 0) | (me == n - 1)
    load_start(pairs[:8])

    @pl.when(jnp.logical_not(counting))
    def _():
        load_start(pairs[8:])

    loaded("boxes", "counts")
    row = lax.broadcasted_iota(jnp.int32, (cells, 128), 0)
    row_h, row_w = row // side, row % side
    masks = []
    for crop in range(crops):
        inside = jnp.zeros((cells, 128), f32)
        for r in range(slots):
            hit = ((row_h >= boxes_ref[crop, 0, r]) & (row_h < boxes_ref[crop, 1, r])
                   & (row_w >= boxes_ref[crop, 2, r]) & (row_w < boxes_ref[crop, 3, r])
                   & (counts_ref[0, crop] > r))
            inside = jnp.where(hit, 1.0, inside)
        masks.append(inside)
    mask = jnp.concatenate(masks, axis=0)
    cnt[me] = jnp.broadcast_to(jnp.sum(mask, axis=0, keepdims=True), (8, 128))

    pl.semaphore_wait(barrier, n + jnp.where(s > 0, 1, 0) + jnp.where(s < last, 1, 0)
                      + jnp.where(counting, n - 1, 0))

    cnt_copies = [Spread(0, lambda to: cnt.at[me], cnt.at[me], cnt.at[peers], at, {"chan": core})
                  for core, at in ((0, 0), (1, 4))]

    @pl.when(counting)
    def _():
        for copies in cnt_copies:
            copies.start()
        load_start(pairs[8:])

    wr_copy = remote(wr_ref.at[pl.ds(pl.multiple_of(other * half, half), half)], wr_peer,
                     core_send.at[0], core_recv.at[0], {"chan": other})
    loaded("second")
    sec_all[me] = jnp.maximum(second_ref[...], 0)
    sec_moves = [[line(step, lambda j, q=q: sec_all.at[j, pl.ds(q * hrows, hrows)],
                       sec_send.at[step, q], sec_recv.at[step, q])
                  for q in range(2)] for step in range(n - 1)]
    if n > 1:
        for q in range(2):
            line_start(sec_moves[0][q])
    loaded("pair")
    for j in range(n):
        bi_send[j] = bi_ref[:, j * share : (j + 1) * share]
    bi_all[me, mine] = bi_send[me, mine]

    bi_copies = Spread(1, lambda to: bi_send.at[to, mine], bi_all.at[me, mine],
                       bi_all.at[peers, mine])
    bi_share = share_copy(0, bi_all)

    def sec_forward(step):
        for q in range(2):
            line_forward(sec_moves[step][q], sec_moves[step + 1][q])

    def bi_forward():
        bi_copies.wait_recv()
        bi_share.start()

    pair = gw * gw
    iota = lambda shape, dim: lax.broadcasted_iota(jnp.int32, shape, dim)
    same = iota((blk, blk), 0) // gw == iota((blk, blk), 1) // gw

    def build_taps():
        same_out = iota((width, pair), 0) % gw == iota((width, pair), 1) % gw
        spread = (iota((pair, blk), 0) // gw == iota((pair, blk), 1) % gw).astype(f32).astype(bf16)
        inside = iota((width, blk), 0) // gw % (blk // gw) == iota((width, blk), 1) // gw
        by_group = wg_ref[...].astype(f32).T
        for t in range(9):
            values = by_group[:, t * pair : (t + 1) * pair]
            values = jnp.broadcast_to(values[:, None, :], (groups, gw, pair)).reshape(width, pair)
            values = jnp.where(same_out, values, 0.0).astype(bf16)
            taps[t] = jnp.where(inside, dot_nn(values, spread), 0.0).astype(bf16)

    def shifter(count):
        prow = lax.broadcasted_iota(jnp.int32, (count, blk), 0)
        p_w = prow % side
        p_h = (prow // side) % side

        def moved(x, a, b):
            shift = (side * a + b) % count
            if shift:
                x = pltpu.roll(x, shift, 0)
            if a:
                x = jnp.where(p_h >= 1 if a == 1 else p_h < side - 1, x, 0.0)
            if b:
                x = jnp.where(p_w >= 1 if b == 1 else p_w < side - 1, x, 0.0)
            return x

        return moved

    def prepare_first():
        moved = shifter(rows)
        for b in range(blocks):
            first = jnp.maximum(first_ref[:, b * blk : (b + 1) * blk], 0).astype(f32)
            for t, (da, db) in enumerate(tap_offsets):
                ft[t, b] = moved(first, -da, -db).T.astype(bf16)

    hop_copies = [
        remote(ng.at[c, crop_rows[q]], inc.at[c, crop_rows[q]],
               hop_send.at[q], hop_recv.at[q], {"section": lax.max(s - 1, 0)})
        for q in range(2)
    ]
    fwd_copies = [
        remote(inc.at[c, crop_rows[q]], inc.at[c, crop_rows[q]],
               fwd_send.at[q], fwd_recv.at[q], {"chan": other})
        for q in range(2)
    ]

    @pl.when(s == last)
    def _():
        loaded("wl", "teacher")
        feature = jnp.maximum(out_ref[...], 0)
        lateral = dot_nn(feature, wl_ref[...])
        error = (mask[:, 0:1] * (lateral - teacher_ref[...].astype(f32))).astype(bf16)
        imitation = dot_nt(error, wl_ref[...])
        loaded("wg")
        build_taps()
        loaded("top", "first", "we", "wr")
        wr_copy.start()
        cnt_copies[0].wait_recv()
        bi_copies.start()
        covered = cnt[0]
        for j in range(1, n):
            covered = covered + cnt[j]
        scale = (imitation_weight * pixels) / covered[0:1, 0:1]
        start = (top_ref[...].astype(f32) + imitation * scale).astype(bf16)
        start = jnp.where(out_ref[...] > 0, start, jnp.zeros_like(start))
        pas[0] = start[:, :half]
        pas[1] = start[:, half:]

    @pl.when(s < last)
    def _():
        loaded("wl", "teacher", "wg", "top", "first", "we", "wr")
        wr_copy.start()
        build_taps()
        prepare_first()
        for step in range(n - 2):
            sec_forward(step)
        pl.when(jnp.logical_not(at_end))(bi_copies.start)

    ps_copies = Spread(2, lambda to: ps_send.at[to, mine], ps_all.at[me, mine],
                       ps_all.at[peers, mine])
    ps_share = share_copy(1, ps_all)
    d_moves = [[line(step, lambda j, q=q: d_all.at[j, crop_rows[q]], d_send.at[step, q],
                     d_recv.at[step, q]) for q in range(2)] for step in range(n - 1)]
    dfx_copies = [remote(d_all.at[me, crop_rows[q]], dfx.at[crop_rows[q]], core_send.at[1 + q],
                         core_recv.at[1 + q], {"chan": other}) for q in range(2)]
    ng_copy = remote(ng.at[c], ng.at[c], core_send.at[3], core_recv.at[3], {"chan": other})

    def gate_half(h, q):
        at = pl.ds(pl.multiple_of(h * half, half), half)
        value = inc[h, crop_rows[q]]
        gate = out_ref[q * hrows : (q + 1) * hrows, at] > 0
        pas[h, crop_rows[q]] = jnp.where(gate, value, jnp.zeros_like(value))

    def own_arrives(q, where=None):
        @pl.when((s < last) & where if where is not None else s < last)
        def _():
            hop_copies[q].wait_recv()
            fwd_copies[q].start()
            if q == 0:
                pl.when(at_end)(bi_copies.start)
            gate_half(c, q)

    def other_arrives(q):
        @pl.when(s < last)
        def _():
            fwd_copies[q].wait_recv()
            gate_half(other, q)

    moved = shifter(hrows)
    own_arrives(0)
    for q in range(2):
        top, end = q * hrows, (q + 1) * hrows
        second_full = dot_nt(pas[c, top:end], we_ref[c])
        if q == 0:
            own_arrives(1, c == 1)
        other_arrives(q)
        for j in range(n):
            at = (j * share) // half
            ps_send[j, top:end] = pas[at, top:end, j * share - at * half : (j + 1) * share - at * half]

        @pl.when(c == q)
        def _():
            ps_all[me, top:end] = ps_send[me, top:end]
            pl.when(jnp.logical_not(at_end))(ps_copies.start)

        second_full = second_full + dot_nt(pas[other, top:end], we_ref[other])
        for b in range(blocks):
            lo, hi = b * blk, (b + 1) * blk
            lhs = jnp.where(second_ref[top:end, lo:hi] > 0, second_full[:, lo:hi], 0.0).astype(bf16)
            ds[top:end, lo:hi] = lhs
            total = None
            for db in (-1, 0, 1):
                column = None
                for da in (-1, 0, 1):
                    t = 3 * (da + 1) + db + 1
                    y = moved(dot_nn(lhs, taps[t, lo:hi, :]), da, 0)
                    column = y if column is None else column + y
                column = moved(column, 0, db)
                total = column if total is None else total + column
            d_all[me, top:end, lo:hi] = jnp.where(
                first_ref[top:end, lo:hi] > 0, total, 0.0).astype(bf16)
            if q == 0 and b == 0:
                own_arrives(1, c == 0)
        dfx_copies[q].start()
        if n > 1:
            @pl.when(s < last)
            def _():
                line_start(d_moves[0][q])

    @pl.when(at_end)
    def _():
        ps_copies.start()

    own_rows = pl.ds(pl.multiple_of(c * half, half), half)
    wr_copy.wait_recv()
    for q in range(2):
        top, end = q * hrows, (q + 1) * hrows
        grad = dot_nt(d_all[me, top:end], wr_ref[own_rows, :]) + pas[c, top:end].astype(f32)
        dfx_copies[q].wait_recv()
        ng[c, top:end] = (grad + dot_nt(dfx[top:end], wr_peer[...])).astype(bf16)

        @pl.when(s > 0)
        def _():
            hop_copies[q].start()

    ng_copy.start()

    @pl.when(s == last)
    def _():
        prepare_first()

    gf[...] = jnp.zeros_like(gf)
    for b in range(blocks):
        rhs = ds[:, b * blk : (b + 1) * blk]
        for t in range(9):
            dense = jnp.where(same, dot_nn(ft[t, b], rhs), 0.0)
            folded = jnp.sum(dense.reshape(blk // gw, gw, blk), axis=0)
            for j in range(n):
                gf[j, t * k : (t + 1) * k, b * blk : (b + 1) * blk] = folded[j * k : (j + 1) * k]
    g_send[...] = gf[...].astype(bf16)
    def g_copy(part, dst, recv, where):
        return remote(g_send.at[part], dst, dp_send.at[3], recv, {"dp": where})

    relayed = n > 3
    ends = ((0, 1, me >= 2), (n - 1, n - 2, me <= n - 3))

    def g_start():
        for step in range(1, n):
            to = lax.rem(me + step, n)
            direct = (to != 0) & (to != n - 1) if relayed else to >= 0

            @pl.when(direct)
            def _():
                g_copy(to, g_recv.at[me], dp_recv.at[3], to).start()

        if relayed:
            for i, (end, by, far) in enumerate(ends):
                @pl.when(far)
                def _():
                    g_copy(end, g_far.at[i, me], far_recv.at[i], by).start()

    def g_relay():
        for i, (end, by, _) in enumerate(ends):
            @pl.when(me == by)
            def _():
                others = pl.ds(2 if end == 0 else 0, n - 2)
                arrived = g_far.at[i, others]
                pltpu.make_async_copy(arrived, arrived, far_recv.at[i]).wait()
                total = gf[end]
                for j in range(n - 2):
                    total = total + g_far[i, j + (2 if end == 0 else 0)].astype(f32)
                g_send[end] = total.astype(bf16)
                g_copy(end, g_recv.at[me], dp_recv.at[3], end).start()

    def g_wait(sem, count):
        some = g_recv.at[pl.ds(0, count)]
        pltpu.make_async_copy(some, some, sem).wait()

    if n > 1:
        @pl.when(s == last)
        def _():
            for q in range(2):
                line_start(d_moves[0][q])

    def d_forward(step):
        for q in range(2):
            line_forward(d_moves[step][q], d_moves[step + 1][q])

    for step in range(n - 2):
        @pl.when(s == last)
        def _():
            sec_forward(step)
            if step == 0:
                bi_forward()

        d_forward(step)

        @pl.when(s == last)
        def _():
            if step == 0:
                g_start()

        if step == 0:
            @pl.when(s < last)
            def _():
                bi_forward()

            ps_copies.wait_recv()
            ps_share.start()

            @pl.when((s < last) & at_end)
            def _():
                g_start()

            ng_copy.wait_recv()
            grads_ref[:, :half] = ng[0]
            grads_ref[:, half:] = ng[1]
    @pl.when((s < last) & jnp.logical_not(at_end))
    def _():
        g_start()

    if relayed:
        g_relay()

    for q in range(2):
        line_finish([step_moves[q] for step_moves in sec_moves])
    ps_share.wait_recv()
    expand = dot_tn(sec_all[...].reshape(n * rows, width), ps_all[...].reshape(n * rows, share))
    expand_ref[...] = expand * norm
    bi_share.wait_recv()

    def reduce_crop(q):
        line_finish([step_moves[q] for step_moves in d_moves])
        bi_rows = bi_all[:, q * hrows : (q + 1) * hrows].reshape(n * hrows, share)
        d_rows = d_all[:, q * hrows : (q + 1) * hrows].reshape(n * hrows, width)
        reduced = dot_tn(bi_rows, d_rows) * norm
        reduce_ref[...] = reduced if q == 0 else reduce_ref[...] + reduced

    reduce_crop(0)
    reduce_crop(1)
    if relayed:
        @pl.when(at_end)
        def _():
            for j in range(n):
                if 0 < j < n - 1:
                    @pl.when((me == 0) & (j != 1) | (me == n - 1) & (j != n - 2))
                    def _():
                        g_recv[j] = jnp.zeros(g_recv.shape[1:], bf16)
                else:
                    g_recv[j] = jnp.zeros(g_recv.shape[1:], bf16)
            g_wait(dp_recv.at[3], 1)

        @pl.when(jnp.logical_not(at_end))
        def _():
            g_recv[me] = jnp.zeros(g_recv.shape[1:], bf16)
            g_wait(dp_recv.at[3], n - 1)
    else:
        g_recv[me] = jnp.zeros(g_recv.shape[1:], bf16)
        g_wait(dp_recv.at[3], n - 1)
    total = gf[me]
    for j in range(n):
        total = total + g_recv[j].astype(f32)
    total = (total * norm)[: 9 * k]
    wide = jnp.broadcast_to(total[:, None, :], (9 * k, gw, width)).reshape(9 * k * gw, width)
    out_of = iota((9 * k * gw, width), 0) % gw == iota((9 * k * gw, width), 1) % gw
    wide = jnp.where(out_of, wide, 0.0)
    high = wide.astype(bf16)
    low = (wide - high.astype(f32)).astype(bf16)
    group_of = (iota((width, groups), 0) // gw == iota((width, groups), 1)).astype(f32).astype(bf16)
    group_ref[...] = dot_nn(high, group_of) + dot_nn(low, group_of)

    for move in [move for step_moves in sec_moves + d_moves for move in step_moves]:
        for copy, sends, _ in move:
            pl.when(sends)(copy.wait_send)
    g_wait(dp_send.at[3], n - 1)
    for copy in [bi_share, ps_share, bi_copies, ps_copies, wr_copy, ng_copy] + dfx_copies:
        copy.wait_send()

    @pl.when(counting)
    def _():
        for copies in cnt_copies:
            copies.wait_send()

    @pl.when(s > 0)
    def _():
        for copy in hop_copies:
            copy.wait_send()

    @pl.when(s < last)
    def _():
        for copy in fwd_copies:
            copy.wait_send()


def store_kernel(*refs):
    count = (len(refs) - 1) // 2
    copies = [pltpu.make_async_copy(refs[i], refs[count + i], refs[-1].at[i]) for i in range(count)]
    for copy in copies:
        copy.start()
    for copy in copies:
        copy.wait()


def on_device(
    block_inputs, out_pre, first_pre, second_pre, w_reduce, w_group, w_expand, w_lateral,
    teacher, top_grad, boxes, region_counts,
):
    n = lax.axis_size("dp")
    sections = lax.axis_size("section")
    crops, side, _, channels = top_grad.shape
    rows = crops * side * side
    width = first_pre.shape[4]
    lateral_width = w_lateral.shape[1]
    groups, gw = w_group.shape[2], w_group.shape[3]
    slots = boxes.shape[1]
    pixels = rows * n
    share = channels // n
    k = gw // n
    grows = -(-9 * k // 8) * 8
    half = channels // 2
    blk = min(256, width)
    hbm = pl.BlockSpec(memory_space=pltpu.HBM)
    vmem = pl.BlockSpec(memory_space=pltpu.VMEM)
    dma = pltpu.SemaphoreType.DMA
    peers = max(n - 1, 1)
    shapes = (
        ((rows, channels), bf16), ((share, width), f32),
        ((9 * k * gw, groups), f32), ((width, share), f32),
    )
    results = pl.pallas_call(
        functools.partial(kernel, (n, sections, crops, side, slots, pixels)),
        out_shape=tuple(pltpu.VMEM(shape, kind) for shape, kind in shapes),
        in_specs=[hbm] * 12,
        out_specs=(vmem,) * 4,
        scratch_shapes=[
            pltpu.SMEM((crops, 4, slots), jnp.int32),
            pltpu.SMEM((1, crops), jnp.int32),
            pltpu.VMEM((3, rows, channels), bf16),
            pltpu.VMEM((2, rows, width), bf16),
            pltpu.VMEM((channels, width), bf16),
            pltpu.VMEM((9 * gw * gw, groups), bf16),
            pltpu.VMEM((2, width, half), bf16),
            pltpu.VMEM((channels, lateral_width), bf16),
            pltpu.VMEM((rows, lateral_width), bf16),
            dma((11,)),
            pltpu.VMEM((2, rows, half), bf16),
            pltpu.VMEM((2, rows, half), bf16),
            pltpu.VMEM((half, width), bf16),
            pltpu.VMEM((rows, width), bf16),
            pltpu.VMEM((2, rows, half), bf16),
            pltpu.VMEM((rows, width), bf16),
            pltpu.VMEM((n, rows, width), bf16),
            pltpu.VMEM((n, rows, width), bf16),
            pltpu.VMEM((n, rows, share), bf16),
            pltpu.VMEM((n, rows, share), bf16),
            pltpu.VMEM((n, rows, share), bf16),
            pltpu.VMEM((n, rows, share), bf16),
            pltpu.VMEM((n, grows, width), f32),
            pltpu.VMEM((n, grows, width), bf16),
            pltpu.VMEM((n, grows, width), bf16),
            pltpu.VMEM((2, n, grows, width), bf16),
            dma((2,)),
            pltpu.VMEM((n, 8, 128), f32),
            pltpu.VMEM((9, width, blk), bf16),
            pltpu.VMEM((9, width // blk, blk, rows), bf16),
            dma((5,)), dma((4,)), dma((4,)), dma((4,)),
            dma((2,)), dma((2,)), dma((2,)), dma((2,)),
            dma((peers, 2, 2)), dma((peers, 2, 2)), dma((peers, 2, 2)), dma((peers, 2, 2)),
            dma((2,)), dma((2,)),
        ],
        compiler_params=pltpu.CompilerParams(
            collective_id=0, has_side_effects=True, vmem_limit_bytes=44 << 20,
        ),
    )(*(pltpu.with_memory_space_constraint(x, pltpu.HBM) for x in (
        boxes.transpose(0, 2, 1), region_counts.reshape(1, crops),
        block_inputs.reshape(rows, channels), out_pre.reshape(rows, channels),
        first_pre.reshape(rows, width), second_pre.reshape(rows, width),
        w_reduce[0], w_group[0].transpose(0, 2, 3, 1).reshape(9 * gw * gw, groups), w_expand[0], w_lateral,
        teacher.reshape(rows, lateral_width), top_grad.reshape(rows, channels),
    )))
    grads, reduced, group, expand = pl.pallas_call(
        store_kernel,
        out_shape=tuple(jax.ShapeDtypeStruct(shape, kind) for shape, kind in shapes),
        in_specs=[vmem] * 4,
        out_specs=(hbm,) * 4,
        scratch_shapes=[dma((4,))],
    )(*(pltpu.with_memory_space_constraint(x, pltpu.VMEM) for x in results))
    group = group.reshape(9, k, gw, groups).transpose(0, 3, 1, 2)
    return (
        grads.reshape(1, crops, side, side, channels), reduced[None], group[None], expand[None],
    )


def solution(mesh):
    return jax.shard_map(
        on_device,
        mesh=mesh,
        in_specs=(
            P("section", ("parts", "dp"), None, None, None),
            P("section", ("parts", "dp"), None, None, None),
            P("section", ("parts", "dp"), None, None, "chan"),
            P("section", ("parts", "dp"), None, None, "chan"),
            P("section", None, "chan"),
            P("section", None, "chan", None, None),
            P("section", "chan", None),
            P(),
            P(("parts", "dp"), None, None, None),
            P(("parts", "dp"), None, None, None),
            P(("parts", "dp"), None, None),
            P(("parts", "dp")),
        ),
        out_specs=(
            P("section", ("parts", "dp"), None, None, None),
            P(("parts", "section"), "dp", "chan"),
            P(("parts", "section"), None, "chan", "dp", None),
            P(("parts", "section"), "chan", "dp"),
        ),
        check_vma=False,
    )
```

```python
import functools
import math

import jax
import jax.numpy as jnp
from jax import lax
from jax.experimental import pallas as pl
from jax.experimental.pallas import tpu as pltpu
from jax.sharding import PartitionSpec as P

imitation_weight = 0.5
tap_offsets = [(tap // 3 - 1, tap % 3 - 1) for tap in range(9)]
f32 = jnp.float32
bf16 = jnp.bfloat16


def dot_nn(a, b):
    return lax.dot_general(a, b, (((1,), (0,)), ((), ())), preferred_element_type=f32)


def dot_nt(a, b):
    return lax.dot_general(a, b, (((1,), (1,)), ((), ())), preferred_element_type=f32)


def dot_tn(a, b):
    return lax.dot_general(a, b, (((0,), (0,)), ((), ())), preferred_element_type=f32)


def kernel(
    dims,
    boxes_hbm, counts_hbm, bi_hbm, out_hbm, first_hbm, second_hbm, wr_hbm, wg_hbm, we_hbm,
    wl_hbm, teacher_hbm, top_hbm,
    grads_ref, reduce_ref, group_ref, expand_ref,
    boxes_ref, counts_ref,
    full_ref, part_ref, wr_ref, wg_ref, we_ref, wl_ref, teacher_ref, load_sem,
    inc, pas, wr_peer, dfx, ng, ds, d_all, sec_all, bi_send, bi_all, ps_send, ps_all,
    gf, g_send, g_recv, g_far, far_recv, cnt, taps, ft,
    dp_send, dp_recv, core_send, core_recv, hop_send, hop_recv, fwd_send, fwd_recv,
    sec_send, sec_recv, d_send, d_recv, share_send, share_recv,
):
    n, sections, crops, side, slots, pixels = dims
    out_ref, bi_ref, top_ref = (full_ref.at[i] for i in range(3))
    first_ref, second_ref = part_ref.at[0], part_ref.at[1]
    rows, channels = bi_ref.shape
    half = channels // 2
    width = first_ref.shape[1]
    groups = wg_ref.shape[1]
    gw = width // groups
    blk = taps.shape[2]
    blocks = width // blk
    cells = side * side
    share = channels // n
    k = gw // n
    hrows = rows // 2
    me = lax.axis_index("dp")
    s = lax.axis_index("section")
    c = lax.axis_index("chan")
    other = 1 - c
    last = sections - 1
    norm = 1.0 / math.sqrt(pixels)

    def remote(src, dst, send, recv, where):
        return pltpu.make_async_remote_copy(
            src_ref=src, dst_ref=dst, send_sem=send, recv_sem=recv,
            device_id=where, device_id_type=pl.DeviceIdType.MESH,
        )

    class Spread:
        def __init__(self, what, src_of, dst, moved, at=None, where={}):
            at = what if at is None else at
            self.copies = [
                remote(src_of(to), dst, dp_send.at[at], dp_recv.at[what], {"dp": to, **where})
                for to in (lax.rem(me + step, n) for step in range(1, n))
            ]
            self.sent = pltpu.make_async_copy(moved, moved, dp_send.at[at])
            self.received = pltpu.make_async_copy(moved, moved, dp_recv.at[what])

        def start(self):
            for copy in self.copies:
                copy.start()

        def wait_recv(self):
            self.received.wait()

        def wait_send(self):
            self.sent.wait()

    mine = pl.ds(pl.multiple_of(c * hrows, hrows), hrows)
    peers = pl.ds(0, n - 1)
    crop_rows = [pl.ds(q * hrows, hrows) for q in range(2)]

    def share_copy(which, buf):
        return remote(buf.at[:, mine], buf.at[:, mine], share_send.at[which],
                      share_recv.at[which], {"chan": other})

    def line(step, block, send, recv):
        ahead = block(lax.max(me - step, 0))
        behind = block(lax.min(me + step, n - 1))
        right = remote(ahead, ahead, send.at[0], recv.at[0], {"dp": lax.min(me + 1, n - 1)})
        left = remote(behind, behind, send.at[1], recv.at[1], {"dp": lax.max(me - 1, 0)})
        return (
            (right, (me - step >= 0) & (me + 1 < n), me - 1 - step >= 0),
            (left, (me + step < n) & (me >= 1), me + 1 + step < n),
        )

    def line_start(moves):
        for copy, sends, _ in moves:
            pl.when(sends)(copy.start)

    def line_forward(moves, following):
        for (copy, _, receives), (onward, sends, _) in zip(moves, following):
            @pl.when(receives & sends)
            def _():
                copy.wait_recv()
                onward.start()

    def line_settle(moves, following):
        for (copy, _, receives), (_, sends, _) in zip(moves, following):
            pl.when(receives & jnp.logical_not(sends))(copy.wait_recv)

    def line_finish(moves):
        for step in range(n - 1):
            if step == n - 2:
                for copy, _, receives in moves[step]:
                    pl.when(receives)(copy.wait_recv)
            else:
                line_settle(moves[step], moves[step + 1])

    barrier = pltpu.get_barrier_semaphore()
    mesh_type = pl.DeviceIdType.MESH
    for step in range(1, n):
        pl.semaphore_signal(barrier, inc=1, device_id={"dp": lax.rem(me + step, n)},
                            device_id_type=mesh_type)
    pl.semaphore_signal(barrier, inc=1, device_id={"chan": other}, device_id_type=mesh_type)

    @pl.when((s == last) & (c == 0))
    def _():
        for step in range(1, n):
            pl.semaphore_signal(barrier, inc=1, device_id_type=mesh_type,
                                device_id={"dp": lax.rem(me + step, n), "chan": other})

    @pl.when(s > 0)
    def _():
        pl.semaphore_signal(barrier, inc=1, device_id={"section": s - 1},
                            device_id_type=mesh_type)

    @pl.when(s < last)
    def _():
        pl.semaphore_signal(barrier, inc=1, device_id={"section": s + 1},
                            device_id_type=mesh_type)

    pairs = (
        ("boxes", boxes_hbm, boxes_ref), ("counts", counts_hbm, counts_ref),
        ("second", second_hbm, second_ref), ("pair", out_hbm, out_ref), ("wl", wl_hbm, wl_ref),
        ("teacher", teacher_hbm, teacher_ref), ("pair", bi_hbm, bi_ref),
        ("wg", wg_hbm, wg_ref), ("top", top_hbm, top_ref), ("we", we_hbm.at[:, :half], we_ref.at[0]),
        ("we", we_hbm.at[:, half:], we_ref.at[1]), ("first", first_hbm, first_ref),
        ("wr", wr_hbm, wr_ref),
    )
    whole = {
        "boxes": boxes_ref, "counts": counts_ref, "pair": full_ref.at[0:2], "top": top_ref,
        "first": first_ref, "second": second_ref, "wl": wl_ref, "teacher": teacher_ref,
        "wg": wg_ref, "we": we_ref, "wr": wr_ref,
    }
    load_at = {name: load_sem.at[i] for i, name in enumerate(whole)}

    def load_start(some):
        for name, a, b in some:
            pltpu.make_async_copy(a, b, load_at[name]).start()

    def loaded(*names):
        for name in names:
            pltpu.make_async_copy(whole[name], whole[name], load_at[name]).wait()

    counting = (s == last) & (c == 1)
    at_end = (me == 0) | (me == n - 1)
    load_start(pairs[:8])

    @pl.when(jnp.logical_not(counting))
    def _():
        load_start(pairs[8:])

    loaded("boxes", "counts")
    row = lax.broadcasted_iota(jnp.int32, (cells, 128), 0)
    row_h, row_w = row // side, row % side
    masks = []
    for crop in range(crops):
        inside = jnp.zeros((cells, 128), f32)
        for r in range(slots):
            hit = ((row_h >= boxes_ref[crop, 0, r]) & (row_h < boxes_ref[crop, 1, r])
                   & (row_w >= boxes_ref[crop, 2, r]) & (row_w < boxes_ref[crop, 3, r])
                   & (counts_ref[0, crop] > r))
            inside = jnp.where(hit, 1.0, inside)
        masks.append(inside)
    mask = jnp.concatenate(masks, axis=0)
    cnt[me] = jnp.broadcast_to(jnp.sum(mask, axis=0, keepdims=True), (8, 128))

    pl.semaphore_wait(barrier, n + jnp.where(s > 0, 1, 0) + jnp.where(s < last, 1, 0)
                      + jnp.where(counting, n - 1, 0))

    cnt_copies = [Spread(0, lambda to: cnt.at[me], cnt.at[me], cnt.at[peers], at, {"chan": core})
                  for core, at in ((0, 0), (1, 4))]

    @pl.when(counting)
    def _():
        for copies in cnt_copies:
            copies.start()
        load_start(pairs[8:])

    wr_copy = remote(wr_ref.at[pl.ds(pl.multiple_of(other * half, half), half)], wr_peer,
                     core_send.at[0], core_recv.at[0], {"chan": other})
    loaded("second")
    sec_all[me] = jnp.maximum(second_ref[...], 0)
    sec_moves = [[line(step, lambda j, q=q: sec_all.at[j, pl.ds(q * hrows, hrows)],
                       sec_send.at[step, q], sec_recv.at[step, q])
                  for q in range(2)] for step in range(n - 1)]
    if n > 1:
        for q in range(2):
            line_start(sec_moves[0][q])
    loaded("pair")
    for j in range(n):
        bi_send[j] = bi_ref[:, j * share : (j + 1) * share]
    bi_all[me, mine] = bi_send[me, mine]

    bi_copies = Spread(1, lambda to: bi_send.at[to, mine], bi_all.at[me, mine],
                       bi_all.at[peers, mine])
    bi_share = share_copy(0, bi_all)

    def sec_forward(step):
        for q in range(2):
            line_forward(sec_moves[step][q], sec_moves[step + 1][q])

    def bi_forward():
        bi_copies.wait_recv()
        bi_share.start()

    pair = gw * gw
    iota = lambda shape, dim: lax.broadcasted_iota(jnp.int32, shape, dim)
    same = iota((blk, blk), 0) // gw == iota((blk, blk), 1) // gw

    def build_taps():
        same_out = iota((width, pair), 0) % gw == iota((width, pair), 1) % gw
        spread = (iota((pair, blk), 0) // gw == iota((pair, blk), 1) % gw).astype(f32).astype(bf16)
        inside = iota((width, blk), 0) // gw % (blk // gw) == iota((width, blk), 1) // gw
        by_group = wg_ref[...].astype(f32).T
        for t in range(9):
            values = by_group[:, t * pair : (t + 1) * pair]
            values = jnp.broadcast_to(values[:, None, :], (groups, gw, pair)).reshape(width, pair)
            values = jnp.where(same_out, values, 0.0).astype(bf16)
            taps[t] = jnp.where(inside, dot_nn(values, spread), 0.0).astype(bf16)

    def shifter(count):
        prow = lax.broadcasted_iota(jnp.int32, (count, blk), 0)
        p_w = prow % side
        p_h = (prow // side) % side

        def moved(x, a, b):
            shift = (side * a + b) % count
            if shift:
                x = pltpu.roll(x, shift, 0)
            if a:
                x = jnp.where(p_h >= 1 if a == 1 else p_h < side - 1, x, 0.0)
            if b:
                x = jnp.where(p_w >= 1 if b == 1 else p_w < side - 1, x, 0.0)
            return x

        return moved

    def prepare_first():
        moved = shifter(rows)
        for b in range(blocks):
            first = jnp.maximum(first_ref[:, b * blk : (b + 1) * blk], 0).astype(f32)
            for t, (da, db) in enumerate(tap_offsets):
                ft[t, b] = moved(first, -da, -db).T.astype(bf16)

    hop_copies = [
        remote(ng.at[c, crop_rows[q]], inc.at[c, crop_rows[q]],
               hop_send.at[q], hop_recv.at[q], {"section": lax.max(s - 1, 0)})
        for q in range(2)
    ]
    fwd_copies = [
        remote(inc.at[c, crop_rows[q]], inc.at[c, crop_rows[q]],
               fwd_send.at[q], fwd_recv.at[q], {"chan": other})
        for q in range(2)
    ]

    @pl.when(s == last)
    def _():
        loaded("wl", "teacher")
        feature = jnp.maximum(out_ref[...], 0)
        lateral = dot_nn(feature, wl_ref[...])
        error = (mask[:, 0:1] * (lateral - teacher_ref[...].astype(f32))).astype(bf16)
        imitation = dot_nt(error, wl_ref[...])
        loaded("wg")
        build_taps()
        loaded("top", "first", "we", "wr")
        wr_copy.start()
        cnt_copies[0].wait_recv()
        bi_copies.start()
        covered = cnt[0]
        for j in range(1, n):
            covered = covered + cnt[j]
        scale = (imitation_weight * pixels) / covered[0:1, 0:1]
        start = (top_ref[...].astype(f32) + imitation * scale).astype(bf16)
        start = jnp.where(out_ref[...] > 0, start, jnp.zeros_like(start))
        pas[0] = start[:, :half]
        pas[1] = start[:, half:]

    @pl.when(s < last)
    def _():
        loaded("wl", "teacher", "wg", "top", "first", "we", "wr")
        wr_copy.start()
        build_taps()
        prepare_first()
        for step in range(n - 2):
            sec_forward(step)
        pl.when(jnp.logical_not(at_end))(bi_copies.start)

    ps_copies = Spread(2, lambda to: ps_send.at[to, mine], ps_all.at[me, mine],
                       ps_all.at[peers, mine])
    ps_share = share_copy(1, ps_all)
    d_moves = [[line(step, lambda j, q=q: d_all.at[j, crop_rows[q]], d_send.at[step, q],
                     d_recv.at[step, q]) for q in range(2)] for step in range(n - 1)]
    dfx_copies = [remote(d_all.at[me, crop_rows[q]], dfx.at[crop_rows[q]], core_send.at[1 + q],
                         core_recv.at[1 + q], {"chan": other}) for q in range(2)]
    ng_copy = remote(ng.at[c], ng.at[c], core_send.at[3], core_recv.at[3], {"chan": other})

    def gate_half(h, q):
        at = pl.ds(pl.multiple_of(h * half, half), half)
        value = inc[h, crop_rows[q]]
        gate = out_ref[q * hrows : (q + 1) * hrows, at] > 0
        pas[h, crop_rows[q]] = jnp.where(gate, value, jnp.zeros_like(value))

    def own_arrives(q, where=None):
        @pl.when((s < last) & where if where is not None else s < last)
        def _():
            hop_copies[q].wait_recv()
            fwd_copies[q].start()
            if q == 0:
                pl.when(at_end)(bi_copies.start)
            gate_half(c, q)

    def other_arrives(q):
        @pl.when(s < last)
        def _():
            fwd_copies[q].wait_recv()
            gate_half(other, q)

    moved = shifter(hrows)
    own_arrives(0)
    for q in range(2):
        top, end = q * hrows, (q + 1) * hrows
        second_full = dot_nt(pas[c, top:end], we_ref[c])
        if q == 0:
            own_arrives(1, c == 1)
        other_arrives(q)
        for j in range(n):
            at = (j * share) // half
            ps_send[j, top:end] = pas[at, top:end, j * share - at * half : (j + 1) * share - at * half]

        @pl.when(c == q)
        def _():
            ps_all[me, top:end] = ps_send[me, top:end]
            pl.when(jnp.logical_not(at_end))(ps_copies.start)

        second_full = second_full + dot_nt(pas[other, top:end], we_ref[other])
        for b in range(blocks):
            lo, hi = b * blk, (b + 1) * blk
            lhs = jnp.where(second_ref[top:end, lo:hi] > 0, second_full[:, lo:hi], 0.0).astype(bf16)
            ds[top:end, lo:hi] = lhs
            total = None
            for db in (-1, 0, 1):
                column = None
                for da in (-1, 0, 1):
                    t = 3 * (da + 1) + db + 1
                    y = moved(dot_nn(lhs, taps[t, lo:hi, :]), da, 0)
                    column = y if column is None else column + y
                column = moved(column, 0, db)
                total = column if total is None else total + column
            d_all[me, top:end, lo:hi] = jnp.where(
                first_ref[top:end, lo:hi] > 0, total, 0.0).astype(bf16)
            if q == 0 and b == 0:
                own_arrives(1, c == 0)
        dfx_copies[q].start()
        if n > 1:
            @pl.when(s < last)
            def _():
                line_start(d_moves[0][q])

    @pl.when(at_end)
    def _():
        ps_copies.start()

    own_rows = pl.ds(pl.multiple_of(c * half, half), half)
    wr_copy.wait_recv()
    for q in range(2):
        top, end = q * hrows, (q + 1) * hrows
        grad = dot_nt(d_all[me, top:end], wr_ref[own_rows, :]) + pas[c, top:end].astype(f32)
        dfx_copies[q].wait_recv()
        ng[c, top:end] = (grad + dot_nt(dfx[top:end], wr_peer[...])).astype(bf16)

        @pl.when(s > 0)
        def _():
            hop_copies[q].start()

    ng_copy.start()

    @pl.when(s == last)
    def _():
        prepare_first()

    gf[...] = jnp.zeros_like(gf)
    for b in range(blocks):
        rhs = ds[:, b * blk : (b + 1) * blk]
        for t in range(9):
            dense = jnp.where(same, dot_nn(ft[t, b], rhs), 0.0)
            folded = jnp.sum(dense.reshape(blk // gw, gw, blk), axis=0)
            for j in range(n):
                gf[j, t * k : (t + 1) * k, b * blk : (b + 1) * blk] = folded[j * k : (j + 1) * k]
    g_send[...] = gf[...].astype(bf16)
    def g_copy(part, dst, recv, where):
        return remote(g_send.at[part], dst, dp_send.at[3], recv, {"dp": where})

    relayed = n > 3
    ends = ((0, 1, me >= 2), (n - 1, n - 2, me <= n - 3))

    def g_start():
        for step in range(1, n):
            to = lax.rem(me + step, n)
            direct = (to != 0) & (to != n - 1) if relayed else to >= 0

            @pl.when(direct)
            def _():
                g_copy(to, g_recv.at[me], dp_recv.at[3], to).start()

        if relayed:
            for i, (end, by, far) in enumerate(ends):
                @pl.when(far)
                def _():
                    g_copy(end, g_far.at[i, me], far_recv.at[i], by).start()

    def g_relay():
        for i, (end, by, _) in enumerate(ends):
            @pl.when(me == by)
            def _():
                others = pl.ds(2 if end == 0 else 0, n - 2)
                arrived = g_far.at[i, others]
                pltpu.make_async_copy(arrived, arrived, far_recv.at[i]).wait()
                total = gf[end]
                for j in range(n - 2):
                    total = total + g_far[i, j + (2 if end == 0 else 0)].astype(f32)
                g_send[end] = total.astype(bf16)
                g_copy(end, g_recv.at[me], dp_recv.at[3], end).start()

    def g_wait(sem, count):
        some = g_recv.at[pl.ds(0, count)]
        pltpu.make_async_copy(some, some, sem).wait()

    if n > 1:
        @pl.when(s == last)
        def _():
            for q in range(2):
                line_start(d_moves[0][q])

    def d_forward(step):
        for q in range(2):
            line_forward(d_moves[step][q], d_moves[step + 1][q])

    for step in range(n - 2):
        @pl.when(s == last)
        def _():
            sec_forward(step)
            if step == 0:
                bi_forward()

        d_forward(step)

        @pl.when(s == last)
        def _():
            if step == 0:
                g_start()

        if step == 0:
            @pl.when(s < last)
            def _():
                bi_forward()

            ps_copies.wait_recv()
            ps_share.start()

            @pl.when(s < last)
            def _():
                g_start()

            ng_copy.wait_recv()
            grads_ref[:, :half] = ng[0]
            grads_ref[:, half:] = ng[1]
    if relayed:
        g_relay()

    for q in range(2):
        line_finish([step_moves[q] for step_moves in sec_moves])
    ps_share.wait_recv()
    expand = dot_tn(sec_all[...].reshape(n * rows, width), ps_all[...].reshape(n * rows, share))
    expand_ref[...] = expand * norm
    bi_share.wait_recv()

    def reduce_crop(q):
        line_finish([step_moves[q] for step_moves in d_moves])
        bi_rows = bi_all[:, q * hrows : (q + 1) * hrows].reshape(n * hrows, share)
        d_rows = d_all[:, q * hrows : (q + 1) * hrows].reshape(n * hrows, width)
        reduced = dot_tn(bi_rows, d_rows) * norm
        reduce_ref[...] = reduced if q == 0 else reduce_ref[...] + reduced

    reduce_crop(0)
    reduce_crop(1)
    if relayed:
        @pl.when(at_end)
        def _():
            for j in range(n):
                if 0 < j < n - 1:
                    @pl.when((me == 0) & (j != 1) | (me == n - 1) & (j != n - 2))
                    def _():
                        g_recv[j] = jnp.zeros(g_recv.shape[1:], bf16)
                else:
                    g_recv[j] = jnp.zeros(g_recv.shape[1:], bf16)
            g_wait(dp_recv.at[3], 1)

        @pl.when(jnp.logical_not(at_end))
        def _():
            g_recv[me] = jnp.zeros(g_recv.shape[1:], bf16)
            g_wait(dp_recv.at[3], n - 1)
    else:
        g_recv[me] = jnp.zeros(g_recv.shape[1:], bf16)
        g_wait(dp_recv.at[3], n - 1)
    total = gf[me]
    for j in range(n):
        total = total + g_recv[j].astype(f32)
    total = (total * norm)[: 9 * k]
    wide = jnp.broadcast_to(total[:, None, :], (9 * k, gw, width)).reshape(9 * k * gw, width)
    out_of = iota((9 * k * gw, width), 0) % gw == iota((9 * k * gw, width), 1) % gw
    wide = jnp.where(out_of, wide, 0.0)
    high = wide.astype(bf16)
    low = (wide - high.astype(f32)).astype(bf16)
    group_of = (iota((width, groups), 0) // gw == iota((width, groups), 1)).astype(f32).astype(bf16)
    group_ref[...] = dot_nn(high, group_of) + dot_nn(low, group_of)

    for move in [move for step_moves in sec_moves + d_moves for move in step_moves]:
        for copy, sends, _ in move:
            pl.when(sends)(copy.wait_send)
    g_wait(dp_send.at[3], n - 1)
    for copy in [bi_share, ps_share, bi_copies, ps_copies, wr_copy, ng_copy] + dfx_copies:
        copy.wait_send()

    @pl.when(counting)
    def _():
        for copies in cnt_copies:
            copies.wait_send()

    @pl.when(s > 0)
    def _():
        for copy in hop_copies:
            copy.wait_send()

    @pl.when(s < last)
    def _():
        for copy in fwd_copies:
            copy.wait_send()


def store_kernel(*refs):
    count = (len(refs) - 1) // 2
    copies = [pltpu.make_async_copy(refs[i], refs[count + i], refs[-1].at[i]) for i in range(count)]
    for copy in copies:
        copy.start()
    for copy in copies:
        copy.wait()


def on_device(
    block_inputs, out_pre, first_pre, second_pre, w_reduce, w_group, w_expand, w_lateral,
    teacher, top_grad, boxes, region_counts,
):
    n = lax.axis_size("dp")
    sections = lax.axis_size("section")
    crops, side, _, channels = top_grad.shape
    rows = crops * side * side
    width = first_pre.shape[4]
    lateral_width = w_lateral.shape[1]
    groups, gw = w_group.shape[2], w_group.shape[3]
    slots = boxes.shape[1]
    pixels = rows * n
    share = channels // n
    k = gw // n
    grows = -(-9 * k // 8) * 8
    half = channels // 2
    blk = min(256, width)
    hbm = pl.BlockSpec(memory_space=pltpu.HBM)
    vmem = pl.BlockSpec(memory_space=pltpu.VMEM)
    dma = pltpu.SemaphoreType.DMA
    peers = max(n - 1, 1)
    shapes = (
        ((rows, channels), bf16), ((share, width), f32),
        ((9 * k * gw, groups), f32), ((width, share), f32),
    )
    results = pl.pallas_call(
        functools.partial(kernel, (n, sections, crops, side, slots, pixels)),
        out_shape=tuple(pltpu.VMEM(shape, kind) for shape, kind in shapes),
        in_specs=[hbm] * 12,
        out_specs=(vmem,) * 4,
        scratch_shapes=[
            pltpu.SMEM((crops, 4, slots), jnp.int32),
            pltpu.SMEM((1, crops), jnp.int32),
            pltpu.VMEM((3, rows, channels), bf16),
            pltpu.VMEM((2, rows, width), bf16),
            pltpu.VMEM((channels, width), bf16),
            pltpu.VMEM((9 * gw * gw, groups), bf16),
            pltpu.VMEM((2, width, half), bf16),
            pltpu.VMEM((channels, lateral_width), bf16),
            pltpu.VMEM((rows, lateral_width), bf16),
            dma((11,)),
            pltpu.VMEM((2, rows, half), bf16),
            pltpu.VMEM((2, rows, half), bf16),
            pltpu.VMEM((half, width), bf16),
            pltpu.VMEM((rows, width), bf16),
            pltpu.VMEM((2, rows, half), bf16),
            pltpu.VMEM((rows, width), bf16),
            pltpu.VMEM((n, rows, width), bf16),
            pltpu.VMEM((n, rows, width), bf16),
            pltpu.VMEM((n, rows, share), bf16),
            pltpu.VMEM((n, rows, share), bf16),
            pltpu.VMEM((n, rows, share), bf16),
            pltpu.VMEM((n, rows, share), bf16),
            pltpu.VMEM((n, grows, width), f32),
            pltpu.VMEM((n, grows, width), bf16),
            pltpu.VMEM((n, grows, width), bf16),
            pltpu.VMEM((2, n, grows, width), bf16),
            dma((2,)),
            pltpu.VMEM((n, 8, 128), f32),
            pltpu.VMEM((9, width, blk), bf16),
            pltpu.VMEM((9, width // blk, blk, rows), bf16),
            dma((5,)), dma((4,)), dma((4,)), dma((4,)),
            dma((2,)), dma((2,)), dma((2,)), dma((2,)),
            dma((peers, 2, 2)), dma((peers, 2, 2)), dma((peers, 2, 2)), dma((peers, 2, 2)),
            dma((2,)), dma((2,)),
        ],
        compiler_params=pltpu.CompilerParams(
            collective_id=0, has_side_effects=True, vmem_limit_bytes=44 << 20,
        ),
    )(*(pltpu.with_memory_space_constraint(x, pltpu.HBM) for x in (
        boxes.transpose(0, 2, 1), region_counts.reshape(1, crops),
        block_inputs.reshape(rows, channels), out_pre.reshape(rows, channels),
        first_pre.reshape(rows, width), second_pre.reshape(rows, width),
        w_reduce[0], w_group[0].transpose(0, 2, 3, 1).reshape(9 * gw * gw, groups), w_expand[0], w_lateral,
        teacher.reshape(rows, lateral_width), top_grad.reshape(rows, channels),
    )))
    grads, reduced, group, expand = pl.pallas_call(
        store_kernel,
        out_shape=tuple(jax.ShapeDtypeStruct(shape, kind) for shape, kind in shapes),
        in_specs=[vmem] * 4,
        out_specs=(hbm,) * 4,
        scratch_shapes=[dma((4,))],
    )(*(pltpu.with_memory_space_constraint(x, pltpu.VMEM) for x in results))
    group = group.reshape(9, k, gw, groups).transpose(0, 3, 1, 2)
    return (
        grads.reshape(1, crops, side, side, channels), reduced[None], group[None], expand[None],
    )


def solution(mesh):
    return jax.shard_map(
        on_device,
        mesh=mesh,
        in_specs=(
            P("section", ("parts", "dp"), None, None, None),
            P("section", ("parts", "dp"), None, None, None),
            P("section", ("parts", "dp"), None, None, "chan"),
            P("section", ("parts", "dp"), None, None, "chan"),
            P("section", None, "chan"),
            P("section", None, "chan", None, None),
            P("section", "chan", None),
            P(),
            P(("parts", "dp"), None, None, None),
            P(("parts", "dp"), None, None, None),
            P(("parts", "dp"), None, None),
            P(("parts", "dp")),
        ),
        out_specs=(
            P("section", ("parts", "dp"), None, None, None),
            P(("parts", "section"), "dp", "chan"),
            P(("parts", "section"), None, "chan", "dp", None),
            P(("parts", "section"), "chan", "dp"),
        ),
        check_vma=False,
    )
```

```python
import functools
import math

import jax
import jax.numpy as jnp
from jax import lax
from jax.experimental import pallas as pl
from jax.experimental.pallas import tpu as pltpu
from jax.sharding import PartitionSpec as P

imitation_weight = 0.5
tap_offsets = [(tap // 3 - 1, tap % 3 - 1) for tap in range(9)]
f32 = jnp.float32
bf16 = jnp.bfloat16


def dot_nn(a, b):
    return lax.dot_general(a, b, (((1,), (0,)), ((), ())), preferred_element_type=f32)


def dot_nt(a, b):
    return lax.dot_general(a, b, (((1,), (1,)), ((), ())), preferred_element_type=f32)


def dot_tn(a, b):
    return lax.dot_general(a, b, (((0,), (0,)), ((), ())), preferred_element_type=f32)


def kernel(
    dims,
    boxes_hbm, counts_hbm, bi_hbm, out_hbm, first_hbm, second_hbm, wr_hbm, wg_hbm, we_hbm,
    wl_hbm, teacher_hbm, top_hbm,
    grads_ref, reduce_ref, group_ref, expand_ref,
    boxes_ref, counts_ref,
    full_ref, part_ref, wr_ref, wg_ref, we_ref, wl_ref, teacher_ref, load_sem,
    inc, pas, wr_peer, dfx, ng, ds, d_all, sec_all, bi_send, bi_all, ps_send, ps_all,
    gf, g_send, g_recv, g_far, far_recv, cnt, taps, ft,
    dp_send, dp_recv, core_send, core_recv, hop_send, hop_recv, fwd_send, fwd_recv,
    sec_send, sec_recv, d_send, d_recv, share_send, share_recv,
):
    n, sections, crops, side, slots, pixels = dims
    out_ref, bi_ref, top_ref = (full_ref.at[i] for i in range(3))
    first_ref, second_ref = part_ref.at[0], part_ref.at[1]
    rows, channels = bi_ref.shape
    half = channels // 2
    width = first_ref.shape[1]
    groups = wg_ref.shape[1]
    gw = width // groups
    blk = taps.shape[2]
    blocks = width // blk
    cells = side * side
    share = channels // n
    k = gw // n
    hrows = rows // 2
    me = lax.axis_index("dp")
    s = lax.axis_index("section")
    c = lax.axis_index("chan")
    other = 1 - c
    last = sections - 1
    norm = 1.0 / math.sqrt(pixels)

    def remote(src, dst, send, recv, where):
        return pltpu.make_async_remote_copy(
            src_ref=src, dst_ref=dst, send_sem=send, recv_sem=recv,
            device_id=where, device_id_type=pl.DeviceIdType.MESH,
        )

    class Spread:
        def __init__(self, what, src_of, dst, moved, at=None, where={}):
            at = what if at is None else at
            self.copies = [
                remote(src_of(to), dst, dp_send.at[at], dp_recv.at[what], {"dp": to, **where})
                for to in (lax.rem(me + step, n) for step in range(1, n))
            ]
            self.sent = pltpu.make_async_copy(moved, moved, dp_send.at[at])
            self.received = pltpu.make_async_copy(moved, moved, dp_recv.at[what])

        def start(self):
            for copy in self.copies:
                copy.start()

        def wait_recv(self):
            self.received.wait()

        def wait_send(self):
            self.sent.wait()

    mine = pl.ds(pl.multiple_of(c * hrows, hrows), hrows)
    peers = pl.ds(0, n - 1)
    crop_rows = [pl.ds(q * hrows, hrows) for q in range(2)]

    def share_copy(which, buf):
        return remote(buf.at[:, mine], buf.at[:, mine], share_send.at[which],
                      share_recv.at[which], {"chan": other})

    def line(step, block, send, recv):
        ahead = block(lax.max(me - step, 0))
        behind = block(lax.min(me + step, n - 1))
        right = remote(ahead, ahead, send.at[0], recv.at[0], {"dp": lax.min(me + 1, n - 1)})
        left = remote(behind, behind, send.at[1], recv.at[1], {"dp": lax.max(me - 1, 0)})
        return (
            (right, (me - step >= 0) & (me + 1 < n), me - 1 - step >= 0),
            (left, (me + step < n) & (me >= 1), me + 1 + step < n),
        )

    def line_start(moves):
        for copy, sends, _ in moves:
            pl.when(sends)(copy.start)

    def line_forward(moves, following):
        for (copy, _, receives), (onward, sends, _) in zip(moves, following):
            @pl.when(receives & sends)
            def _():
                copy.wait_recv()
                onward.start()

    def line_settle(moves, following):
        for (copy, _, receives), (_, sends, _) in zip(moves, following):
            pl.when(receives & jnp.logical_not(sends))(copy.wait_recv)

    def line_finish(moves):
        for step in range(n - 1):
            if step == n - 2:
                for copy, _, receives in moves[step]:
                    pl.when(receives)(copy.wait_recv)
            else:
                line_settle(moves[step], moves[step + 1])

    barrier = pltpu.get_barrier_semaphore()
    mesh_type = pl.DeviceIdType.MESH
    for step in range(1, n):
        pl.semaphore_signal(barrier, inc=1, device_id={"dp": lax.rem(me + step, n)},
                            device_id_type=mesh_type)
    pl.semaphore_signal(barrier, inc=1, device_id={"chan": other}, device_id_type=mesh_type)

    @pl.when((s == last) & (c == 0))
    def _():
        for step in range(1, n):
            pl.semaphore_signal(barrier, inc=1, device_id_type=mesh_type,
                                device_id={"dp": lax.rem(me + step, n), "chan": other})

    @pl.when(s > 0)
    def _():
        pl.semaphore_signal(barrier, inc=1, device_id={"section": s - 1},
                            device_id_type=mesh_type)

    @pl.when(s < last)
    def _():
        pl.semaphore_signal(barrier, inc=1, device_id={"section": s + 1},
                            device_id_type=mesh_type)

    pairs = (
        ("boxes", boxes_hbm, boxes_ref), ("counts", counts_hbm, counts_ref),
        ("second", second_hbm, second_ref), ("pair", out_hbm, out_ref), ("wl", wl_hbm, wl_ref),
        ("teacher", teacher_hbm, teacher_ref), ("pair", bi_hbm, bi_ref),
        ("wg", wg_hbm, wg_ref), ("top", top_hbm, top_ref), ("we", we_hbm.at[:, :half], we_ref.at[0]),
        ("we", we_hbm.at[:, half:], we_ref.at[1]), ("first", first_hbm, first_ref),
        ("wr", wr_hbm, wr_ref),
    )
    whole = {
        "boxes": boxes_ref, "counts": counts_ref, "pair": full_ref.at[0:2], "top": top_ref,
        "first": first_ref, "second": second_ref, "wl": wl_ref, "teacher": teacher_ref,
        "wg": wg_ref, "we": we_ref, "wr": wr_ref,
    }
    load_at = {name: load_sem.at[i] for i, name in enumerate(whole)}

    def load_start(some):
        for name, a, b in some:
            pltpu.make_async_copy(a, b, load_at[name]).start()

    def loaded(*names):
        for name in names:
            pltpu.make_async_copy(whole[name], whole[name], load_at[name]).wait()

    counting = (s == last) & (c == 1)
    at_end = (me == 0) | (me == n - 1)
    load_start(pairs[:8])

    @pl.when(jnp.logical_not(counting))
    def _():
        load_start(pairs[8:])

    loaded("boxes", "counts")
    row = lax.broadcasted_iota(jnp.int32, (cells, 128), 0)
    row_h, row_w = row // side, row % side
    masks = []
    for crop in range(crops):
        inside = jnp.zeros((cells, 128), f32)
        for r in range(slots):
            hit = ((row_h >= boxes_ref[crop, 0, r]) & (row_h < boxes_ref[crop, 1, r])
                   & (row_w >= boxes_ref[crop, 2, r]) & (row_w < boxes_ref[crop, 3, r])
                   & (counts_ref[0, crop] > r))
            inside = jnp.where(hit, 1.0, inside)
        masks.append(inside)
    mask = jnp.concatenate(masks, axis=0)
    cnt[me] = jnp.broadcast_to(jnp.sum(mask, axis=0, keepdims=True), (8, 128))

    pl.semaphore_wait(barrier, n + jnp.where(s > 0, 1, 0) + jnp.where(s < last, 1, 0)
                      + jnp.where(counting, n - 1, 0))

    cnt_copies = [Spread(0, lambda to: cnt.at[me], cnt.at[me], cnt.at[peers], at, {"chan": core})
                  for core, at in ((0, 0), (1, 4))]

    @pl.when(counting)
    def _():
        for copies in cnt_copies:
            copies.start()
        load_start(pairs[8:])

    wr_copy = remote(wr_ref.at[pl.ds(pl.multiple_of(other * half, half), half)], wr_peer,
                     core_send.at[0], core_recv.at[0], {"chan": other})
    loaded("second")
    sec_all[me] = jnp.maximum(second_ref[...], 0)
    sec_moves = [[line(step, lambda j, q=q: sec_all.at[j, pl.ds(q * hrows, hrows)],
                       sec_send.at[step, q], sec_recv.at[step, q])
                  for q in range(2)] for step in range(n - 1)]
    if n > 1:
        for q in range(2):
            line_start(sec_moves[0][q])
    loaded("pair")
    for j in range(n):
        bi_send[j] = bi_ref[:, j * share : (j + 1) * share]
    bi_all[me, mine] = bi_send[me, mine]

    bi_copies = Spread(1, lambda to: bi_send.at[to, mine], bi_all.at[me, mine],
                       bi_all.at[peers, mine])
    bi_share = share_copy(0, bi_all)

    def sec_forward(step):
        for q in range(2):
            line_forward(sec_moves[step][q], sec_moves[step + 1][q])

    def bi_forward():
        bi_copies.wait_recv()
        bi_share.start()

    pair = gw * gw
    iota = lambda shape, dim: lax.broadcasted_iota(jnp.int32, shape, dim)
    same = iota((blk, blk), 0) // gw == iota((blk, blk), 1) // gw

    def build_taps():
        same_out = iota((width, pair), 0) % gw == iota((width, pair), 1) % gw
        spread = (iota((pair, blk), 0) // gw == iota((pair, blk), 1) % gw).astype(f32).astype(bf16)
        inside = iota((width, blk), 0) // gw % (blk // gw) == iota((width, blk), 1) // gw
        by_group = wg_ref[...].astype(f32).T
        for t in range(9):
            values = by_group[:, t * pair : (t + 1) * pair]
            values = jnp.broadcast_to(values[:, None, :], (groups, gw, pair)).reshape(width, pair)
            values = jnp.where(same_out, values, 0.0).astype(bf16)
            taps[t] = jnp.where(inside, dot_nn(values, spread), 0.0).astype(bf16)

    def shifter(count):
        prow = lax.broadcasted_iota(jnp.int32, (count, blk), 0)
        p_w = prow % side
        p_h = (prow // side) % side

        def moved(x, a, b):
            shift = (side * a + b) % count
            if shift:
                x = pltpu.roll(x, shift, 0)
            if a:
                x = jnp.where(p_h >= 1 if a == 1 else p_h < side - 1, x, 0.0)
            if b:
                x = jnp.where(p_w >= 1 if b == 1 else p_w < side - 1, x, 0.0)
            return x

        return moved

    def prepare_first():
        moved = shifter(rows)
        for b in range(blocks):
            first = jnp.maximum(first_ref[:, b * blk : (b + 1) * blk], 0).astype(f32)
            for t, (da, db) in enumerate(tap_offsets):
                ft[t, b] = moved(first, -da, -db).T.astype(bf16)

    hop_copies = [
        remote(ng.at[c, crop_rows[q]], inc.at[c, crop_rows[q]],
               hop_send.at[q], hop_recv.at[q], {"section": lax.max(s - 1, 0)})
        for q in range(2)
    ]
    fwd_copies = [
        remote(inc.at[c, crop_rows[q]], inc.at[c, crop_rows[q]],
               fwd_send.at[q], fwd_recv.at[q], {"chan": other})
        for q in range(2)
    ]

    @pl.when(s == last)
    def _():
        loaded("wl", "teacher")
        feature = jnp.maximum(out_ref[...], 0)
        lateral = dot_nn(feature, wl_ref[...])
        error = (mask[:, 0:1] * (lateral - teacher_ref[...].astype(f32))).astype(bf16)
        imitation = dot_nt(error, wl_ref[...])
        loaded("wg")
        build_taps()
        loaded("top", "first", "we", "wr")
        wr_copy.start()
        cnt_copies[0].wait_recv()
        bi_copies.start()
        covered = cnt[0]
        for j in range(1, n):
            covered = covered + cnt[j]
        scale = (imitation_weight * pixels) / covered[0:1, 0:1]
        start = (top_ref[...].astype(f32) + imitation * scale).astype(bf16)
        start = jnp.where(out_ref[...] > 0, start, jnp.zeros_like(start))
        pas[0] = start[:, :half]
        pas[1] = start[:, half:]

    @pl.when(s < last)
    def _():
        loaded("wl", "teacher", "wg", "top", "first", "we", "wr")
        wr_copy.start()
        build_taps()
        prepare_first()
        pl.when(at_end)(bi_copies.start)
        for step in range(n - 2):
            sec_forward(step)
        pl.when(jnp.logical_not(at_end))(bi_copies.start)

    ps_copies = Spread(2, lambda to: ps_send.at[to, mine], ps_all.at[me, mine],
                       ps_all.at[peers, mine])
    ps_share = share_copy(1, ps_all)
    d_moves = [[line(step, lambda j, q=q: d_all.at[j, crop_rows[q]], d_send.at[step, q],
                     d_recv.at[step, q]) for q in range(2)] for step in range(n - 1)]
    dfx_copies = [remote(d_all.at[me, crop_rows[q]], dfx.at[crop_rows[q]], core_send.at[1 + q],
                         core_recv.at[1 + q], {"chan": other}) for q in range(2)]
    ng_copy = remote(ng.at[c], ng.at[c], core_send.at[3], core_recv.at[3], {"chan": other})

    def gate_half(h, q):
        at = pl.ds(pl.multiple_of(h * half, half), half)
        value = inc[h, crop_rows[q]]
        gate = out_ref[q * hrows : (q + 1) * hrows, at] > 0
        pas[h, crop_rows[q]] = jnp.where(gate, value, jnp.zeros_like(value))

    def own_arrives(q, where=None):
        @pl.when((s < last) & where if where is not None else s < last)
        def _():
            hop_copies[q].wait_recv()
            fwd_copies[q].start()
            gate_half(c, q)

    def other_arrives(q):
        @pl.when(s < last)
        def _():
            fwd_copies[q].wait_recv()
            gate_half(other, q)

    moved = shifter(hrows)
    own_arrives(0)
    for q in range(2):
        top, end = q * hrows, (q + 1) * hrows
        second_full = dot_nt(pas[c, top:end], we_ref[c])
        if q == 0:
            own_arrives(1, c == 1)
        other_arrives(q)
        for j in range(n):
            at = (j * share) // half
            ps_send[j, top:end] = pas[at, top:end, j * share - at * half : (j + 1) * share - at * half]

        @pl.when(c == q)
        def _():
            ps_all[me, top:end] = ps_send[me, top:end]
            pl.when(jnp.logical_not(at_end))(ps_copies.start)

        second_full = second_full + dot_nt(pas[other, top:end], we_ref[other])
        for b in range(blocks):
            lo, hi = b * blk, (b + 1) * blk
            lhs = jnp.where(second_ref[top:end, lo:hi] > 0, second_full[:, lo:hi], 0.0).astype(bf16)
            ds[top:end, lo:hi] = lhs
            total = None
            for db in (-1, 0, 1):
                column = None
                for da in (-1, 0, 1):
                    t = 3 * (da + 1) + db + 1
                    y = moved(dot_nn(lhs, taps[t, lo:hi, :]), da, 0)
                    column = y if column is None else column + y
                column = moved(column, 0, db)
                total = column if total is None else total + column
            d_all[me, top:end, lo:hi] = jnp.where(
                first_ref[top:end, lo:hi] > 0, total, 0.0).astype(bf16)
            if q == 0 and b == 0:
                own_arrives(1, c == 0)
        dfx_copies[q].start()
        if n > 1:
            @pl.when(s < last)
            def _():
                line_start(d_moves[0][q])

    @pl.when(at_end)
    def _():
        ps_copies.start()

    own_rows = pl.ds(pl.multiple_of(c * half, half), half)
    wr_copy.wait_recv()
    for q in range(2):
        top, end = q * hrows, (q + 1) * hrows
        grad = dot_nt(d_all[me, top:end], wr_ref[own_rows, :]) + pas[c, top:end].astype(f32)
        dfx_copies[q].wait_recv()
        ng[c, top:end] = (grad + dot_nt(dfx[top:end], wr_peer[...])).astype(bf16)

        @pl.when(s > 0)
        def _():
            hop_copies[q].start()

    ng_copy.start()

    @pl.when(s == last)
    def _():
        prepare_first()

    gf[...] = jnp.zeros_like(gf)
    for b in range(blocks):
        rhs = ds[:, b * blk : (b + 1) * blk]
        for t in range(9):
            dense = jnp.where(same, dot_nn(ft[t, b], rhs), 0.0)
            folded = jnp.sum(dense.reshape(blk // gw, gw, blk), axis=0)
            for j in range(n):
                gf[j, t * k : (t + 1) * k, b * blk : (b + 1) * blk] = folded[j * k : (j + 1) * k]
    g_send[...] = gf[...].astype(bf16)
    def g_copy(part, dst, recv, where):
        return remote(g_send.at[part], dst, dp_send.at[3], recv, {"dp": where})

    relayed = n > 3
    ends = ((0, 1, me >= 2), (n - 1, n - 2, me <= n - 3))

    def g_start(relayed):
        for step in range(1, n):
            to = lax.rem(me + step, n)
            direct = (to != 0) & (to != n - 1) if relayed else to >= 0

            @pl.when(direct)
            def _():
                g_copy(to, g_recv.at[me], dp_recv.at[3], to).start()

        if relayed:
            for i, (end, by, far) in enumerate(ends):
                @pl.when(far)
                def _():
                    g_copy(end, g_far.at[i, me], far_recv.at[i], by).start()

    def g_relay():
        for i, (end, by, _) in enumerate(ends):
            @pl.when(me == by)
            def _():
                others = pl.ds(2 if end == 0 else 0, n - 2)
                arrived = g_far.at[i, others]
                pltpu.make_async_copy(arrived, arrived, far_recv.at[i]).wait()
                total = gf[end]
                for j in range(n - 2):
                    total = total + g_far[i, j + (2 if end == 0 else 0)].astype(f32)
                g_send[end] = total.astype(bf16)
                g_copy(end, g_recv.at[me], dp_recv.at[3], end).start()

    def g_wait(sem, count):
        some = g_recv.at[pl.ds(0, count)]
        pltpu.make_async_copy(some, some, sem).wait()

    if n > 1:
        @pl.when(s == last)
        def _():
            for q in range(2):
                line_start(d_moves[0][q])

    def d_forward(step):
        for q in range(2):
            line_forward(d_moves[step][q], d_moves[step + 1][q])

    for step in range(n - 2):
        @pl.when(s == last)
        def _():
            sec_forward(step)
            if step == 0:
                bi_forward()

        d_forward(step)

        @pl.when(s == last)
        def _():
            if step == 0:
                g_start(relayed)

        if step == 0:
            @pl.when(s < last)
            def _():
                bi_forward()

            ps_copies.wait_recv()
            ps_share.start()

            @pl.when((s < last) & at_end)
            def _():
                g_start(False)

            ng_copy.wait_recv()
            grads_ref[:, :half] = ng[0]
            grads_ref[:, half:] = ng[1]
    @pl.when((s < last) & jnp.logical_not(at_end))
    def _():
        g_start(False)

    if relayed:
        pl.when(s == last)(g_relay)

    for q in range(2):
        line_finish([step_moves[q] for step_moves in sec_moves])
    ps_share.wait_recv()
    expand = dot_tn(sec_all[...].reshape(n * rows, width), ps_all[...].reshape(n * rows, share))
    expand_ref[...] = expand * norm
    bi_share.wait_recv()

    def reduce_crop(q):
        line_finish([step_moves[q] for step_moves in d_moves])
        bi_rows = bi_all[:, q * hrows : (q + 1) * hrows].reshape(n * hrows, share)
        d_rows = d_all[:, q * hrows : (q + 1) * hrows].reshape(n * hrows, width)
        reduced = dot_tn(bi_rows, d_rows) * norm
        reduce_ref[...] = reduced if q == 0 else reduce_ref[...] + reduced

    reduce_crop(0)
    reduce_crop(1)
    if relayed:
        @pl.when(at_end & (s == last))
        def _():
            for j in range(n):
                if 0 < j < n - 1:
                    @pl.when((me == 0) & (j != 1) | (me == n - 1) & (j != n - 2))
                    def _():
                        g_recv[j] = jnp.zeros(g_recv.shape[1:], bf16)
                else:
                    g_recv[j] = jnp.zeros(g_recv.shape[1:], bf16)
            g_wait(dp_recv.at[3], 1)

        @pl.when(jnp.logical_not(at_end & (s == last)))
        def _():
            g_recv[me] = jnp.zeros(g_recv.shape[1:], bf16)
            g_wait(dp_recv.at[3], n - 1)
    else:
        g_recv[me] = jnp.zeros(g_recv.shape[1:], bf16)
        g_wait(dp_recv.at[3], n - 1)
    total = gf[me]
    for j in range(n):
        total = total + g_recv[j].astype(f32)
    total = (total * norm)[: 9 * k]
    wide = jnp.broadcast_to(total[:, None, :], (9 * k, gw, width)).reshape(9 * k * gw, width)
    out_of = iota((9 * k * gw, width), 0) % gw == iota((9 * k * gw, width), 1) % gw
    wide = jnp.where(out_of, wide, 0.0)
    high = wide.astype(bf16)
    low = (wide - high.astype(f32)).astype(bf16)
    group_of = (iota((width, groups), 0) // gw == iota((width, groups), 1)).astype(f32).astype(bf16)
    group_ref[...] = dot_nn(high, group_of) + dot_nn(low, group_of)

    for move in [move for step_moves in sec_moves + d_moves for move in step_moves]:
        for copy, sends, _ in move:
            pl.when(sends)(copy.wait_send)
    g_wait(dp_send.at[3], n - 1)
    for copy in [bi_share, ps_share, bi_copies, ps_copies, wr_copy, ng_copy] + dfx_copies:
        copy.wait_send()

    @pl.when(counting)
    def _():
        for copies in cnt_copies:
            copies.wait_send()

    @pl.when(s > 0)
    def _():
        for copy in hop_copies:
            copy.wait_send()

    @pl.when(s < last)
    def _():
        for copy in fwd_copies:
            copy.wait_send()


def store_kernel(*refs):
    count = (len(refs) - 1) // 2
    copies = [pltpu.make_async_copy(refs[i], refs[count + i], refs[-1].at[i]) for i in range(count)]
    for copy in copies:
        copy.start()
    for copy in copies:
        copy.wait()


def on_device(
    block_inputs, out_pre, first_pre, second_pre, w_reduce, w_group, w_expand, w_lateral,
    teacher, top_grad, boxes, region_counts,
):
    n = lax.axis_size("dp")
    sections = lax.axis_size("section")
    crops, side, _, channels = top_grad.shape
    rows = crops * side * side
    width = first_pre.shape[4]
    lateral_width = w_lateral.shape[1]
    groups, gw = w_group.shape[2], w_group.shape[3]
    slots = boxes.shape[1]
    pixels = rows * n
    share = channels // n
    k = gw // n
    grows = -(-9 * k // 8) * 8
    half = channels // 2
    blk = min(256, width)
    hbm = pl.BlockSpec(memory_space=pltpu.HBM)
    vmem = pl.BlockSpec(memory_space=pltpu.VMEM)
    dma = pltpu.SemaphoreType.DMA
    peers = max(n - 1, 1)
    shapes = (
        ((rows, channels), bf16), ((share, width), f32),
        ((9 * k * gw, groups), f32), ((width, share), f32),
    )
    results = pl.pallas_call(
        functools.partial(kernel, (n, sections, crops, side, slots, pixels)),
        out_shape=tuple(pltpu.VMEM(shape, kind) for shape, kind in shapes),
        in_specs=[hbm] * 12,
        out_specs=(vmem,) * 4,
        scratch_shapes=[
            pltpu.SMEM((crops, 4, slots), jnp.int32),
            pltpu.SMEM((1, crops), jnp.int32),
            pltpu.VMEM((3, rows, channels), bf16),
            pltpu.VMEM((2, rows, width), bf16),
            pltpu.VMEM((channels, width), bf16),
            pltpu.VMEM((9 * gw * gw, groups), bf16),
            pltpu.VMEM((2, width, half), bf16),
            pltpu.VMEM((channels, lateral_width), bf16),
            pltpu.VMEM((rows, lateral_width), bf16),
            dma((11,)),
            pltpu.VMEM((2, rows, half), bf16),
            pltpu.VMEM((2, rows, half), bf16),
            pltpu.VMEM((half, width), bf16),
            pltpu.VMEM((rows, width), bf16),
            pltpu.VMEM((2, rows, half), bf16),
            pltpu.VMEM((rows, width), bf16),
            pltpu.VMEM((n, rows, width), bf16),
            pltpu.VMEM((n, rows, width), bf16),
            pltpu.VMEM((n, rows, share), bf16),
            pltpu.VMEM((n, rows, share), bf16),
            pltpu.VMEM((n, rows, share), bf16),
            pltpu.VMEM((n, rows, share), bf16),
            pltpu.VMEM((n, grows, width), f32),
            pltpu.VMEM((n, grows, width), bf16),
            pltpu.VMEM((n, grows, width), bf16),
            pltpu.VMEM((2, n, grows, width), bf16),
            dma((2,)),
            pltpu.VMEM((n, 8, 128), f32),
            pltpu.VMEM((9, width, blk), bf16),
            pltpu.VMEM((9, width // blk, blk, rows), bf16),
            dma((5,)), dma((4,)), dma((4,)), dma((4,)),
            dma((2,)), dma((2,)), dma((2,)), dma((2,)),
            dma((peers, 2, 2)), dma((peers, 2, 2)), dma((peers, 2, 2)), dma((peers, 2, 2)),
            dma((2,)), dma((2,)),
        ],
        compiler_params=pltpu.CompilerParams(
            collective_id=0, has_side_effects=True, vmem_limit_bytes=44 << 20,
        ),
    )(*(pltpu.with_memory_space_constraint(x, pltpu.HBM) for x in (
        boxes.transpose(0, 2, 1), region_counts.reshape(1, crops),
        block_inputs.reshape(rows, channels), out_pre.reshape(rows, channels),
        first_pre.reshape(rows, width), second_pre.reshape(rows, width),
        w_reduce[0], w_group[0].transpose(0, 2, 3, 1).reshape(9 * gw * gw, groups), w_expand[0], w_lateral,
        teacher.reshape(rows, lateral_width), top_grad.reshape(rows, channels),
    )))
    grads, reduced, group, expand = pl.pallas_call(
        store_kernel,
        out_shape=tuple(jax.ShapeDtypeStruct(shape, kind) for shape, kind in shapes),
        in_specs=[vmem] * 4,
        out_specs=(hbm,) * 4,
        scratch_shapes=[dma((4,))],
    )(*(pltpu.with_memory_space_constraint(x, pltpu.VMEM) for x in results))
    group = group.reshape(9, k, gw, groups).transpose(0, 3, 1, 2)
    return (
        grads.reshape(1, crops, side, side, channels), reduced[None], group[None], expand[None],
    )


def solution(mesh):
    return jax.shard_map(
        on_device,
        mesh=mesh,
        in_specs=(
            P("section", ("parts", "dp"), None, None, None),
            P("section", ("parts", "dp"), None, None, None),
            P("section", ("parts", "dp"), None, None, "chan"),
            P("section", ("parts", "dp"), None, None, "chan"),
            P("section", None, "chan"),
            P("section", None, "chan", None, None),
            P("section", "chan", None),
            P(),
            P(("parts", "dp"), None, None, None),
            P(("parts", "dp"), None, None, None),
            P(("parts", "dp"), None, None),
            P(("parts", "dp")),
        ),
        out_specs=(
            P("section", ("parts", "dp"), None, None, None),
            P(("parts", "section"), "dp", "chan"),
            P(("parts", "section"), None, "chan", "dp", None),
            P(("parts", "section"), "chan", "dp"),
        ),
        check_vma=False,
    )
```

```python
import functools
import math

import jax
import jax.numpy as jnp
from jax import lax
from jax.experimental import pallas as pl
from jax.experimental.pallas import tpu as pltpu
from jax.sharding import PartitionSpec as P

imitation_weight = 0.5
tap_offsets = [(tap // 3 - 1, tap % 3 - 1) for tap in range(9)]
f32 = jnp.float32
bf16 = jnp.bfloat16


def dot_nn(a, b):
    return lax.dot_general(a, b, (((1,), (0,)), ((), ())), preferred_element_type=f32)


def dot_nt(a, b):
    return lax.dot_general(a, b, (((1,), (1,)), ((), ())), preferred_element_type=f32)


def dot_tn(a, b):
    return lax.dot_general(a, b, (((0,), (0,)), ((), ())), preferred_element_type=f32)


def kernel(
    dims,
    boxes_hbm, counts_hbm, bi_hbm, out_hbm, first_hbm, second_hbm, wr_hbm, wg_hbm, we_hbm,
    wl_hbm, teacher_hbm, top_hbm,
    grads_ref, reduce_ref, group_ref, expand_ref,
    boxes_ref, counts_ref,
    full_ref, part_ref, wr_ref, wg_ref, we_ref, wl_ref, teacher_ref, load_sem,
    inc, pas, wr_peer, dfx, ng, ds, d_all, sec_all, bi_send, bi_all, ps_send, ps_all,
    gf, g_send, g_recv, g_far, far_recv, cnt, taps, ft,
    dp_send, dp_recv, core_send, core_recv, hop_send, hop_recv, fwd_send, fwd_recv,
    sec_send, sec_recv, d_send, d_recv, share_send, share_recv,
):
    n, sections, crops, side, slots, pixels = dims
    out_ref, bi_ref, top_ref = (full_ref.at[i] for i in range(3))
    first_ref, second_ref = part_ref.at[0], part_ref.at[1]
    rows, channels = bi_ref.shape
    half = channels // 2
    width = first_ref.shape[1]
    groups = wg_ref.shape[1]
    gw = width // groups
    blk = taps.shape[2]
    blocks = width // blk
    cells = side * side
    share = channels // n
    k = gw // n
    hrows = rows // 2
    me = lax.axis_index("dp")
    s = lax.axis_index("section")
    c = lax.axis_index("chan")
    other = 1 - c
    last = sections - 1
    norm = 1.0 / math.sqrt(pixels)

    def remote(src, dst, send, recv, where):
        return pltpu.make_async_remote_copy(
            src_ref=src, dst_ref=dst, send_sem=send, recv_sem=recv,
            device_id=where, device_id_type=pl.DeviceIdType.MESH,
        )

    class Spread:
        def __init__(self, what, src_of, dst, moved, at=None, where={}):
            at = what if at is None else at
            self.copies = [
                remote(src_of(to), dst, dp_send.at[at], dp_recv.at[what], {"dp": to, **where})
                for to in (lax.rem(me + step, n) for step in range(1, n))
            ]
            self.sent = pltpu.make_async_copy(moved, moved, dp_send.at[at])
            self.received = pltpu.make_async_copy(moved, moved, dp_recv.at[what])

        def start(self):
            for copy in self.copies:
                copy.start()

        def wait_recv(self):
            self.received.wait()

        def wait_send(self):
            self.sent.wait()

    mine = pl.ds(pl.multiple_of(c * hrows, hrows), hrows)
    peers = pl.ds(0, n - 1)
    crop_rows = [pl.ds(q * hrows, hrows) for q in range(2)]

    def share_copy(which, buf):
        return remote(buf.at[:, mine], buf.at[:, mine], share_send.at[which],
                      share_recv.at[which], {"chan": other})

    def line(step, block, send, recv):
        ahead = block(lax.max(me - step, 0))
        behind = block(lax.min(me + step, n - 1))
        right = remote(ahead, ahead, send.at[0], recv.at[0], {"dp": lax.min(me + 1, n - 1)})
        left = remote(behind, behind, send.at[1], recv.at[1], {"dp": lax.max(me - 1, 0)})
        return (
            (right, (me - step >= 0) & (me + 1 < n), me - 1 - step >= 0),
            (left, (me + step < n) & (me >= 1), me + 1 + step < n),
        )

    def line_start(moves):
        for copy, sends, _ in moves:
            pl.when(sends)(copy.start)

    def line_forward(moves, following):
        for (copy, _, receives), (onward, sends, _) in zip(moves, following):
            @pl.when(receives & sends)
            def _():
                copy.wait_recv()
                onward.start()

    def line_settle(moves, following):
        for (copy, _, receives), (_, sends, _) in zip(moves, following):
            pl.when(receives & jnp.logical_not(sends))(copy.wait_recv)

    def line_finish(moves):
        for step in range(n - 1):
            if step == n - 2:
                for copy, _, receives in moves[step]:
                    pl.when(receives)(copy.wait_recv)
            else:
                line_settle(moves[step], moves[step + 1])

    barrier = pltpu.get_barrier_semaphore()
    mesh_type = pl.DeviceIdType.MESH
    for step in range(1, n):
        pl.semaphore_signal(barrier, inc=1, device_id={"dp": lax.rem(me + step, n)},
                            device_id_type=mesh_type)
    pl.semaphore_signal(barrier, inc=1, device_id={"chan": other}, device_id_type=mesh_type)

    @pl.when((s == last) & (c == 0))
    def _():
        for step in range(1, n):
            pl.semaphore_signal(barrier, inc=1, device_id_type=mesh_type,
                                device_id={"dp": lax.rem(me + step, n), "chan": other})

    @pl.when(s > 0)
    def _():
        pl.semaphore_signal(barrier, inc=1, device_id={"section": s - 1},
                            device_id_type=mesh_type)

    @pl.when(s < last)
    def _():
        pl.semaphore_signal(barrier, inc=1, device_id={"section": s + 1},
                            device_id_type=mesh_type)

    pairs = (
        ("boxes", boxes_hbm, boxes_ref), ("counts", counts_hbm, counts_ref),
        ("second", second_hbm, second_ref), ("pair", out_hbm, out_ref), ("wl", wl_hbm, wl_ref),
        ("teacher", teacher_hbm, teacher_ref), ("pair", bi_hbm, bi_ref),
        ("wg", wg_hbm, wg_ref), ("top", top_hbm, top_ref), ("we", we_hbm.at[:, :half], we_ref.at[0]),
        ("we", we_hbm.at[:, half:], we_ref.at[1]), ("first", first_hbm, first_ref),
        ("wr", wr_hbm, wr_ref),
    )
    whole = {
        "boxes": boxes_ref, "counts": counts_ref, "pair": full_ref.at[0:2], "top": top_ref,
        "first": first_ref, "second": second_ref, "wl": wl_ref, "teacher": teacher_ref,
        "wg": wg_ref, "we": we_ref, "wr": wr_ref,
    }
    load_at = {name: load_sem.at[i] for i, name in enumerate(whole)}

    def load_start(some):
        for name, a, b in some:
            pltpu.make_async_copy(a, b, load_at[name]).start()

    def loaded(*names):
        for name in names:
            pltpu.make_async_copy(whole[name], whole[name], load_at[name]).wait()

    counting = (s == last) & (c == 1)
    at_end = (me == 0) | (me == n - 1)
    load_start(pairs[:8])

    @pl.when(jnp.logical_not(counting))
    def _():
        load_start(pairs[8:])

    loaded("boxes", "counts")
    row = lax.broadcasted_iota(jnp.int32, (cells, 128), 0)
    row_h, row_w = row // side, row % side
    masks = []
    for crop in range(crops):
        inside = jnp.zeros((cells, 128), f32)
        for r in range(slots):
            hit = ((row_h >= boxes_ref[crop, 0, r]) & (row_h < boxes_ref[crop, 1, r])
                   & (row_w >= boxes_ref[crop, 2, r]) & (row_w < boxes_ref[crop, 3, r])
                   & (counts_ref[0, crop] > r))
            inside = jnp.where(hit, 1.0, inside)
        masks.append(inside)
    mask = jnp.concatenate(masks, axis=0)
    cnt[me] = jnp.broadcast_to(jnp.sum(mask, axis=0, keepdims=True), (8, 128))

    pl.semaphore_wait(barrier, n + jnp.where(s > 0, 1, 0) + jnp.where(s < last, 1, 0)
                      + jnp.where(counting, n - 1, 0))

    cnt_copies = [Spread(0, lambda to: cnt.at[me], cnt.at[me], cnt.at[peers], at, {"chan": core})
                  for core, at in ((0, 0), (1, 4))]

    @pl.when(counting)
    def _():
        for copies in cnt_copies:
            copies.start()
        load_start(pairs[8:])

    wr_copy = remote(wr_ref.at[pl.ds(pl.multiple_of(other * half, half), half)], wr_peer,
                     core_send.at[0], core_recv.at[0], {"chan": other})
    loaded("second")
    sec_all[me] = jnp.maximum(second_ref[...], 0)
    sec_moves = [[line(step, lambda j, q=q: sec_all.at[j, pl.ds(q * hrows, hrows)],
                       sec_send.at[step, q], sec_recv.at[step, q])
                  for q in range(2)] for step in range(n - 1)]
    if n > 1:
        for q in range(2):
            line_start(sec_moves[0][q])
    loaded("pair")
    for j in range(n):
        bi_send[j] = bi_ref[:, j * share : (j + 1) * share]
    bi_all[me, mine] = bi_send[me, mine]

    bi_copies = Spread(1, lambda to: bi_send.at[to, mine], bi_all.at[me, mine],
                       bi_all.at[peers, mine])
    bi_share = share_copy(0, bi_all)

    def sec_forward(step):
        for q in range(2):
            line_forward(sec_moves[step][q], sec_moves[step + 1][q])

    def bi_forward():
        bi_copies.wait_recv()
        bi_share.start()

    pair = gw * gw
    iota = lambda shape, dim: lax.broadcasted_iota(jnp.int32, shape, dim)
    same = iota((blk, blk), 0) // gw == iota((blk, blk), 1) // gw

    def build_taps():
        same_out = iota((width, pair), 0) % gw == iota((width, pair), 1) % gw
        spread = (iota((pair, blk), 0) // gw == iota((pair, blk), 1) % gw).astype(f32).astype(bf16)
        inside = iota((width, blk), 0) // gw % (blk // gw) == iota((width, blk), 1) // gw
        by_group = wg_ref[...].astype(f32).T
        for t in range(9):
            values = by_group[:, t * pair : (t + 1) * pair]
            values = jnp.broadcast_to(values[:, None, :], (groups, gw, pair)).reshape(width, pair)
            values = jnp.where(same_out, values, 0.0).astype(bf16)
            taps[t] = jnp.where(inside, dot_nn(values, spread), 0.0).astype(bf16)

    def shifter(count):
        prow = lax.broadcasted_iota(jnp.int32, (count, blk), 0)
        p_w = prow % side
        p_h = (prow // side) % side

        def moved(x, a, b):
            shift = (side * a + b) % count
            if shift:
                x = pltpu.roll(x, shift, 0)
            if a:
                x = jnp.where(p_h >= 1 if a == 1 else p_h < side - 1, x, 0.0)
            if b:
                x = jnp.where(p_w >= 1 if b == 1 else p_w < side - 1, x, 0.0)
            return x

        return moved

    def prepare_first():
        moved = shifter(rows)
        for b in range(blocks):
            first = jnp.maximum(first_ref[:, b * blk : (b + 1) * blk], 0).astype(f32)
            for t, (da, db) in enumerate(tap_offsets):
                ft[t, b] = moved(first, -da, -db).T.astype(bf16)

    hop_copies = [
        remote(ng.at[c, crop_rows[q]], inc.at[c, crop_rows[q]],
               hop_send.at[q], hop_recv.at[q], {"section": lax.max(s - 1, 0)})
        for q in range(2)
    ]
    fwd_copies = [
        remote(inc.at[c, crop_rows[q]], inc.at[c, crop_rows[q]],
               fwd_send.at[q], fwd_recv.at[q], {"chan": other})
        for q in range(2)
    ]

    @pl.when(s == last)
    def _():
        loaded("wl", "teacher")
        feature = jnp.maximum(out_ref[...], 0)
        lateral = dot_nn(feature, wl_ref[...])
        error = (mask[:, 0:1] * (lateral - teacher_ref[...].astype(f32))).astype(bf16)
        imitation = dot_nt(error, wl_ref[...])
        loaded("wg")
        build_taps()
        loaded("top", "first", "we", "wr")
        wr_copy.start()
        cnt_copies[0].wait_recv()
        bi_copies.start()
        covered = cnt[0]
        for j in range(1, n):
            covered = covered + cnt[j]
        scale = (imitation_weight * pixels) / covered[0:1, 0:1]
        start = (top_ref[...].astype(f32) + imitation * scale).astype(bf16)
        start = jnp.where(out_ref[...] > 0, start, jnp.zeros_like(start))
        pas[0] = start[:, :half]
        pas[1] = start[:, half:]

    @pl.when(s < last)
    def _():
        loaded("wl", "teacher", "wg", "top", "first", "we", "wr")
        wr_copy.start()
        build_taps()
        prepare_first()
        pl.when(at_end)(bi_copies.start)
        for step in range(n - 2):
            sec_forward(step)
        pl.when(jnp.logical_not(at_end))(bi_copies.start)

    ps_copies = Spread(2, lambda to: ps_send.at[to, mine], ps_all.at[me, mine],
                       ps_all.at[peers, mine])
    ps_share = share_copy(1, ps_all)
    d_moves = [[line(step, lambda j, q=q: d_all.at[j, crop_rows[q]], d_send.at[step, q],
                     d_recv.at[step, q]) for q in range(2)] for step in range(n - 1)]
    dfx_copies = [remote(d_all.at[me, crop_rows[q]], dfx.at[crop_rows[q]], core_send.at[1 + q],
                         core_recv.at[1 + q], {"chan": other}) for q in range(2)]
    ng_copy = remote(ng.at[c], ng.at[c], core_send.at[3], core_recv.at[3], {"chan": other})

    def gate_half(h, q):
        at = pl.ds(pl.multiple_of(h * half, half), half)
        value = inc[h, crop_rows[q]]
        gate = out_ref[q * hrows : (q + 1) * hrows, at] > 0
        pas[h, crop_rows[q]] = jnp.where(gate, value, jnp.zeros_like(value))

    def own_arrives(q, where=None):
        @pl.when((s < last) & where if where is not None else s < last)
        def _():
            hop_copies[q].wait_recv()
            fwd_copies[q].start()
            gate_half(c, q)

    def other_arrives(q):
        @pl.when(s < last)
        def _():
            fwd_copies[q].wait_recv()
            gate_half(other, q)

    moved = shifter(hrows)
    own_arrives(0)
    for q in range(2):
        top, end = q * hrows, (q + 1) * hrows
        second_full = dot_nt(pas[c, top:end], we_ref[c])
        if q == 0:
            own_arrives(1, c == 1)
        other_arrives(q)
        for j in range(n):
            at = (j * share) // half
            ps_send[j, top:end] = pas[at, top:end, j * share - at * half : (j + 1) * share - at * half]

        @pl.when(c == q)
        def _():
            ps_all[me, top:end] = ps_send[me, top:end]
            ps_copies.start()

        second_full = second_full + dot_nt(pas[other, top:end], we_ref[other])
        for b in range(blocks):
            lo, hi = b * blk, (b + 1) * blk
            lhs = jnp.where(second_ref[top:end, lo:hi] > 0, second_full[:, lo:hi], 0.0).astype(bf16)
            ds[top:end, lo:hi] = lhs
            total = None
            for db in (-1, 0, 1):
                column = None
                for da in (-1, 0, 1):
                    t = 3 * (da + 1) + db + 1
                    y = moved(dot_nn(lhs, taps[t, lo:hi, :]), da, 0)
                    column = y if column is None else column + y
                column = moved(column, 0, db)
                total = column if total is None else total + column
            d_all[me, top:end, lo:hi] = jnp.where(
                first_ref[top:end, lo:hi] > 0, total, 0.0).astype(bf16)
            if q == 0 and b == 0:
                own_arrives(1, c == 0)
        dfx_copies[q].start()
        if n > 1:
            @pl.when(s < last)
            def _():
                line_start(d_moves[0][q])

    own_rows = pl.ds(pl.multiple_of(c * half, half), half)
    wr_copy.wait_recv()
    for q in range(2):
        top, end = q * hrows, (q + 1) * hrows
        grad = dot_nt(d_all[me, top:end], wr_ref[own_rows, :]) + pas[c, top:end].astype(f32)
        dfx_copies[q].wait_recv()
        ng[c, top:end] = (grad + dot_nt(dfx[top:end], wr_peer[...])).astype(bf16)

        @pl.when(s > 0)
        def _():
            hop_copies[q].start()

    ng_copy.start()

    @pl.when(s == last)
    def _():
        prepare_first()

    gf[...] = jnp.zeros_like(gf)
    for b in range(blocks):
        rhs = ds[:, b * blk : (b + 1) * blk]
        for t in range(9):
            dense = jnp.where(same, dot_nn(ft[t, b], rhs), 0.0)
            folded = jnp.sum(dense.reshape(blk // gw, gw, blk), axis=0)
            for j in range(n):
                gf[j, t * k : (t + 1) * k, b * blk : (b + 1) * blk] = folded[j * k : (j + 1) * k]
    g_send[...] = gf[...].astype(bf16)
    def g_copy(part, dst, recv, where):
        return remote(g_send.at[part], dst, dp_send.at[3], recv, {"dp": where})

    relayed = n > 3
    ends = ((0, 1, me >= 2), (n - 1, n - 2, me <= n - 3))

    def g_start(relayed):
        for step in range(1, n):
            to = lax.rem(me + step, n)
            direct = (to != 0) & (to != n - 1) if relayed else to >= 0

            @pl.when(direct)
            def _():
                g_copy(to, g_recv.at[me], dp_recv.at[3], to).start()

        if relayed:
            for i, (end, by, far) in enumerate(ends):
                @pl.when(far)
                def _():
                    g_copy(end, g_far.at[i, me], far_recv.at[i], by).start()

    def g_relay():
        for i, (end, by, _) in enumerate(ends):
            @pl.when(me == by)
            def _():
                others = pl.ds(2 if end == 0 else 0, n - 2)
                arrived = g_far.at[i, others]
                pltpu.make_async_copy(arrived, arrived, far_recv.at[i]).wait()
                total = gf[end]
                for j in range(n - 2):
                    total = total + g_far[i, j + (2 if end == 0 else 0)].astype(f32)
                g_send[end] = total.astype(bf16)
                g_copy(end, g_recv.at[me], dp_recv.at[3], end).start()

    def g_wait(sem, count):
        some = g_recv.at[pl.ds(0, count)]
        pltpu.make_async_copy(some, some, sem).wait()

    if n > 1:
        @pl.when(s == last)
        def _():
            for q in range(2):
                line_start(d_moves[0][q])

    def d_forward(step):
        for q in range(2):
            line_forward(d_moves[step][q], d_moves[step + 1][q])

    for step in range(n - 2):
        @pl.when(s == last)
        def _():
            sec_forward(step)
            if step == 0:
                bi_forward()

        d_forward(step)

        @pl.when(s == last)
        def _():
            if step == 0:
                g_start(relayed)

        if step == 0:
            @pl.when(s < last)
            def _():
                bi_forward()

            ps_copies.wait_recv()
            ps_share.start()

            ng_copy.wait_recv()
            grads_ref[:, :half] = ng[0]
            grads_ref[:, half:] = ng[1]
    @pl.when((s < last) & jnp.logical_not(at_end))
    def _():
        g_start(False)

    if relayed:
        pl.when(s == last)(g_relay)

    for q in range(2):
        line_finish([step_moves[q] for step_moves in sec_moves])
    ps_share.wait_recv()
    expand = dot_tn(sec_all[...].reshape(n * rows, width), ps_all[...].reshape(n * rows, share))
    expand_ref[...] = expand * norm

    @pl.when((s < last) & at_end)
    def _():
        g_start(False)

    bi_share.wait_recv()

    def reduce_crop(q):
        line_finish([step_moves[q] for step_moves in d_moves])
        bi_rows = bi_all[:, q * hrows : (q + 1) * hrows].reshape(n * hrows, share)
        d_rows = d_all[:, q * hrows : (q + 1) * hrows].reshape(n * hrows, width)
        reduced = dot_tn(bi_rows, d_rows) * norm
        reduce_ref[...] = reduced if q == 0 else reduce_ref[...] + reduced

    reduce_crop(0)
    reduce_crop(1)
    if relayed:
        @pl.when(at_end & (s == last))
        def _():
            for j in range(n):
                if 0 < j < n - 1:
                    @pl.when((me == 0) & (j != 1) | (me == n - 1) & (j != n - 2))
                    def _():
                        g_recv[j] = jnp.zeros(g_recv.shape[1:], bf16)
                else:
                    g_recv[j] = jnp.zeros(g_recv.shape[1:], bf16)
            g_wait(dp_recv.at[3], 1)

        @pl.when(jnp.logical_not(at_end & (s == last)))
        def _():
            g_recv[me] = jnp.zeros(g_recv.shape[1:], bf16)
            g_wait(dp_recv.at[3], n - 1)
    else:
        g_recv[me] = jnp.zeros(g_recv.shape[1:], bf16)
        g_wait(dp_recv.at[3], n - 1)
    total = gf[me]
    for j in range(n):
        total = total + g_recv[j].astype(f32)
    total = (total * norm)[: 9 * k]
    wide = jnp.broadcast_to(total[:, None, :], (9 * k, gw, width)).reshape(9 * k * gw, width)
    out_of = iota((9 * k * gw, width), 0) % gw == iota((9 * k * gw, width), 1) % gw
    wide = jnp.where(out_of, wide, 0.0)
    high = wide.astype(bf16)
    low = (wide - high.astype(f32)).astype(bf16)
    group_of = (iota((width, groups), 0) // gw == iota((width, groups), 1)).astype(f32).astype(bf16)
    group_ref[...] = dot_nn(high, group_of) + dot_nn(low, group_of)

    for move in [move for step_moves in sec_moves + d_moves for move in step_moves]:
        for copy, sends, _ in move:
            pl.when(sends)(copy.wait_send)
    g_wait(dp_send.at[3], n - 1)
    for copy in [bi_share, ps_share, bi_copies, ps_copies, wr_copy, ng_copy] + dfx_copies:
        copy.wait_send()

    @pl.when(counting)
    def _():
        for copies in cnt_copies:
            copies.wait_send()

    @pl.when(s > 0)
    def _():
        for copy in hop_copies:
            copy.wait_send()

    @pl.when(s < last)
    def _():
        for copy in fwd_copies:
            copy.wait_send()


def store_kernel(*refs):
    count = (len(refs) - 1) // 2
    copies = [pltpu.make_async_copy(refs[i], refs[count + i], refs[-1].at[i]) for i in range(count)]
    for copy in copies:
        copy.start()
    for copy in copies:
        copy.wait()


def on_device(
    block_inputs, out_pre, first_pre, second_pre, w_reduce, w_group, w_expand, w_lateral,
    teacher, top_grad, boxes, region_counts,
):
    n = lax.axis_size("dp")
    sections = lax.axis_size("section")
    crops, side, _, channels = top_grad.shape
    rows = crops * side * side
    width = first_pre.shape[4]
    lateral_width = w_lateral.shape[1]
    groups, gw = w_group.shape[2], w_group.shape[3]
    slots = boxes.shape[1]
    pixels = rows * n
    share = channels // n
    k = gw // n
    grows = -(-9 * k // 8) * 8
    half = channels // 2
    blk = min(256, width)
    hbm = pl.BlockSpec(memory_space=pltpu.HBM)
    vmem = pl.BlockSpec(memory_space=pltpu.VMEM)
    dma = pltpu.SemaphoreType.DMA
    peers = max(n - 1, 1)
    shapes = (
        ((rows, channels), bf16), ((share, width), f32),
        ((9 * k * gw, groups), f32), ((width, share), f32),
    )
    results = pl.pallas_call(
        functools.partial(kernel, (n, sections, crops, side, slots, pixels)),
        out_shape=tuple(pltpu.VMEM(shape, kind) for shape, kind in shapes),
        in_specs=[hbm] * 12,
        out_specs=(vmem,) * 4,
        scratch_shapes=[
            pltpu.SMEM((crops, 4, slots), jnp.int32),
            pltpu.SMEM((1, crops), jnp.int32),
            pltpu.VMEM((3, rows, channels), bf16),
            pltpu.VMEM((2, rows, width), bf16),
            pltpu.VMEM((channels, width), bf16),
            pltpu.VMEM((9 * gw * gw, groups), bf16),
            pltpu.VMEM((2, width, half), bf16),
            pltpu.VMEM((channels, lateral_width), bf16),
            pltpu.VMEM((rows, lateral_width), bf16),
            dma((11,)),
            pltpu.VMEM((2, rows, half), bf16),
            pltpu.VMEM((2, rows, half), bf16),
            pltpu.VMEM((half, width), bf16),
            pltpu.VMEM((rows, width), bf16),
            pltpu.VMEM((2, rows, half), bf16),
            pltpu.VMEM((rows, width), bf16),
            pltpu.VMEM((n, rows, width), bf16),
            pltpu.VMEM((n, rows, width), bf16),
            pltpu.VMEM((n, rows, share), bf16),
            pltpu.VMEM((n, rows, share), bf16),
            pltpu.VMEM((n, rows, share), bf16),
            pltpu.VMEM((n, rows, share), bf16),
            pltpu.VMEM((n, grows, width), f32),
            pltpu.VMEM((n, grows, width), bf16),
            pltpu.VMEM((n, grows, width), bf16),
            pltpu.VMEM((2, n, grows, width), bf16),
            dma((2,)),
            pltpu.VMEM((n, 8, 128), f32),
            pltpu.VMEM((9, width, blk), bf16),
            pltpu.VMEM((9, width // blk, blk, rows), bf16),
            dma((5,)), dma((4,)), dma((4,)), dma((4,)),
            dma((2,)), dma((2,)), dma((2,)), dma((2,)),
            dma((peers, 2, 2)), dma((peers, 2, 2)), dma((peers, 2, 2)), dma((peers, 2, 2)),
            dma((2,)), dma((2,)),
        ],
        compiler_params=pltpu.CompilerParams(
            collective_id=0, has_side_effects=True, vmem_limit_bytes=44 << 20,
        ),
    )(*(pltpu.with_memory_space_constraint(x, pltpu.HBM) for x in (
        boxes.transpose(0, 2, 1), region_counts.reshape(1, crops),
        block_inputs.reshape(rows, channels), out_pre.reshape(rows, channels),
        first_pre.reshape(rows, width), second_pre.reshape(rows, width),
        w_reduce[0], w_group[0].transpose(0, 2, 3, 1).reshape(9 * gw * gw, groups), w_expand[0], w_lateral,
        teacher.reshape(rows, lateral_width), top_grad.reshape(rows, channels),
    )))
    grads, reduced, group, expand = pl.pallas_call(
        store_kernel,
        out_shape=tuple(jax.ShapeDtypeStruct(shape, kind) for shape, kind in shapes),
        in_specs=[vmem] * 4,
        out_specs=(hbm,) * 4,
        scratch_shapes=[dma((4,))],
    )(*(pltpu.with_memory_space_constraint(x, pltpu.VMEM) for x in results))
    group = group.reshape(9, k, gw, groups).transpose(0, 3, 1, 2)
    return (
        grads.reshape(1, crops, side, side, channels), reduced[None], group[None], expand[None],
    )


def solution(mesh):
    return jax.shard_map(
        on_device,
        mesh=mesh,
        in_specs=(
            P("section", ("parts", "dp"), None, None, None),
            P("section", ("parts", "dp"), None, None, None),
            P("section", ("parts", "dp"), None, None, "chan"),
            P("section", ("parts", "dp"), None, None, "chan"),
            P("section", None, "chan"),
            P("section", None, "chan", None, None),
            P("section", "chan", None),
            P(),
            P(("parts", "dp"), None, None, None),
            P(("parts", "dp"), None, None, None),
            P(("parts", "dp"), None, None),
            P(("parts", "dp")),
        ),
        out_specs=(
            P("section", ("parts", "dp"), None, None, None),
            P(("parts", "section"), "dp", "chan"),
            P(("parts", "section"), None, "chan", "dp", None),
            P(("parts", "section"), "chan", "dp"),
        ),
        check_vma=False,
    )
```

```python
import functools
import math

import jax
import jax.numpy as jnp
from jax import lax
from jax.experimental import pallas as pl
from jax.experimental.pallas import tpu as pltpu
from jax.sharding import PartitionSpec as P

imitation_weight = 0.5
tap_offsets = [(tap // 3 - 1, tap % 3 - 1) for tap in range(9)]
f32 = jnp.float32
bf16 = jnp.bfloat16


def dot_nn(a, b):
    return lax.dot_general(a, b, (((1,), (0,)), ((), ())), preferred_element_type=f32)


def dot_nt(a, b):
    return lax.dot_general(a, b, (((1,), (1,)), ((), ())), preferred_element_type=f32)


def dot_tn(a, b):
    return lax.dot_general(a, b, (((0,), (0,)), ((), ())), preferred_element_type=f32)


def kernel(
    dims,
    boxes_hbm, counts_hbm, bi_hbm, out_hbm, first_hbm, second_hbm, wr_hbm, wg_hbm, we_hbm,
    wl_hbm, teacher_hbm, top_hbm,
    grads_ref, reduce_ref, group_ref, expand_ref,
    boxes_ref, counts_ref,
    full_ref, part_ref, wr_ref, wg_ref, we_ref, wl_ref, teacher_ref, load_sem,
    inc, pas, wr_peer, dfx, ng, ds, d_all, sec_all, bi_send, bi_all, ps_send, ps_all,
    gf, g_send, g_recv, g_far, far_recv, cnt, taps, ft,
    dp_send, dp_recv, core_send, core_recv, hop_send, hop_recv, fwd_send, fwd_recv,
    sec_send, sec_recv, d_send, d_recv, share_send, share_recv,
):
    n, sections, crops, side, slots, pixels = dims
    out_ref, bi_ref, top_ref = (full_ref.at[i] for i in range(3))
    first_ref, second_ref = part_ref.at[0], part_ref.at[1]
    rows, channels = bi_ref.shape
    half = channels // 2
    width = first_ref.shape[1]
    groups = wg_ref.shape[1]
    gw = width // groups
    blk = taps.shape[2]
    blocks = width // blk
    cells = side * side
    share = channels // n
    k = gw // n
    hrows = rows // 2
    me = lax.axis_index("dp")
    s = lax.axis_index("section")
    c = lax.axis_index("chan")
    other = 1 - c
    last = sections - 1
    norm = 1.0 / math.sqrt(pixels)

    def remote(src, dst, send, recv, where):
        return pltpu.make_async_remote_copy(
            src_ref=src, dst_ref=dst, send_sem=send, recv_sem=recv,
            device_id=where, device_id_type=pl.DeviceIdType.MESH,
        )

    class Spread:
        def __init__(self, what, src_of, dst, moved, at=None, where={}):
            at = what if at is None else at
            self.copies = [
                remote(src_of(to), dst, dp_send.at[at], dp_recv.at[what], {"dp": to, **where})
                for to in (lax.rem(me + step, n) for step in range(1, n))
            ]
            self.sent = pltpu.make_async_copy(moved, moved, dp_send.at[at])
            self.received = pltpu.make_async_copy(moved, moved, dp_recv.at[what])

        def start(self):
            for copy in self.copies:
                copy.start()

        def wait_recv(self):
            self.received.wait()

        def wait_send(self):
            self.sent.wait()

    mine = pl.ds(pl.multiple_of(c * hrows, hrows), hrows)
    peers = pl.ds(0, n - 1)
    crop_rows = [pl.ds(q * hrows, hrows) for q in range(2)]

    def share_copy(which, buf):
        return remote(buf.at[:, mine], buf.at[:, mine], share_send.at[which],
                      share_recv.at[which], {"chan": other})

    def line(step, block, send, recv):
        ahead = block(lax.max(me - step, 0))
        behind = block(lax.min(me + step, n - 1))
        right = remote(ahead, ahead, send.at[0], recv.at[0], {"dp": lax.min(me + 1, n - 1)})
        left = remote(behind, behind, send.at[1], recv.at[1], {"dp": lax.max(me - 1, 0)})
        return (
            (right, (me - step >= 0) & (me + 1 < n), me - 1 - step >= 0),
            (left, (me + step < n) & (me >= 1), me + 1 + step < n),
        )

    def line_start(moves):
        for copy, sends, _ in moves:
            pl.when(sends)(copy.start)

    def line_forward(moves, following):
        for (copy, _, receives), (onward, sends, _) in zip(moves, following):
            @pl.when(receives & sends)
            def _():
                copy.wait_recv()
                onward.start()

    def line_settle(moves, following):
        for (copy, _, receives), (_, sends, _) in zip(moves, following):
            pl.when(receives & jnp.logical_not(sends))(copy.wait_recv)

    def line_finish(moves):
        for step in range(n - 1):
            if step == n - 2:
                for copy, _, receives in moves[step]:
                    pl.when(receives)(copy.wait_recv)
            else:
                line_settle(moves[step], moves[step + 1])

    barrier = pltpu.get_barrier_semaphore()
    mesh_type = pl.DeviceIdType.MESH
    for step in range(1, n):
        pl.semaphore_signal(barrier, inc=1, device_id={"dp": lax.rem(me + step, n)},
                            device_id_type=mesh_type)
    pl.semaphore_signal(barrier, inc=1, device_id={"chan": other}, device_id_type=mesh_type)

    @pl.when((s == last) & (c == 0))
    def _():
        for step in range(1, n):
            pl.semaphore_signal(barrier, inc=1, device_id_type=mesh_type,
                                device_id={"dp": lax.rem(me + step, n), "chan": other})

    @pl.when(s > 0)
    def _():
        pl.semaphore_signal(barrier, inc=1, device_id={"section": s - 1},
                            device_id_type=mesh_type)

    @pl.when(s < last)
    def _():
        pl.semaphore_signal(barrier, inc=1, device_id={"section": s + 1},
                            device_id_type=mesh_type)

    pairs = (
        ("boxes", boxes_hbm, boxes_ref), ("counts", counts_hbm, counts_ref),
        ("second", second_hbm, second_ref), ("pair", out_hbm, out_ref), ("wl", wl_hbm, wl_ref),
        ("teacher", teacher_hbm, teacher_ref), ("pair", bi_hbm, bi_ref),
        ("wg", wg_hbm, wg_ref), ("top", top_hbm, top_ref), ("we", we_hbm.at[:, :half], we_ref.at[0]),
        ("we", we_hbm.at[:, half:], we_ref.at[1]), ("first", first_hbm, first_ref),
        ("wr", wr_hbm, wr_ref),
    )
    whole = {
        "boxes": boxes_ref, "counts": counts_ref, "pair": full_ref.at[0:2], "top": top_ref,
        "first": first_ref, "second": second_ref, "wl": wl_ref, "teacher": teacher_ref,
        "wg": wg_ref, "we": we_ref, "wr": wr_ref,
    }
    load_at = {name: load_sem.at[i] for i, name in enumerate(whole)}

    def load_start(some):
        for name, a, b in some:
            pltpu.make_async_copy(a, b, load_at[name]).start()

    def loaded(*names):
        for name in names:
            pltpu.make_async_copy(whole[name], whole[name], load_at[name]).wait()

    counting = (s == last) & (c == 1)
    at_end = (me == 0) | (me == n - 1)
    load_start(pairs[:8])

    @pl.when(jnp.logical_not(counting))
    def _():
        load_start(pairs[8:])

    loaded("boxes", "counts")
    row = lax.broadcasted_iota(jnp.int32, (cells, 128), 0)
    row_h, row_w = row // side, row % side
    masks = []
    for crop in range(crops):
        inside = jnp.zeros((cells, 128), f32)
        for r in range(slots):
            hit = ((row_h >= boxes_ref[crop, 0, r]) & (row_h < boxes_ref[crop, 1, r])
                   & (row_w >= boxes_ref[crop, 2, r]) & (row_w < boxes_ref[crop, 3, r])
                   & (counts_ref[0, crop] > r))
            inside = jnp.where(hit, 1.0, inside)
        masks.append(inside)
    mask = jnp.concatenate(masks, axis=0)
    cnt[me] = jnp.broadcast_to(jnp.sum(mask, axis=0, keepdims=True), (8, 128))

    pl.semaphore_wait(barrier, n + jnp.where(s > 0, 1, 0) + jnp.where(s < last, 1, 0)
                      + jnp.where(counting, n - 1, 0))

    cnt_copies = [Spread(0, lambda to: cnt.at[me], cnt.at[me], cnt.at[peers], at, {"chan": core})
                  for core, at in ((0, 0), (1, 4))]

    @pl.when(counting)
    def _():
        for copies in cnt_copies:
            copies.start()
        load_start(pairs[8:])

    wr_copy = remote(wr_ref.at[pl.ds(pl.multiple_of(other * half, half), half)], wr_peer,
                     core_send.at[0], core_recv.at[0], {"chan": other})
    loaded("second")
    sec_all[me] = jnp.maximum(second_ref[...], 0)
    sec_moves = [[line(step, lambda j, q=q: sec_all.at[j, pl.ds(q * hrows, hrows)],
                       sec_send.at[step, q], sec_recv.at[step, q])
                  for q in range(2)] for step in range(n - 1)]
    if n > 1:
        for q in range(2):
            line_start(sec_moves[0][q])
    loaded("pair")
    for j in range(n):
        bi_send[j] = bi_ref[:, j * share : (j + 1) * share]
    bi_all[me, mine] = bi_send[me, mine]

    bi_copies = Spread(1, lambda to: bi_send.at[to, mine], bi_all.at[me, mine],
                       bi_all.at[peers, mine])
    bi_share = share_copy(0, bi_all)

    def sec_forward(step):
        for q in range(2):
            line_forward(sec_moves[step][q], sec_moves[step + 1][q])

    def bi_forward():
        bi_copies.wait_recv()
        bi_share.start()

    pair = gw * gw
    iota = lambda shape, dim: lax.broadcasted_iota(jnp.int32, shape, dim)
    same = iota((blk, blk), 0) // gw == iota((blk, blk), 1) // gw

    def build_taps():
        same_out = iota((width, pair), 0) % gw == iota((width, pair), 1) % gw
        spread = (iota((pair, blk), 0) // gw == iota((pair, blk), 1) % gw).astype(f32).astype(bf16)
        inside = iota((width, blk), 0) // gw % (blk // gw) == iota((width, blk), 1) // gw
        by_group = wg_ref[...].astype(f32).T
        for t in range(9):
            values = by_group[:, t * pair : (t + 1) * pair]
            values = jnp.broadcast_to(values[:, None, :], (groups, gw, pair)).reshape(width, pair)
            values = jnp.where(same_out, values, 0.0).astype(bf16)
            taps[t] = jnp.where(inside, dot_nn(values, spread), 0.0).astype(bf16)

    def shifter(count):
        prow = lax.broadcasted_iota(jnp.int32, (count, blk), 0)
        p_w = prow % side
        p_h = (prow // side) % side

        def moved(x, a, b):
            shift = (side * a + b) % count
            if shift:
                x = pltpu.roll(x, shift, 0)
            if a:
                x = jnp.where(p_h >= 1 if a == 1 else p_h < side - 1, x, 0.0)
            if b:
                x = jnp.where(p_w >= 1 if b == 1 else p_w < side - 1, x, 0.0)
            return x

        return moved

    def prepare_first():
        moved = shifter(rows)
        for b in range(blocks):
            first = jnp.maximum(first_ref[:, b * blk : (b + 1) * blk], 0).astype(f32)
            for t, (da, db) in enumerate(tap_offsets):
                ft[t, b] = moved(first, -da, -db).T.astype(bf16)

    hop_copies = [
        remote(ng.at[c, crop_rows[q]], inc.at[c, crop_rows[q]],
               hop_send.at[q], hop_recv.at[q], {"section": lax.max(s - 1, 0)})
        for q in range(2)
    ]
    fwd_copies = [
        remote(inc.at[c, crop_rows[q]], inc.at[c, crop_rows[q]],
               fwd_send.at[q], fwd_recv.at[q], {"chan": other})
        for q in range(2)
    ]

    @pl.when(s == last)
    def _():
        loaded("wl", "teacher")
        feature = jnp.maximum(out_ref[...], 0)
        lateral = dot_nn(feature, wl_ref[...])
        error = (mask[:, 0:1] * (lateral - teacher_ref[...].astype(f32))).astype(bf16)
        imitation = dot_nt(error, wl_ref[...])
        loaded("wg")
        build_taps()
        loaded("top", "first", "we", "wr")
        wr_copy.start()
        cnt_copies[0].wait_recv()
        bi_copies.start()
        covered = cnt[0]
        for j in range(1, n):
            covered = covered + cnt[j]
        scale = (imitation_weight * pixels) / covered[0:1, 0:1]
        start = (top_ref[...].astype(f32) + imitation * scale).astype(bf16)
        start = jnp.where(out_ref[...] > 0, start, jnp.zeros_like(start))
        pas[0] = start[:, :half]
        pas[1] = start[:, half:]

    @pl.when(s < last)
    def _():
        loaded("wl", "teacher", "wg", "top", "first", "we", "wr")
        wr_copy.start()
        build_taps()
        prepare_first()
        pl.when(at_end)(bi_copies.start)
        for step in range(n - 2):
            sec_forward(step)
        pl.when(jnp.logical_not(at_end))(bi_copies.start)

    ps_copies = Spread(2, lambda to: ps_send.at[to, mine], ps_all.at[me, mine],
                       ps_all.at[peers, mine])
    ps_share = share_copy(1, ps_all)
    d_moves = [[line(step, lambda j, q=q: d_all.at[j, crop_rows[q]], d_send.at[step, q],
                     d_recv.at[step, q]) for q in range(2)] for step in range(n - 1)]
    dfx_copies = [remote(d_all.at[me, crop_rows[q]], dfx.at[crop_rows[q]], core_send.at[1 + q],
                         core_recv.at[1 + q], {"chan": other}) for q in range(2)]
    ng_copy = remote(ng.at[c], ng.at[c], core_send.at[3], core_recv.at[3], {"chan": other})

    def gate_half(h, q):
        at = pl.ds(pl.multiple_of(h * half, half), half)
        value = inc[h, crop_rows[q]]
        gate = out_ref[q * hrows : (q + 1) * hrows, at] > 0
        pas[h, crop_rows[q]] = jnp.where(gate, value, jnp.zeros_like(value))

    def own_arrives(q, where=None):
        @pl.when((s < last) & where if where is not None else s < last)
        def _():
            hop_copies[q].wait_recv()
            fwd_copies[q].start()
            gate_half(c, q)

    def other_arrives(q):
        @pl.when(s < last)
        def _():
            fwd_copies[q].wait_recv()
            gate_half(other, q)

    moved = shifter(hrows)
    own_arrives(0)
    for q in range(2):
        top, end = q * hrows, (q + 1) * hrows
        second_full = dot_nt(pas[c, top:end], we_ref[c])
        if q == 0:
            own_arrives(1, c == 1)
        other_arrives(q)
        for j in range(n):
            at = (j * share) // half
            ps_send[j, top:end] = pas[at, top:end, j * share - at * half : (j + 1) * share - at * half]

        @pl.when(c == q)
        def _():
            ps_all[me, top:end] = ps_send[me, top:end]
            ps_copies.start()

        second_full = second_full + dot_nt(pas[other, top:end], we_ref[other])
        for b in range(blocks):
            lo, hi = b * blk, (b + 1) * blk
            lhs = jnp.where(second_ref[top:end, lo:hi] > 0, second_full[:, lo:hi], 0.0).astype(bf16)
            ds[top:end, lo:hi] = lhs
            total = None
            for db in (-1, 0, 1):
                column = None
                for da in (-1, 0, 1):
                    t = 3 * (da + 1) + db + 1
                    y = moved(dot_nn(lhs, taps[t, lo:hi, :]), da, 0)
                    column = y if column is None else column + y
                column = moved(column, 0, db)
                total = column if total is None else total + column
            d_all[me, top:end, lo:hi] = jnp.where(
                first_ref[top:end, lo:hi] > 0, total, 0.0).astype(bf16)
            if q == 0 and b == 0:
                own_arrives(1, c == 0)
        dfx_copies[q].start()
        if n > 1:
            @pl.when(s < last)
            def _():
                line_start(d_moves[0][q])

    own_rows = pl.ds(pl.multiple_of(c * half, half), half)
    wr_copy.wait_recv()
    for q in range(2):
        top, end = q * hrows, (q + 1) * hrows
        grad = dot_nt(d_all[me, top:end], wr_ref[own_rows, :]) + pas[c, top:end].astype(f32)
        dfx_copies[q].wait_recv()
        ng[c, top:end] = (grad + dot_nt(dfx[top:end], wr_peer[...])).astype(bf16)

        @pl.when(s > 0)
        def _():
            hop_copies[q].start()

    ng_copy.start()

    @pl.when(s == last)
    def _():
        prepare_first()

    gf[...] = jnp.zeros_like(gf)
    for b in range(blocks):
        rhs = ds[:, b * blk : (b + 1) * blk]
        for t in range(9):
            dense = jnp.where(same, dot_nn(ft[t, b], rhs), 0.0)
            folded = jnp.sum(dense.reshape(blk // gw, gw, blk), axis=0)
            for j in range(n):
                gf[j, t * k : (t + 1) * k, b * blk : (b + 1) * blk] = folded[j * k : (j + 1) * k]
    g_send[...] = gf[...].astype(bf16)
    def g_copy(part, dst, recv, where):
        return remote(g_send.at[part], dst, dp_send.at[3], recv, {"dp": where})

    relayed = n > 3
    ends = ((0, 1, me >= 2), (n - 1, n - 2, me <= n - 3))

    def g_start(relayed):
        for step in range(1, n):
            to = lax.rem(me + step, n)
            direct = (to != 0) & (to != n - 1) if relayed else to >= 0

            @pl.when(direct)
            def _():
                g_copy(to, g_recv.at[me], dp_recv.at[3], to).start()

        if relayed:
            for i, (end, by, far) in enumerate(ends):
                @pl.when(far)
                def _():
                    g_copy(end, g_far.at[i, me], far_recv.at[i], by).start()

    def g_relay():
        for i, (end, by, _) in enumerate(ends):
            @pl.when(me == by)
            def _():
                others = pl.ds(2 if end == 0 else 0, n - 2)
                arrived = g_far.at[i, others]
                pltpu.make_async_copy(arrived, arrived, far_recv.at[i]).wait()
                total = gf[end]
                for j in range(n - 2):
                    total = total + g_far[i, j + (2 if end == 0 else 0)].astype(f32)
                g_send[end] = total.astype(bf16)
                g_copy(end, g_recv.at[me], dp_recv.at[3], end).start()

    def g_wait(sem, count):
        some = g_recv.at[pl.ds(0, count)]
        pltpu.make_async_copy(some, some, sem).wait()

    if n > 1:
        @pl.when(s == last)
        def _():
            for q in range(2):
                line_start(d_moves[0][q])

    def d_forward(step):
        for q in range(2):
            line_forward(d_moves[step][q], d_moves[step + 1][q])

    for step in range(n - 2):
        @pl.when(s == last)
        def _():
            sec_forward(step)
            if step == 0:
                bi_forward()

        d_forward(step)

        @pl.when(s == last)
        def _():
            if step == 0:
                g_start(relayed)

        if step == 0:
            @pl.when(s < last)
            def _():
                bi_forward()

            ps_copies.wait_recv()
            ps_share.start()

            ng_copy.wait_recv()
            grads_ref[:, :half] = ng[0]
            grads_ref[:, half:] = ng[1]
    @pl.when((s < last) & jnp.logical_not(at_end))
    def _():
        g_start(False)

    if relayed:
        pl.when(s == last)(g_relay)

    for q in range(2):
        line_finish([step_moves[q] for step_moves in sec_moves])
    ps_share.wait_recv()
    expand = dot_tn(sec_all[...].reshape(n * rows, width), ps_all[...].reshape(n * rows, share))
    expand_ref[...] = expand * norm

    @pl.when((s < last) & at_end)
    def _():
        g_start(False)

    bi_share.wait_recv()

    def reduce_crop(q):
        line_finish([step_moves[q] for step_moves in d_moves])
        bi_rows = bi_all[:, q * hrows : (q + 1) * hrows].reshape(n * hrows, share)
        d_rows = d_all[:, q * hrows : (q + 1) * hrows].reshape(n * hrows, width)
        reduced = dot_tn(bi_rows, d_rows) * norm
        reduce_ref[...] = reduced if q == 0 else reduce_ref[...] + reduced

    reduce_crop(0)
    reduce_crop(1)
    if relayed:
        @pl.when(at_end & (s == last))
        def _():
            for j in range(n):
                if 0 < j < n - 1:
                    @pl.when((me == 0) & (j != 1) | (me == n - 1) & (j != n - 2))
                    def _():
                        g_recv[j] = jnp.zeros(g_recv.shape[1:], bf16)
                else:
                    g_recv[j] = jnp.zeros(g_recv.shape[1:], bf16)
            g_wait(dp_recv.at[3], 1)

        @pl.when(jnp.logical_not(at_end & (s == last)))
        def _():
            g_recv[me] = jnp.zeros(g_recv.shape[1:], bf16)
            g_wait(dp_recv.at[3], n - 1)
    else:
        g_recv[me] = jnp.zeros(g_recv.shape[1:], bf16)
        g_wait(dp_recv.at[3], n - 1)
    total = gf[me]
    for j in range(n):
        total = total + g_recv[j].astype(f32)
    group_ref[...] = (total * norm)[: 9 * k]

    for move in [move for step_moves in sec_moves + d_moves for move in step_moves]:
        for copy, sends, _ in move:
            pl.when(sends)(copy.wait_send)
    g_wait(dp_send.at[3], n - 1)
    for copy in [bi_share, ps_share, bi_copies, ps_copies, wr_copy, ng_copy] + dfx_copies:
        copy.wait_send()

    @pl.when(counting)
    def _():
        for copies in cnt_copies:
            copies.wait_send()

    @pl.when(s > 0)
    def _():
        for copy in hop_copies:
            copy.wait_send()

    @pl.when(s < last)
    def _():
        for copy in fwd_copies:
            copy.wait_send()


def store_kernel(
    gw, grads_ref, reduce_ref, rows_ref, expand_ref, grads_hbm, reduce_hbm, group_hbm, expand_hbm,
    group_ref, sem,
):
    copies = [
        pltpu.make_async_copy(a, b, sem.at[i])
        for i, (a, b) in enumerate((
            (expand_ref, expand_hbm), (reduce_ref, reduce_hbm), (grads_ref, grads_hbm),
            (group_ref, group_hbm)))
    ]
    for copy in copies[:3]:
        copy.start()
    count, width = rows_ref.shape
    iota = lambda shape, dim: lax.broadcasted_iota(jnp.int32, shape, dim)
    wide = jnp.broadcast_to(rows_ref[...][:, None, :], (count, gw, width)).reshape(count * gw, width)
    out_of = iota((count * gw, width), 0) % gw == iota((count * gw, width), 1) % gw
    wide = jnp.where(out_of, wide, 0.0)
    high = wide.astype(bf16)
    low = (wide - high.astype(f32)).astype(bf16)
    group_of = iota((width, width // gw), 0) // gw == iota((width, width // gw), 1)
    group_of = group_of.astype(f32).astype(bf16)
    group_ref[...] = dot_nn(high, group_of) + dot_nn(low, group_of)
    copies[3].start()
    for copy in copies:
        copy.wait()


def on_device(
    block_inputs, out_pre, first_pre, second_pre, w_reduce, w_group, w_expand, w_lateral,
    teacher, top_grad, boxes, region_counts,
):
    n = lax.axis_size("dp")
    sections = lax.axis_size("section")
    crops, side, _, channels = top_grad.shape
    rows = crops * side * side
    width = first_pre.shape[4]
    lateral_width = w_lateral.shape[1]
    groups, gw = w_group.shape[2], w_group.shape[3]
    slots = boxes.shape[1]
    pixels = rows * n
    share = channels // n
    k = gw // n
    grows = -(-9 * k // 8) * 8
    half = channels // 2
    blk = min(256, width)
    hbm = pl.BlockSpec(memory_space=pltpu.HBM)
    vmem = pl.BlockSpec(memory_space=pltpu.VMEM)
    dma = pltpu.SemaphoreType.DMA
    peers = max(n - 1, 1)
    shapes = (
        ((rows, channels), bf16), ((share, width), f32),
        ((9 * k * gw, groups), f32), ((width, share), f32),
    )
    results = pl.pallas_call(
        functools.partial(kernel, (n, sections, crops, side, slots, pixels)),
        out_shape=tuple(pltpu.VMEM(shape, kind)
                        for shape, kind in shapes[:2] + (((9 * k, width), f32),) + shapes[3:]),
        in_specs=[hbm] * 12,
        out_specs=(vmem,) * 4,
        scratch_shapes=[
            pltpu.SMEM((crops, 4, slots), jnp.int32),
            pltpu.SMEM((1, crops), jnp.int32),
            pltpu.VMEM((3, rows, channels), bf16),
            pltpu.VMEM((2, rows, width), bf16),
            pltpu.VMEM((channels, width), bf16),
            pltpu.VMEM((9 * gw * gw, groups), bf16),
            pltpu.VMEM((2, width, half), bf16),
            pltpu.VMEM((channels, lateral_width), bf16),
            pltpu.VMEM((rows, lateral_width), bf16),
            dma((11,)),
            pltpu.VMEM((2, rows, half), bf16),
            pltpu.VMEM((2, rows, half), bf16),
            pltpu.VMEM((half, width), bf16),
            pltpu.VMEM((rows, width), bf16),
            pltpu.VMEM((2, rows, half), bf16),
            pltpu.VMEM((rows, width), bf16),
            pltpu.VMEM((n, rows, width), bf16),
            pltpu.VMEM((n, rows, width), bf16),
            pltpu.VMEM((n, rows, share), bf16),
            pltpu.VMEM((n, rows, share), bf16),
            pltpu.VMEM((n, rows, share), bf16),
            pltpu.VMEM((n, rows, share), bf16),
            pltpu.VMEM((n, grows, width), f32),
            pltpu.VMEM((n, grows, width), bf16),
            pltpu.VMEM((n, grows, width), bf16),
            pltpu.VMEM((2, n, grows, width), bf16),
            dma((2,)),
            pltpu.VMEM((n, 8, 128), f32),
            pltpu.VMEM((9, width, blk), bf16),
            pltpu.VMEM((9, width // blk, blk, rows), bf16),
            dma((5,)), dma((4,)), dma((4,)), dma((4,)),
            dma((2,)), dma((2,)), dma((2,)), dma((2,)),
            dma((peers, 2, 2)), dma((peers, 2, 2)), dma((peers, 2, 2)), dma((peers, 2, 2)),
            dma((2,)), dma((2,)),
        ],
        compiler_params=pltpu.CompilerParams(
            collective_id=0, has_side_effects=True, vmem_limit_bytes=44 << 20,
        ),
    )(*(pltpu.with_memory_space_constraint(x, pltpu.HBM) for x in (
        boxes.transpose(0, 2, 1), region_counts.reshape(1, crops),
        block_inputs.reshape(rows, channels), out_pre.reshape(rows, channels),
        first_pre.reshape(rows, width), second_pre.reshape(rows, width),
        w_reduce[0], w_group[0].transpose(0, 2, 3, 1).reshape(9 * gw * gw, groups), w_expand[0], w_lateral,
        teacher.reshape(rows, lateral_width), top_grad.reshape(rows, channels),
    )))
    grads, reduced, group, expand = pl.pallas_call(
        functools.partial(store_kernel, gw),
        out_shape=tuple(jax.ShapeDtypeStruct(shape, kind) for shape, kind in shapes),
        in_specs=[vmem] * 4,
        out_specs=(hbm,) * 4,
        scratch_shapes=[pltpu.VMEM((9 * k * gw, groups), f32), dma((4,))],
        compiler_params=pltpu.CompilerParams(vmem_limit_bytes=16 << 20),
    )(*(pltpu.with_memory_space_constraint(x, pltpu.VMEM) for x in results))
    group = group.reshape(9, k, gw, groups).transpose(0, 3, 1, 2)
    return (
        grads.reshape(1, crops, side, side, channels), reduced[None], group[None], expand[None],
    )


def solution(mesh):
    return jax.shard_map(
        on_device,
        mesh=mesh,
        in_specs=(
            P("section", ("parts", "dp"), None, None, None),
            P("section", ("parts", "dp"), None, None, None),
            P("section", ("parts", "dp"), None, None, "chan"),
            P("section", ("parts", "dp"), None, None, "chan"),
            P("section", None, "chan"),
            P("section", None, "chan", None, None),
            P("section", "chan", None),
            P(),
            P(("parts", "dp"), None, None, None),
            P(("parts", "dp"), None, None, None),
            P(("parts", "dp"), None, None),
            P(("parts", "dp")),
        ),
        out_specs=(
            P("section", ("parts", "dp"), None, None, None),
            P(("parts", "section"), "dp", "chan"),
            P(("parts", "section"), None, "chan", "dp", None),
            P(("parts", "section"), "chan", "dp"),
        ),
        check_vma=False,
    )
```

```python
import functools
import math

import jax
import jax.numpy as jnp
from jax import lax
from jax.experimental import pallas as pl
from jax.experimental.pallas import tpu as pltpu
from jax.sharding import PartitionSpec as P

imitation_weight = 0.5
tap_offsets = [(tap // 3 - 1, tap % 3 - 1) for tap in range(9)]
f32 = jnp.float32
bf16 = jnp.bfloat16


def dot_nn(a, b):
    return lax.dot_general(a, b, (((1,), (0,)), ((), ())), preferred_element_type=f32)


def dot_nt(a, b):
    return lax.dot_general(a, b, (((1,), (1,)), ((), ())), preferred_element_type=f32)


def dot_tn(a, b):
    return lax.dot_general(a, b, (((0,), (0,)), ((), ())), preferred_element_type=f32)


def kernel(
    dims,
    boxes_hbm, counts_hbm, bi_hbm, out_hbm, first_hbm, second_hbm, wr_hbm, wg_hbm, we_hbm,
    wl_hbm, teacher_hbm, top_hbm,
    grads_ref, reduce_ref, group_ref, expand_ref,
    boxes_ref, counts_ref,
    full_ref, part_ref, wr_ref, wg_ref, we_ref, wl_ref, teacher_ref, load_sem,
    inc, pas, wr_peer, dfx, ng, ds, d_all, sec_all, bi_send, bi_all, ps_send, ps_all,
    gf, g_send, g_recv, g_far, far_recv, cnt, taps, ft,
    dp_send, dp_recv, core_send, core_recv, hop_send, hop_recv, fwd_send, fwd_recv,
    sec_send, sec_recv, d_send, d_recv, share_send, share_recv,
):
    n, sections, crops, side, slots, pixels = dims
    out_ref, bi_ref, top_ref = (full_ref.at[i] for i in range(3))
    first_ref, second_ref = part_ref.at[0], part_ref.at[1]
    rows, channels = bi_ref.shape
    half = channels // 2
    width = first_ref.shape[1]
    groups = wg_ref.shape[1]
    gw = width // groups
    blk = taps.shape[2]
    blocks = width // blk
    cells = side * side
    share = channels // n
    k = gw // n
    hrows = rows // 2
    me = lax.axis_index("dp")
    s = lax.axis_index("section")
    c = lax.axis_index("chan")
    other = 1 - c
    last = sections - 1
    norm = 1.0 / math.sqrt(pixels)

    def remote(src, dst, send, recv, where):
        return pltpu.make_async_remote_copy(
            src_ref=src, dst_ref=dst, send_sem=send, recv_sem=recv,
            device_id=where, device_id_type=pl.DeviceIdType.MESH,
        )

    class Spread:
        def __init__(self, what, src_of, dst, moved, at=None, where={}):
            at = what if at is None else at
            self.copies = [
                remote(src_of(to), dst, dp_send.at[at], dp_recv.at[what], {"dp": to, **where})
                for to in (lax.rem(me + step, n) for step in range(1, n))
            ]
            self.sent = pltpu.make_async_copy(moved, moved, dp_send.at[at])
            self.received = pltpu.make_async_copy(moved, moved, dp_recv.at[what])

        def start(self):
            for copy in self.copies:
                copy.start()

        def wait_recv(self):
            self.received.wait()

        def wait_send(self):
            self.sent.wait()

    mine = pl.ds(pl.multiple_of(c * hrows, hrows), hrows)
    peers = pl.ds(0, n - 1)
    crop_rows = [pl.ds(q * hrows, hrows) for q in range(2)]

    def share_copy(which, buf):
        return remote(buf.at[:, mine], buf.at[:, mine], share_send.at[which],
                      share_recv.at[which], {"chan": other})

    def line(step, block, send, recv):
        ahead = block(lax.max(me - step, 0))
        behind = block(lax.min(me + step, n - 1))
        right = remote(ahead, ahead, send.at[0], recv.at[0], {"dp": lax.min(me + 1, n - 1)})
        left = remote(behind, behind, send.at[1], recv.at[1], {"dp": lax.max(me - 1, 0)})
        return (
            (right, (me - step >= 0) & (me + 1 < n), me - 1 - step >= 0),
            (left, (me + step < n) & (me >= 1), me + 1 + step < n),
        )

    def line_start(moves):
        for copy, sends, _ in moves:
            pl.when(sends)(copy.start)

    def line_forward(moves, following):
        for (copy, _, receives), (onward, sends, _) in zip(moves, following):
            @pl.when(receives & sends)
            def _():
                copy.wait_recv()
                onward.start()

    def line_settle(moves, following):
        for (copy, _, receives), (_, sends, _) in zip(moves, following):
            pl.when(receives & jnp.logical_not(sends))(copy.wait_recv)

    def line_finish(moves):
        for step in range(n - 1):
            if step == n - 2:
                for copy, _, receives in moves[step]:
                    pl.when(receives)(copy.wait_recv)
            else:
                line_settle(moves[step], moves[step + 1])

    barrier = pltpu.get_barrier_semaphore()
    mesh_type = pl.DeviceIdType.MESH
    for step in range(1, n):
        pl.semaphore_signal(barrier, inc=1, device_id={"dp": lax.rem(me + step, n)},
                            device_id_type=mesh_type)
    pl.semaphore_signal(barrier, inc=1, device_id={"chan": other}, device_id_type=mesh_type)

    @pl.when((s == last) & (c == 0))
    def _():
        for step in range(1, n):
            pl.semaphore_signal(barrier, inc=1, device_id_type=mesh_type,
                                device_id={"dp": lax.rem(me + step, n), "chan": other})

    @pl.when(s > 0)
    def _():
        pl.semaphore_signal(barrier, inc=1, device_id={"section": s - 1},
                            device_id_type=mesh_type)

    @pl.when(s < last)
    def _():
        pl.semaphore_signal(barrier, inc=1, device_id={"section": s + 1},
                            device_id_type=mesh_type)

    pairs = (
        ("boxes", boxes_hbm, boxes_ref), ("counts", counts_hbm, counts_ref),
        ("second", second_hbm, second_ref), ("pair", out_hbm, out_ref), ("wl", wl_hbm, wl_ref),
        ("teacher", teacher_hbm, teacher_ref), ("pair", bi_hbm, bi_ref),
        ("wg", wg_hbm, wg_ref), ("top", top_hbm, top_ref), ("we", we_hbm.at[:, :half], we_ref.at[0]),
        ("we", we_hbm.at[:, half:], we_ref.at[1]), ("first", first_hbm, first_ref),
        ("wr", wr_hbm, wr_ref),
    )
    whole = {
        "boxes": boxes_ref, "counts": counts_ref, "pair": full_ref.at[0:2], "top": top_ref,
        "first": first_ref, "second": second_ref, "wl": wl_ref, "teacher": teacher_ref,
        "wg": wg_ref, "we": we_ref, "wr": wr_ref,
    }
    load_at = {name: load_sem.at[i] for i, name in enumerate(whole)}

    def load_start(some):
        for name, a, b in some:
            pltpu.make_async_copy(a, b, load_at[name]).start()

    def loaded(*names):
        for name in names:
            pltpu.make_async_copy(whole[name], whole[name], load_at[name]).wait()

    counting = (s == last) & (c == 1)
    at_end = (me == 0) | (me == n - 1)
    load_start(pairs[:8])

    @pl.when(jnp.logical_not(counting))
    def _():
        load_start(pairs[8:])

    loaded("boxes", "counts")
    row = lax.broadcasted_iota(jnp.int32, (cells, 128), 0)
    row_h, row_w = row // side, row % side
    masks = []
    for crop in range(crops):
        inside = jnp.zeros((cells, 128), f32)
        for r in range(slots):
            hit = ((row_h >= boxes_ref[crop, 0, r]) & (row_h < boxes_ref[crop, 1, r])
                   & (row_w >= boxes_ref[crop, 2, r]) & (row_w < boxes_ref[crop, 3, r])
                   & (counts_ref[0, crop] > r))
            inside = jnp.where(hit, 1.0, inside)
        masks.append(inside)
    mask = jnp.concatenate(masks, axis=0)
    cnt[me] = jnp.broadcast_to(jnp.sum(mask, axis=0, keepdims=True), (8, 128))

    pl.semaphore_wait(barrier, n + jnp.where(s > 0, 1, 0) + jnp.where(s < last, 1, 0)
                      + jnp.where(counting, n - 1, 0))

    cnt_copies = [Spread(0, lambda to: cnt.at[me], cnt.at[me], cnt.at[peers], at, {"chan": core})
                  for core, at in ((0, 0), (1, 4))]

    @pl.when(counting)
    def _():
        for copies in cnt_copies:
            copies.start()
        load_start(pairs[8:])

    wr_copy = remote(wr_ref.at[pl.ds(pl.multiple_of(other * half, half), half)], wr_peer,
                     core_send.at[0], core_recv.at[0], {"chan": other})
    loaded("second")
    sec_all[me] = jnp.maximum(second_ref[...], 0)
    sec_moves = [[line(step, lambda j, q=q: sec_all.at[j, pl.ds(q * hrows, hrows)],
                       sec_send.at[step, q], sec_recv.at[step, q])
                  for q in range(2)] for step in range(n - 1)]
    if n > 1:
        for q in range(2):
            line_start(sec_moves[0][q])
    loaded("pair")
    for j in range(n):
        bi_send[j] = bi_ref[:, j * share : (j + 1) * share]
    bi_all[me, mine] = bi_send[me, mine]

    bi_copies = Spread(1, lambda to: bi_send.at[to, mine], bi_all.at[me, mine],
                       bi_all.at[peers, mine])
    bi_share = share_copy(0, bi_all)

    def sec_forward(step):
        for q in range(2):
            line_forward(sec_moves[step][q], sec_moves[step + 1][q])

    def bi_forward():
        bi_copies.wait_recv()
        bi_share.start()

    pair = gw * gw
    iota = lambda shape, dim: lax.broadcasted_iota(jnp.int32, shape, dim)
    same = iota((blk, blk), 0) // gw == iota((blk, blk), 1) // gw

    def build_taps():
        same_out = iota((width, pair), 0) % gw == iota((width, pair), 1) % gw
        spread = (iota((pair, blk), 0) // gw == iota((pair, blk), 1) % gw).astype(f32).astype(bf16)
        inside = iota((width, blk), 0) // gw % (blk // gw) == iota((width, blk), 1) // gw
        by_group = wg_ref[...].astype(f32).T
        for t in range(9):
            values = by_group[:, t * pair : (t + 1) * pair]
            values = jnp.broadcast_to(values[:, None, :], (groups, gw, pair)).reshape(width, pair)
            values = jnp.where(same_out, values, 0.0).astype(bf16)
            taps[t] = jnp.where(inside, dot_nn(values, spread), 0.0).astype(bf16)

    def shifter(count):
        prow = lax.broadcasted_iota(jnp.int32, (count, blk), 0)
        p_w = prow % side
        p_h = (prow // side) % side

        def moved(x, a, b):
            shift = (side * a + b) % count
            if shift:
                x = pltpu.roll(x, shift, 0)
            if a:
                x = jnp.where(p_h >= 1 if a == 1 else p_h < side - 1, x, 0.0)
            if b:
                x = jnp.where(p_w >= 1 if b == 1 else p_w < side - 1, x, 0.0)
            return x

        return moved

    def prepare_first():
        moved = shifter(rows)
        for b in range(blocks):
            first = jnp.maximum(first_ref[:, b * blk : (b + 1) * blk], 0).astype(f32)
            for t, (da, db) in enumerate(tap_offsets):
                ft[t, b] = moved(first, -da, -db).T.astype(bf16)

    hop_copies = [
        remote(ng.at[c, crop_rows[q]], inc.at[c, crop_rows[q]],
               hop_send.at[q], hop_recv.at[q], {"section": lax.max(s - 1, 0)})
        for q in range(2)
    ]
    fwd_copies = [
        remote(inc.at[c, crop_rows[q]], inc.at[c, crop_rows[q]],
               fwd_send.at[q], fwd_recv.at[q], {"chan": other})
        for q in range(2)
    ]

    @pl.when(s == last)
    def _():
        loaded("wl", "teacher")
        feature = jnp.maximum(out_ref[...], 0)
        lateral = dot_nn(feature, wl_ref[...])
        error = (mask[:, 0:1] * (lateral - teacher_ref[...].astype(f32))).astype(bf16)
        imitation = dot_nt(error, wl_ref[...])
        loaded("wg")
        build_taps()
        loaded("top", "first", "we", "wr")
        wr_copy.start()
        cnt_copies[0].wait_recv()
        bi_copies.start()
        covered = cnt[0]
        for j in range(1, n):
            covered = covered + cnt[j]
        scale = (imitation_weight * pixels) / covered[0:1, 0:1]
        start = (top_ref[...].astype(f32) + imitation * scale).astype(bf16)
        start = jnp.where(out_ref[...] > 0, start, jnp.zeros_like(start))
        pas[0] = start[:, :half]
        pas[1] = start[:, half:]

    @pl.when(s < last)
    def _():
        loaded("wl", "teacher", "wg", "top", "first", "we", "wr")
        wr_copy.start()
        build_taps()
        prepare_first()
        pl.when(at_end)(bi_copies.start)
        if n > 2:
            sec_forward(0)
        pl.when(jnp.logical_not(at_end))(bi_copies.start)
        for step in range(1, n - 2):
            sec_forward(step)

    ps_copies = Spread(2, lambda to: ps_send.at[to, mine], ps_all.at[me, mine],
                       ps_all.at[peers, mine])
    ps_share = share_copy(1, ps_all)
    d_moves = [[line(step, lambda j, q=q: d_all.at[j, crop_rows[q]], d_send.at[step, q],
                     d_recv.at[step, q]) for q in range(2)] for step in range(n - 1)]
    dfx_copies = [remote(d_all.at[me, crop_rows[q]], dfx.at[crop_rows[q]], core_send.at[1 + q],
                         core_recv.at[1 + q], {"chan": other}) for q in range(2)]
    ng_copy = remote(ng.at[c], ng.at[c], core_send.at[3], core_recv.at[3], {"chan": other})

    def gate_half(h, q):
        at = pl.ds(pl.multiple_of(h * half, half), half)
        value = inc[h, crop_rows[q]]
        gate = out_ref[q * hrows : (q + 1) * hrows, at] > 0
        pas[h, crop_rows[q]] = jnp.where(gate, value, jnp.zeros_like(value))

    def own_arrives(q, where=None):
        @pl.when((s < last) & where if where is not None else s < last)
        def _():
            hop_copies[q].wait_recv()
            fwd_copies[q].start()
            gate_half(c, q)

    def other_arrives(q):
        @pl.when(s < last)
        def _():
            fwd_copies[q].wait_recv()
            gate_half(other, q)

    moved = shifter(hrows)
    own_arrives(0)
    for q in range(2):
        top, end = q * hrows, (q + 1) * hrows
        second_full = dot_nt(pas[c, top:end], we_ref[c])
        if q == 0:
            own_arrives(1, c == 1)
        other_arrives(q)
        for j in range(n):
            at = (j * share) // half
            ps_send[j, top:end] = pas[at, top:end, j * share - at * half : (j + 1) * share - at * half]

        @pl.when(c == q)
        def _():
            ps_all[me, top:end] = ps_send[me, top:end]
            ps_copies.start()

        second_full = second_full + dot_nt(pas[other, top:end], we_ref[other])
        for b in range(blocks):
            lo, hi = b * blk, (b + 1) * blk
            lhs = jnp.where(second_ref[top:end, lo:hi] > 0, second_full[:, lo:hi], 0.0).astype(bf16)
            ds[top:end, lo:hi] = lhs
            total = None
            for db in (-1, 0, 1):
                column = None
                for da in (-1, 0, 1):
                    t = 3 * (da + 1) + db + 1
                    y = moved(dot_nn(lhs, taps[t, lo:hi, :]), da, 0)
                    column = y if column is None else column + y
                column = moved(column, 0, db)
                total = column if total is None else total + column
            d_all[me, top:end, lo:hi] = jnp.where(
                first_ref[top:end, lo:hi] > 0, total, 0.0).astype(bf16)
            if q == 0 and b == 0:
                own_arrives(1, c == 0)
        dfx_copies[q].start()
        if n > 1:
            @pl.when(s < last)
            def _():
                line_start(d_moves[0][q])

    own_rows = pl.ds(pl.multiple_of(c * half, half), half)
    wr_copy.wait_recv()
    for q in range(2):
        top, end = q * hrows, (q + 1) * hrows
        grad = dot_nt(d_all[me, top:end], wr_ref[own_rows, :]) + pas[c, top:end].astype(f32)
        dfx_copies[q].wait_recv()
        ng[c, top:end] = (grad + dot_nt(dfx[top:end], wr_peer[...])).astype(bf16)

        @pl.when(s > 0)
        def _():
            hop_copies[q].start()

    ng_copy.start()

    @pl.when(s == last)
    def _():
        prepare_first()

    gf[...] = jnp.zeros_like(gf)
    for b in range(blocks):
        rhs = ds[:, b * blk : (b + 1) * blk]
        for t in range(9):
            dense = jnp.where(same, dot_nn(ft[t, b], rhs), 0.0)
            folded = jnp.sum(dense.reshape(blk // gw, gw, blk), axis=0)
            for j in range(n):
                gf[j, t * k : (t + 1) * k, b * blk : (b + 1) * blk] = folded[j * k : (j + 1) * k]
    g_send[...] = gf[...].astype(bf16)
    def g_copy(part, dst, recv, where):
        return remote(g_send.at[part], dst, dp_send.at[3], recv, {"dp": where})

    relayed = n > 3
    ends = ((0, 1, me >= 2), (n - 1, n - 2, me <= n - 3))

    def g_start(relayed):
        for step in range(1, n):
            to = lax.rem(me + step, n)
            direct = (to != 0) & (to != n - 1) if relayed else to >= 0

            @pl.when(direct)
            def _():
                g_copy(to, g_recv.at[me], dp_recv.at[3], to).start()

        if relayed:
            for i, (end, by, far) in enumerate(ends):
                @pl.when(far)
                def _():
                    g_copy(end, g_far.at[i, me], far_recv.at[i], by).start()

    def g_relay():
        for i, (end, by, _) in enumerate(ends):
            @pl.when(me == by)
            def _():
                others = pl.ds(2 if end == 0 else 0, n - 2)
                arrived = g_far.at[i, others]
                pltpu.make_async_copy(arrived, arrived, far_recv.at[i]).wait()
                total = gf[end]
                for j in range(n - 2):
                    total = total + g_far[i, j + (2 if end == 0 else 0)].astype(f32)
                g_send[end] = total.astype(bf16)
                g_copy(end, g_recv.at[me], dp_recv.at[3], end).start()

    def g_wait(sem, count):
        some = g_recv.at[pl.ds(0, count)]
        pltpu.make_async_copy(some, some, sem).wait()

    if n > 1:
        @pl.when(s == last)
        def _():
            for q in range(2):
                line_start(d_moves[0][q])

    def d_forward(step):
        for q in range(2):
            line_forward(d_moves[step][q], d_moves[step + 1][q])

    for step in range(n - 2):
        @pl.when(s == last)
        def _():
            sec_forward(step)
            if step == 0:
                bi_forward()

        d_forward(step)

        @pl.when(s == last)
        def _():
            if step == 0:
                g_start(relayed)

        if step == 0:
            @pl.when(s < last)
            def _():
                bi_forward()

            ps_copies.wait_recv()
            ps_share.start()

            ng_copy.wait_recv()
            grads_ref[:, :half] = ng[0]
            grads_ref[:, half:] = ng[1]
    @pl.when((s < last) & jnp.logical_not(at_end))
    def _():
        g_start(False)

    if relayed:
        pl.when(s == last)(g_relay)

    for q in range(2):
        line_finish([step_moves[q] for step_moves in sec_moves])
    ps_share.wait_recv()
    expand = dot_tn(sec_all[...].reshape(n * rows, width), ps_all[...].reshape(n * rows, share))
    expand_ref[...] = expand * norm

    @pl.when((s < last) & at_end)
    def _():
        g_start(False)

    bi_share.wait_recv()

    def reduce_crop(q):
        line_finish([step_moves[q] for step_moves in d_moves])
        bi_rows = bi_all[:, q * hrows : (q + 1) * hrows].reshape(n * hrows, share)
        d_rows = d_all[:, q * hrows : (q + 1) * hrows].reshape(n * hrows, width)
        reduced = dot_tn(bi_rows, d_rows) * norm
        reduce_ref[...] = reduced if q == 0 else reduce_ref[...] + reduced

    reduce_crop(0)
    reduce_crop(1)
    if relayed:
        @pl.when(at_end & (s == last))
        def _():
            for j in range(n):
                if 0 < j < n - 1:
                    @pl.when((me == 0) & (j != 1) | (me == n - 1) & (j != n - 2))
                    def _():
                        g_recv[j] = jnp.zeros(g_recv.shape[1:], bf16)
                else:
                    g_recv[j] = jnp.zeros(g_recv.shape[1:], bf16)
            g_wait(dp_recv.at[3], 1)

        @pl.when(jnp.logical_not(at_end & (s == last)))
        def _():
            g_recv[me] = jnp.zeros(g_recv.shape[1:], bf16)
            g_wait(dp_recv.at[3], n - 1)
    else:
        g_recv[me] = jnp.zeros(g_recv.shape[1:], bf16)
        g_wait(dp_recv.at[3], n - 1)
    total = gf[me]
    for j in range(n):
        total = total + g_recv[j].astype(f32)
    group_ref[...] = (total * norm)[: 9 * k]

    for move in [move for step_moves in sec_moves + d_moves for move in step_moves]:
        for copy, sends, _ in move:
            pl.when(sends)(copy.wait_send)
    g_wait(dp_send.at[3], n - 1)
    for copy in [bi_share, ps_share, bi_copies, ps_copies, wr_copy, ng_copy] + dfx_copies:
        copy.wait_send()

    @pl.when(counting)
    def _():
        for copies in cnt_copies:
            copies.wait_send()

    @pl.when(s > 0)
    def _():
        for copy in hop_copies:
            copy.wait_send()

    @pl.when(s < last)
    def _():
        for copy in fwd_copies:
            copy.wait_send()


def store_kernel(
    gw, grads_ref, reduce_ref, rows_ref, expand_ref, grads_hbm, reduce_hbm, group_hbm, expand_hbm,
    group_ref, sem,
):
    copies = [
        pltpu.make_async_copy(a, b, sem.at[i])
        for i, (a, b) in enumerate((
            (expand_ref, expand_hbm), (reduce_ref, reduce_hbm), (grads_ref, grads_hbm),
            (group_ref, group_hbm)))
    ]
    for copy in copies[:3]:
        copy.start()
    count, width = rows_ref.shape
    iota = lambda shape, dim: lax.broadcasted_iota(jnp.int32, shape, dim)
    wide = jnp.broadcast_to(rows_ref[...][:, None, :], (count, gw, width)).reshape(count * gw, width)
    out_of = iota((count * gw, width), 0) % gw == iota((count * gw, width), 1) % gw
    wide = jnp.where(out_of, wide, 0.0)
    high = wide.astype(bf16)
    low = (wide - high.astype(f32)).astype(bf16)
    group_of = iota((width, width // gw), 0) // gw == iota((width, width // gw), 1)
    group_of = group_of.astype(f32).astype(bf16)
    group_ref[...] = dot_nn(high, group_of) + dot_nn(low, group_of)
    copies[3].start()
    for copy in copies:
        copy.wait()


def on_device(
    block_inputs, out_pre, first_pre, second_pre, w_reduce, w_group, w_expand, w_lateral,
    teacher, top_grad, boxes, region_counts,
):
    n = lax.axis_size("dp")
    sections = lax.axis_size("section")
    crops, side, _, channels = top_grad.shape
    rows = crops * side * side
    width = first_pre.shape[4]
    lateral_width = w_lateral.shape[1]
    groups, gw = w_group.shape[2], w_group.shape[3]
    slots = boxes.shape[1]
    pixels = rows * n
    share = channels // n
    k = gw // n
    grows = -(-9 * k // 8) * 8
    half = channels // 2
    blk = min(256, width)
    hbm = pl.BlockSpec(memory_space=pltpu.HBM)
    vmem = pl.BlockSpec(memory_space=pltpu.VMEM)
    dma = pltpu.SemaphoreType.DMA
    peers = max(n - 1, 1)
    shapes = (
        ((rows, channels), bf16), ((share, width), f32),
        ((9 * k * gw, groups), f32), ((width, share), f32),
    )
    results = pl.pallas_call(
        functools.partial(kernel, (n, sections, crops, side, slots, pixels)),
        out_shape=tuple(pltpu.VMEM(shape, kind)
                        for shape, kind in shapes[:2] + (((9 * k, width), f32),) + shapes[3:]),
        in_specs=[hbm] * 12,
        out_specs=(vmem,) * 4,
        scratch_shapes=[
            pltpu.SMEM((crops, 4, slots), jnp.int32),
            pltpu.SMEM((1, crops), jnp.int32),
            pltpu.VMEM((3, rows, channels), bf16),
            pltpu.VMEM((2, rows, width), bf16),
            pltpu.VMEM((channels, width), bf16),
            pltpu.VMEM((9 * gw * gw, groups), bf16),
            pltpu.VMEM((2, width, half), bf16),
            pltpu.VMEM((channels, lateral_width), bf16),
            pltpu.VMEM((rows, lateral_width), bf16),
            dma((11,)),
            pltpu.VMEM((2, rows, half), bf16),
            pltpu.VMEM((2, rows, half), bf16),
            pltpu.VMEM((half, width), bf16),
            pltpu.VMEM((rows, width), bf16),
            pltpu.VMEM((2, rows, half), bf16),
            pltpu.VMEM((rows, width), bf16),
            pltpu.VMEM((n, rows, width), bf16),
            pltpu.VMEM((n, rows, width), bf16),
            pltpu.VMEM((n, rows, share), bf16),
            pltpu.VMEM((n, rows, share), bf16),
            pltpu.VMEM((n, rows, share), bf16),
            pltpu.VMEM((n, rows, share), bf16),
            pltpu.VMEM((n, grows, width), f32),
            pltpu.VMEM((n, grows, width), bf16),
            pltpu.VMEM((n, grows, width), bf16),
            pltpu.VMEM((2, n, grows, width), bf16),
            dma((2,)),
            pltpu.VMEM((n, 8, 128), f32),
            pltpu.VMEM((9, width, blk), bf16),
            pltpu.VMEM((9, width // blk, blk, rows), bf16),
            dma((5,)), dma((4,)), dma((4,)), dma((4,)),
            dma((2,)), dma((2,)), dma((2,)), dma((2,)),
            dma((peers, 2, 2)), dma((peers, 2, 2)), dma((peers, 2, 2)), dma((peers, 2, 2)),
            dma((2,)), dma((2,)),
        ],
        compiler_params=pltpu.CompilerParams(
            collective_id=0, has_side_effects=True, vmem_limit_bytes=44 << 20,
        ),
    )(*(pltpu.with_memory_space_constraint(x, pltpu.HBM) for x in (
        boxes.transpose(0, 2, 1), region_counts.reshape(1, crops),
        block_inputs.reshape(rows, channels), out_pre.reshape(rows, channels),
        first_pre.reshape(rows, width), second_pre.reshape(rows, width),
        w_reduce[0], w_group[0].transpose(0, 2, 3, 1).reshape(9 * gw * gw, groups), w_expand[0], w_lateral,
        teacher.reshape(rows, lateral_width), top_grad.reshape(rows, channels),
    )))
    grads, reduced, group, expand = pl.pallas_call(
        functools.partial(store_kernel, gw),
        out_shape=tuple(jax.ShapeDtypeStruct(shape, kind) for shape, kind in shapes),
        in_specs=[vmem] * 4,
        out_specs=(hbm,) * 4,
        scratch_shapes=[pltpu.VMEM((9 * k * gw, groups), f32), dma((4,))],
        compiler_params=pltpu.CompilerParams(vmem_limit_bytes=16 << 20),
    )(*(pltpu.with_memory_space_constraint(x, pltpu.VMEM) for x in results))
    group = group.reshape(9, k, gw, groups).transpose(0, 3, 1, 2)
    return (
        grads.reshape(1, crops, side, side, channels), reduced[None], group[None], expand[None],
    )


def solution(mesh):
    return jax.shard_map(
        on_device,
        mesh=mesh,
        in_specs=(
            P("section", ("parts", "dp"), None, None, None),
            P("section", ("parts", "dp"), None, None, None),
            P("section", ("parts", "dp"), None, None, "chan"),
            P("section", ("parts", "dp"), None, None, "chan"),
            P("section", None, "chan"),
            P("section", None, "chan", None, None),
            P("section", "chan", None),
            P(),
            P(("parts", "dp"), None, None, None),
            P(("parts", "dp"), None, None, None),
            P(("parts", "dp"), None, None),
            P(("parts", "dp")),
        ),
        out_specs=(
            P("section", ("parts", "dp"), None, None, None),
            P(("parts", "section"), "dp", "chan"),
            P(("parts", "section"), None, "chan", "dp", None),
            P(("parts", "section"), "chan", "dp"),
        ),
        check_vma=False,
    )
```
